32 devices in a mesh: bucket: 4 (over y, core), seq: 8 (over z, x).
Axes of the slice: x: 2, y: 2, z: 4, core: 2. Of those that a mesh axis runs over, the one named last changes fastest.
Arguments:
- tokens: bfloat16 [4, 2, 2048, 768], P('bucket', None, 'seq'), may hold values from -6 to 6
- cotangent: bfloat16 [4, 2, 2048, 768], P('bucket', None, 'seq'), may hold values from -6 to 6
- lengths: int32 [4, 2], P('bucket'), may hold values from 128 to 2048, as said below
- decay_rate: float32 [768], replicated, may hold values from 1 to 100
- norm1_gain: bfloat16 [768], replicated, may hold values from 0.5 to 1.5
- norm1_bias: bfloat16 [768], replicated, may hold values from -1.25 to 1.25
- w_in: bfloat16 [768, 2304], replicated, may hold values from -0.21875 to 0.21875
- b_in: bfloat16 [2304], replicated, may hold values from -1.25 to 1.25
- short_weight: bfloat16 [3, 2304], replicated, may hold values from -3 to 3
- short_bias: bfloat16 [2304], replicated, may hold values from -1.25 to 1.25
- filter_w1: bfloat16 [33, 64], replicated, may hold values from -16 to 16
- filter_b1: bfloat16 [64], replicated, may hold values from -3.140625 to 3.140625
- filter_w2: bfloat16 [64, 64], replicated, may hold values from -6 to 6
- filter_b2: bfloat16 [64], replicated, may hold values from -3.140625 to 3.140625
- filter_w3: bfloat16 [64, 768], replicated, may hold values from -0.0625 to 0.0625
- skip_gain: bfloat16 [768], replicated, may hold values from -6 to 6
- w_out: bfloat16 [768, 768], replicated, may hold values from -0.21875 to 0.21875
- b_out: bfloat16 [768], replicated, may hold values from -1.25 to 1.25
- norm2_gain: bfloat16 [768], replicated, may hold values from 0.5 to 1.5
- norm2_bias: bfloat16 [768], replicated, may hold values from -1.25 to 1.25
- mlp_w1: bfloat16 [768, 3072], replicated, may hold values from -0.21875 to 0.21875
- mlp_b1: bfloat16 [3072], replicated, may hold values from -1.25 to 1.25
- mlp_w2: bfloat16 [3072, 768], replicated, may hold values from -0.109375 to 0.109375
- mlp_b2: bfloat16 [768], replicated, may hold values from -1.25 to 1.25
Outputs:
- output: bfloat16 [4, 2, 2048, 768], P('bucket', None, 'seq')
- tokens_grad: float32 [4, 2, 2048, 768], P('bucket', None, 'seq')
- grad_norm1_gain: float32 [768], replicated
- grad_norm1_bias: float32 [768], replicated
- grad_w_in: float32 [768, 2304], replicated
- grad_b_in: float32 [2304], replicated
- grad_short_weight: float32 [3, 2304], replicated
- grad_short_bias: float32 [2304], replicated
- grad_filter_w1: float32 [33, 64], replicated
- grad_filter_b1: float32 [64], replicated
- grad_filter_w2: float32 [64, 64], replicated
- grad_filter_b2: float32 [64], replicated
- grad_filter_w3: float32 [64, 768], replicated
- grad_skip_gain: float32 [768], replicated
- grad_w_out: float32 [768, 768], replicated
- grad_b_out: float32 [768], replicated
- grad_norm2_gain: float32 [768], replicated
- grad_norm2_bias: float32 [768], replicated
- grad_mlp_w1: float32 [768, 3072], replicated
- grad_mlp_b1: float32 [3072], replicated
- grad_mlp_w2: float32 [3072, 768], replicated
- grad_mlp_b2: float32 [768], replicated
The draws below stay inside these ranges and needn't reach their ends.
Inputs may be any that keep to these rules, and one draw needn't show every extreme that they name: `lengths`: every value lies between 128 and 2048, and some sequence has length exactly 2048.
All inputs are finite; a program needn't handle non-finite values.
Results may differ from the reference program's by a relative error of at most 0.012.
Values may be sent and summed in bfloat16 or wider, within the bound.
No kernel may reach another device: no remote copies, remote signals or barrier semaphores. Data moves between devices by JAX's collectives and lax.ppermute only.
A program may use at most 320 MiB of HBM per device.

```python
import math
import jax
import jax.numpy as jnp
from jax import lax

D = 768
HID = 3072
FILT = 64
EMB = 33
SEQS = 2
MIN_LEN = 128
LEN = 2048
BUCKETS = 4


def draw_lengths(key, part):
    keys = jax.random.split(key, 3)
    octave = jax.random.randint(keys[0], (BUCKETS, SEQS), 0, 7).astype(jnp.int32)
    factor = jnp.left_shift(jnp.ones((BUCKETS, SEQS), jnp.int32), octave)
    extra = jax.random.randint(keys[1], (BUCKETS, SEQS), 0, MIN_LEN).astype(jnp.int32)
    drawn = jnp.minimum(MIN_LEN * factor + extra * factor, LEN)
    chosen = jax.random.randint(keys[2], (), 0, BUCKETS * SEQS).astype(jnp.int32)
    flat = jnp.where(jnp.arange(BUCKETS * SEQS, dtype=jnp.int32) == chosen, LEN, drawn.reshape(BUCKETS * SEQS))
    return flat.reshape(BUCKETS, SEQS).astype(jnp.int32)


def steps_of(rng, extent, cuts, low, high):
    level, own = 1.0, jax.random.fold_in(rng, 6)
    for position, blocks in cuts:
        steps = jnp.exp(jax.random.uniform(jax.random.fold_in(own, position), (blocks,), jnp.float32, low / len(cuts), high / len(cuts)))
        level = level * jnp.repeat(steps, extent[position] // blocks).reshape([-1 if axis == position else 1 for axis in range(len(extent))])
    return level


def gaussian(rng, extent, width, reach, cuts=(), held_as=jnp.bfloat16):
    result = jax.random.normal(rng, extent, jnp.float32) * width
    if len(cuts) > 0:
        result = steps_of(rng, extent, cuts, -0.22, 0.18) * result
    return jnp.clip(result, min=-reach, max=reach).astype(held_as)


def setup_inputs(seed: int = 0) -> dict:
    key_list = jax.random.split(jax.random.key(seed), 25)
    tokens = gaussian(key_list[0], (BUCKETS, SEQS, LEN, D), 1.0, 6.0, ((0, 4), (2, 8)))
    cotangent = gaussian(key_list[1], (BUCKETS, SEQS, LEN, D), 1.0, 6.0, ((0, 4), (2, 8)))
    lengths = draw_lengths(jax.random.fold_in(key_list[24], 71), 0)
    decay_rate = jnp.clip(jnp.exp(jax.random.uniform(key_list[3], (D,), jnp.float32, math.log(1.0), math.log(100.0))), 1.0, 100.0)
    norm1_gain = jnp.clip(1.0 + 0.1 * jax.random.normal(key_list[4], (D,), jnp.float32), 0.5, 1.5).astype(jnp.bfloat16)
    norm1_bias = gaussian(key_list[5], (D,), 0.2, 1.25)
    w_in = gaussian(key_list[6], (D, 3 * D), D ** -0.5, 0.21875)
    b_in = gaussian(key_list[7], (3 * D,), 0.2, 1.25)
    short_weight = gaussian(key_list[8], (3, 3 * D), 0.5, 3.0)
    short_bias = gaussian(key_list[9], (3 * D,), 0.2, 1.25)
    filter_w1 = gaussian(key_list[10], (EMB, FILT), 3.0, 16.0)
    filter_b1 = jnp.clip(jax.random.uniform(key_list[11], (FILT,), jnp.float32, -3.140625, 3.140625), -3.140625, 3.140625).astype(jnp.bfloat16)
    filter_w2 = gaussian(key_list[12], (FILT, FILT), 1.0, 6.0)
    filter_b2 = jnp.clip(jax.random.uniform(key_list[13], (FILT,), jnp.float32, -3.140625, 3.140625), -3.140625, 3.140625).astype(jnp.bfloat16)
    filter_w3 = gaussian(key_list[14], (FILT, D), (4 * LEN) ** -0.5, 0.0625)
    skip_gain = gaussian(key_list[15], (D,), 1.0, 6.0)
    w_out = gaussian(key_list[16], (D, D), D ** -0.5, 0.21875)
    b_out = gaussian(key_list[17], (D,), 0.2, 1.25)
    norm2_gain = jnp.clip(1.0 + 0.1 * jax.random.normal(key_list[18], (D,), jnp.float32), 0.5, 1.5).astype(jnp.bfloat16)
    norm2_bias = gaussian(key_list[19], (D,), 0.2, 1.25)
    mlp_w1 = gaussian(key_list[20], (D, HID), D ** -0.5, 0.21875)
    mlp_b1 = gaussian(key_list[21], (HID,), 0.2, 1.25)
    mlp_w2 = gaussian(key_list[22], (HID, D), HID ** -0.5, 0.109375)
    mlp_b2 = gaussian(key_list[23], (D,), 0.2, 1.25)
    return dict(tokens=tokens, cotangent=cotangent, lengths=lengths, decay_rate=decay_rate, norm1_gain=norm1_gain, norm1_bias=norm1_bias, w_in=w_in, b_in=b_in, short_weight=short_weight, short_bias=short_bias, filter_w1=filter_w1, filter_b1=filter_b1, filter_w2=filter_w2, filter_b2=filter_b2, filter_w3=filter_w3, skip_gain=skip_gain, w_out=w_out, b_out=b_out, norm2_gain=norm2_gain, norm2_bias=norm2_bias, mlp_w1=mlp_w1, mlp_b1=mlp_b1, mlp_w2=mlp_w2, mlp_b2=mlp_b2)


HIGH = lax.Precision.HIGHEST
EPSILON = 1e-05

@jax.custom_vjp
def low(v):
    return lax.optimization_barrier(v.astype(jnp.bfloat16)).astype(jnp.float32)

@jax.custom_vjp
def low_back(v):
    return v

def low_keep(v):
    return (low(v), None)

def low_pass(kept, grad):
    return (grad,)

def back_keep(v):
    return (v, None)

def back_low(kept, grad):
    return (low(grad),)
low.defvjp(low_keep, low_pass)
low_back.defvjp(back_keep, back_low)

def matmul(left, right):
    return jnp.dot(left, right, precision=HIGH, preferred_element_type=jnp.float32)

def layer_norm(values, gain, bias):
    center = values - lax.optimization_barrier(jnp.mean(values, axis=-1, keepdims=True))
    spread = lax.optimization_barrier(jnp.mean(center * center, axis=-1, keepdims=True))
    return center * lax.rsqrt(spread + EPSILON) * gain + bias

def position_features(length):
    steps = jnp.arange(length, dtype=jnp.int32).astype(jnp.float32)
    bands = 0.0001 + jnp.arange(16, dtype=jnp.int32).astype(jnp.float32) * ((15.0 - 0.0001) / 15.0)
    phase = 2.0 * math.pi / length * steps[:, None] * bands[None, :]
    return jnp.concatenate([(steps / length)[:, None], jnp.cos(phase), -jnp.sin(phase)], axis=1)

def make_filter(filter_w1, filter_b1, filter_w2, filter_b2, filter_w3, rates, length):
    feats = position_features(length)
    hidden = jnp.sin(matmul(feats, filter_w1) + filter_b1)
    hidden = jnp.sin(matmul(hidden, filter_w2) + filter_b2)
    shaped = matmul(hidden, filter_w3)
    times = jnp.arange(length, dtype=jnp.int32).astype(jnp.float32)[:, None] / length
    return shaped * (jnp.exp(-times * rates[None, :]) + 0.05)

def sequence_forward(params, filt, seq_tokens, seq_len):
    gain_one, bias_one, w_in, b_in, short_weight, short_bias, skip_gain, w_out, b_out, gain_two, bias_two, mlp_w1, mlp_b1, mlp_w2, mlp_b2 = params
    normed = low(layer_norm(seq_tokens, gain_one, bias_one))
    mixed = low_back(low(matmul(normed, w_in) + b_in))
    padded = jnp.pad(mixed, ((2, 0), (0, 0)))
    conv = short_weight[0] * mixed + short_weight[1] * padded[1:-1] + short_weight[2] * padded[:-2] + short_bias
    gate_out = conv[:, :D]
    gate_in = conv[:, D:2 * D]
    values = conv[:, 2 * D:]
    signal = low(values * gate_in)
    spec_signal = jnp.fft.rfft(signal, n=2 * LEN, axis=0)
    spec_filter = jnp.fft.rfft(filt, n=2 * LEN, axis=0)
    conv_long = jnp.fft.irfft(spec_signal * spec_filter, n=2 * LEN, axis=0)[:LEN]
    long_out = low_back(conv_long + signal * skip_gain)
    gated = low(long_out * gate_out)
    branch = low_back(matmul(gated, w_out) + b_out)
    resid = seq_tokens + branch
    normed_two = low(layer_norm(resid, gain_two, bias_two))
    pre = low_back(matmul(normed_two, mlp_w1) + mlp_b1)
    active = low(jax.nn.gelu(pre, approximate=False))
    final = resid + matmul(active, mlp_w2) + mlp_b2
    valid = (jnp.arange(LEN, dtype=jnp.int32) < seq_len).astype(jnp.float32)[:, None]
    return final * valid

def reference(tokens, cotangent, lengths, decay_rate, norm1_gain, norm1_bias, w_in, b_in, short_weight, short_bias, filter_w1, filter_b1, filter_w2, filter_b2, filter_w3, skip_gain, w_out, b_out, norm2_gain, norm2_bias, mlp_w1, mlp_b1, mlp_w2, mlp_b2):
    main_params = tuple((param.astype(jnp.float32) for param in (norm1_gain, norm1_bias, w_in, b_in, short_weight, short_bias, skip_gain, w_out, b_out, norm2_gain, norm2_bias, mlp_w1, mlp_b1, mlp_w2, mlp_b2)))
    filter_params = tuple((param.astype(jnp.float32) for param in (filter_w1, filter_b1, filter_w2, filter_b2, filter_w3)))
    rates = decay_rate.astype(jnp.float32)
    flat_tokens = tokens.astype(jnp.float32).reshape(BUCKETS * SEQS, LEN, D)
    flat_lengths = lengths.reshape(BUCKETS * SEQS).astype(jnp.int32)

    def forward(main_inner, filter_inner, inputs):
        filt = low(make_filter(filter_inner[0], filter_inner[1], filter_inner[2], filter_inner[3], filter_inner[4], rates, LEN))
        checked = jax.checkpoint(sequence_forward)

        def one_sequence(state, entry):
            return (state, checked(main_inner, filt, entry[0], entry[1]))
        _, results = lax.scan(one_sequence, jnp.zeros((), jnp.float32), (inputs, flat_lengths))
        return results
    results, pull_back = jax.vjp(forward, main_params, filter_params, flat_tokens)
    grad_main, grad_filter, grad_tokens = pull_back(cotangent.astype(jnp.float32).reshape(BUCKETS * SEQS, LEN, D))
    return (results.reshape(BUCKETS, SEQS, LEN, D).astype(jnp.bfloat16), grad_tokens.reshape(BUCKETS, SEQS, LEN, D), grad_main[0], grad_main[1], grad_main[2], grad_main[3], grad_main[4], grad_main[5], grad_filter[0], grad_filter[1], grad_filter[2], grad_filter[3], grad_filter[4], grad_main[6], grad_main[7], grad_main[8], grad_main[9], grad_main[10], grad_main[11], grad_main[12], grad_main[13], grad_main[14])
```

```python
import math

import jax
import jax.numpy as jnp
import numpy as np
from jax import lax
from jax.experimental import pallas as pl
from jax.experimental.pallas import tpu as pltpu
from jax.sharding import PartitionSpec as P

HIGH = lax.Precision.HIGHEST
EPSILON = 1e-05
F32 = jnp.float32
BF16 = jnp.bfloat16


def norm_forward(values, gain, bias):
    center = values - jnp.mean(values, axis=-1, keepdims=True)
    inverse = lax.rsqrt(jnp.mean(center * center, axis=-1, keepdims=True) + EPSILON)
    unit = center * inverse
    return (unit * gain + bias, unit, inverse)


def norm_backward(grad_out, gain, unit, inverse):
    scaled = grad_out * gain
    grad_in = inverse * (
        scaled
        - jnp.mean(scaled, axis=-1, keepdims=True)
        - unit * jnp.mean(scaled * unit, axis=-1, keepdims=True)
    )
    return (grad_in, jnp.sum(grad_out * unit, axis=0), jnp.sum(grad_out, axis=0))


def precise(formula, left, right):
    return jnp.einsum(formula, left, right, precision=HIGH, preferred_element_type=F32)


def dot(left, right, dims):
    return lax.dot_general(left, right, (dims, ((), ())), preferred_element_type=F32)


def position_features(length):
    steps = lax.broadcasted_iota(jnp.int32, (1, length), 1).astype(F32)
    bands = 0.0001 + lax.broadcasted_iota(jnp.int32, (16, 1), 0).astype(F32) * (
        (15.0 - 0.0001) / 15.0
    )
    phase = 2.0 * math.pi / length * steps * bands
    return jnp.concatenate([steps / length, jnp.cos(phase), -jnp.sin(phase)], axis=0)


def filter_values(weight_one, bias_one, weight_two, bias_two, weight_three, rates, length):
    feats = position_features(length)
    hidden = jnp.sin(precise("eh,ep->hp", weight_one, feats) + bias_one[:, None])
    hidden = jnp.sin(precise("hk,hp->kp", weight_two, hidden) + bias_two[:, None])
    shaped = precise("hd,hp->dp", weight_three, hidden)
    times = lax.broadcasted_iota(jnp.int32, (1, length), 1).astype(F32) / length
    return shaped * (jnp.exp(-times * rates[:, None]) + 0.05)


def transform_tables(block):
    spots = np.arange(block, dtype=np.float64)
    angle = np.pi / block * (spots[None, :] + 0.5) * spots[:, None]
    table = np.concatenate([np.cos(angle), -np.sin(angle)], axis=1)
    high = table.astype(np.float32).astype(jnp.bfloat16)
    low = (table - high.astype(np.float64)).astype(np.float32).astype(jnp.bfloat16)
    back = (table / block).T
    back_high = back.astype(np.float32).astype(jnp.bfloat16)
    back_low = (back - back_high.astype(np.float64)).astype(np.float32).astype(jnp.bfloat16)
    return high, low, back_high, back_low


def mm(left, right):
    return lax.dot_general(
        left, right, (((1,), (0,)), ((), ())), preferred_element_type=F32
    )


def spectrum(block, high, low):
    return mm(block, high) + mm(block, low)


def invert(spec, back_high, back_low):
    head = spec.astype(BF16)
    tail = (spec - head.astype(F32)).astype(BF16)
    return mm(head, back_high) + (mm(tail, back_high) + mm(head, back_low))


def filter_spectra(filt_ref, high, low, g_ref, channels, blocks, length):
    sign = (1 - 2 * (lax.broadcasted_iota(jnp.int32, (1, length), 1) % 2)).astype(F32)
    before = None
    for lag in range(blocks):
        now = spectrum(filt_ref[:, lag * length : (lag + 1) * length], high, low)
        rows = slice(lag * channels, (lag + 1) * channels)
        if before is None:
            g_ref[rows, :] = now
        else:
            g_ref[rows, :length] = now[:, :length] - sign * before[:, length:]
            g_ref[rows, length:] = now[:, length:] + sign * before[:, :length]
        before = now


def conv_forward_kernel(
    channels, blocks, length, seqs,
    x_ref, filt_ref, high_ref, low_ref, bhigh_ref, blow_ref, out_ref, s_ref, g_ref,
):
    high, low = high_ref[...], low_ref[...]
    filter_spectra(filt_ref, high, low, g_ref, channels, blocks, length)
    for q in range(seqs):
        s_ref[q] = spectrum(x_ref[:, q * length : (q + 1) * length], high, low)

    def tile(step, carry):
        row = pl.multiple_of(step * 8, 8)
        for lane in range(0, length, 128):
            re, im = slice(lane, lane + 128), slice(length + lane, length + lane + 128)
            for q in range(seqs):
                for i in reversed(range(blocks)):
                    acc_re = acc_im = None
                    for j in range(i + 1):
                        s_rows = pl.ds(j * channels + row, 8)
                        g_rows = pl.ds((i - j) * channels + row, 8)
                        sr, si = s_ref[q, s_rows, re], s_ref[q, s_rows, im]
                        gr, gi = g_ref[g_rows, re], g_ref[g_rows, im]
                        new_re = sr * gr - si * gi
                        new_im = sr * gi + si * gr
                        acc_re = new_re if acc_re is None else acc_re + new_re
                        acc_im = new_im if acc_im is None else acc_im + new_im
                    rows = pl.ds(i * channels + row, 8)
                    s_ref[q, rows, re] = acc_re
                    s_ref[q, rows, im] = acc_im
        return carry

    lax.fori_loop(0, channels // 8, tile, 0)
    bhigh, blow = bhigh_ref[...], blow_ref[...]
    for q in range(seqs):
        out_ref[:, q * length : (q + 1) * length] = invert(s_ref[q], bhigh, blow).astype(BF16)


def conv_backward_kernel(
    channels, blocks, length, seqs,
    x_ref, y_ref, filt_ref, high_ref, low_ref, bhigh_ref, blow_ref,
    out_ref, gfilt_ref, s_ref, q_ref, g_ref, l_ref,
):
    high, low = high_ref[...], low_ref[...]
    filter_spectra(filt_ref, high, low, g_ref, channels, blocks, length)
    for q in range(seqs):
        s_ref[q] = spectrum(x_ref[:, q * length : (q + 1) * length], high, low)
        q_ref[q] = spectrum(y_ref[:, q * length : (q + 1) * length], high, low)

    def tile(step, carry):
        row = pl.multiple_of(step * 8, 8)
        for lane in range(0, length, 128):
            re, im = slice(lane, lane + 128), slice(length + lane, length + lane + 128)
            for d in range(blocks):
                acc_re = acc_im = None
                for q in range(seqs):
                    for j in range(blocks - d):
                        s_rows = pl.ds(j * channels + row, 8)
                        y_rows = pl.ds((j + d) * channels + row, 8)
                        sr, si = s_ref[q, s_rows, re], s_ref[q, s_rows, im]
                        yr, yi = q_ref[q, y_rows, re], q_ref[q, y_rows, im]
                        new_re = sr * yr + si * yi
                        new_im = sr * yi - si * yr
                        acc_re = new_re if acc_re is None else acc_re + new_re
                        acc_im = new_im if acc_im is None else acc_im + new_im
                rows = pl.ds(d * channels + row, 8)
                l_ref[rows, re] = acc_re
                l_ref[rows, im] = acc_im
            for q in range(seqs):
                for j in range(blocks):
                    acc_re = acc_im = None
                    for i in range(j, blocks):
                        y_rows = pl.ds(i * channels + row, 8)
                        g_rows = pl.ds((i - j) * channels + row, 8)
                        yr, yi = q_ref[q, y_rows, re], q_ref[q, y_rows, im]
                        gr, gi = g_ref[g_rows, re], g_ref[g_rows, im]
                        new_re = gr * yr + gi * yi
                        new_im = gr * yi - gi * yr
                        acc_re = new_re if acc_re is None else acc_re + new_re
                        acc_im = new_im if acc_im is None else acc_im + new_im
                    rows = pl.ds(j * channels + row, 8)
                    q_ref[q, rows, re] = acc_re
                    q_ref[q, rows, im] = acc_im
        return carry

    lax.fori_loop(0, channels // 8, tile, 0)
    bhigh, blow = bhigh_ref[...], blow_ref[...]
    for q in range(seqs):
        out_ref[:, q * length : (q + 1) * length] = invert(q_ref[q], bhigh, blow).astype(BF16)
    sign = (1 - 2 * (lax.broadcasted_iota(jnp.int32, (1, length), 1) % 2)).astype(F32)
    for d in range(blocks):
        rows = slice(d * channels, (d + 1) * channels)
        real, imag = l_ref[rows, :length], l_ref[rows, length:]
        if d + 1 < blocks:
            after = slice((d + 1) * channels, (d + 2) * channels)
            real = real + sign * l_ref[after, length:]
            imag = imag - sign * l_ref[after, :length]
        both = jnp.concatenate([real, imag], axis=1)
        gfilt_ref[:, d * length : (d + 1) * length] = invert(both, bhigh, blow)


def vmem_spec():
    return pl.BlockSpec(memory_space=pltpu.VMEM)


def conv_forward(x, filt, tables, channels, blocks, length, seqs):
    rows = blocks * channels
    kernel = lambda *refs: conv_forward_kernel(channels, blocks, length, seqs, *refs)
    return pl.pallas_call(
        kernel,
        name="conv_forward",
        out_shape=jax.ShapeDtypeStruct((rows, seqs * length), BF16),
        in_specs=[vmem_spec()] * 6,
        out_specs=vmem_spec(),
        scratch_shapes=[
            pltpu.VMEM((seqs, rows, 2 * length), F32),
            pltpu.VMEM((rows, 2 * length), F32),
        ],
        compiler_params=pltpu.CompilerParams(vmem_limit_bytes=40 << 20),
    )(x, filt, *tables)


def conv_backward(x, y, filt, tables, channels, blocks, length, seqs):
    rows = blocks * channels
    kernel = lambda *refs: conv_backward_kernel(channels, blocks, length, seqs, *refs)
    return pl.pallas_call(
        kernel,
        name="conv_backward",
        out_shape=(
            jax.ShapeDtypeStruct((rows, seqs * length), BF16),
            jax.ShapeDtypeStruct((channels, blocks * length), F32),
        ),
        in_specs=[vmem_spec()] * 7,
        out_specs=(vmem_spec(), vmem_spec()),
        scratch_shapes=[
            pltpu.VMEM((seqs, rows, 2 * length), F32),
            pltpu.VMEM((seqs, rows, 2 * length), F32),
            pltpu.VMEM((rows, 2 * length), F32),
            pltpu.VMEM((rows, 2 * length), F32),
        ],
        compiler_params=pltpu.CompilerParams(vmem_limit_bytes=48 << 20),
    )(x, y, filt, *tables)


def shifted(block, axis, distance):
    count = lax.axis_size(axis)
    route = [(i - distance, i) for i in range(count) if 0 <= i - distance < count]
    return lax.ppermute(block, axis, route)


def local(
    tokens, cotangent, lengths, decay_rate, norm1_gain, norm1_bias, w_in, b_in,
    short_weight, short_bias, filter_w1, filter_b1, filter_w2, filter_b2, filter_w3,
    skip_gain, w_out, b_out, norm2_gain, norm2_bias, mlp_w1, mlp_b1, mlp_w2, mlp_b2,
):
    seqs, block, width = tokens.shape[1:]
    rows = seqs * block
    blocks = lax.axis_size("seq")
    full = blocks * block
    channels = width // blocks
    position = lax.axis_index("seq")
    tables = [jnp.asarray(t) for t in transform_tables(block)]

    def col(vector):
        return vector.astype(F32)[:, None]

    edge_tokens = shifted(tokens[0, :, block - 2 :, :], "seq", 1).reshape(2 * seqs, width)
    inputs = tokens.reshape(rows, width).astype(F32)
    gain_one = norm1_gain.astype(F32)
    bias_one = norm1_bias.astype(F32)
    normed, unit_one, inverse_one = norm_forward(inputs, gain_one, bias_one)
    normed_low = normed.astype(BF16)
    edge_normed = norm_forward(edge_tokens.astype(F32), gain_one, bias_one)[0].astype(BF16)

    mixed = (dot(w_in, normed_low, ((0,), (1,))) + col(b_in)).astype(BF16)
    mixed = mixed.reshape(3 * width, seqs, block)
    edge = (dot(w_in, edge_normed, ((0,), (1,))) + col(b_in)).astype(BF16)
    edge = jnp.where(position > 0, edge, jnp.zeros_like(edge)).reshape(3 * width, seqs, 2)
    extended = jnp.concatenate([edge, mixed], axis=2).astype(F32)
    taps = short_weight.astype(F32)[:, :, None, None]
    conv = (
        taps[0] * extended[:, :, 2:]
        + taps[1] * extended[:, :, 1:-1]
        + taps[2] * extended[:, :, :-2]
        + short_bias.astype(F32)[:, None, None]
    ).reshape(3 * width, rows)
    gate_out = conv[:width]
    gate_in = conv[width : 2 * width]
    values = conv[2 * width :]
    signal_low = (values * gate_in).astype(BF16)
    signal = signal_low.astype(F32)
    skip = col(skip_gain)
    signal_all = lax.all_to_all(signal_low, "seq", 0, 0, tiled=True)

    own = position * channels
    rates = lax.dynamic_slice_in_dim(decay_rate, own, channels)
    weight_three = lax.dynamic_slice_in_dim(filter_w3.astype(F32), own, channels, axis=1)

    def filter_fn(weight_one, bias_first, weight_two, bias_second, weight_last):
        return filter_values(
            weight_one, bias_first, weight_two, bias_second, weight_last, rates, full
        )

    raw_filter, filter_pull = jax.vjp(
        filter_fn,
        filter_w1.astype(F32),
        filter_b1.astype(F32),
        filter_w2.astype(F32),
        filter_b2.astype(F32),
        weight_three,
    )
    filt = raw_filter.astype(BF16)
    long_all = conv_forward(signal_all, filt, tables, channels, blocks, block, seqs)
    conv_long = lax.all_to_all(long_all, "seq", 0, 0, tiled=True).astype(F32)
    long_out = conv_long + signal * skip
    gated_low = (long_out * gate_out).astype(BF16)

    branch = dot(gated_low, w_out, ((0,), (0,))) + b_out.astype(F32)
    resid = inputs + branch
    gain_two = norm2_gain.astype(F32)
    normed_two, unit_two, inverse_two = norm_forward(resid, gain_two, norm2_bias.astype(F32))
    normed_two_low = normed_two.astype(BF16)
    pre = dot(normed_two_low, mlp_w1, ((1,), (0,))) + mlp_b1.astype(F32)
    cumulative = 0.5 * (1.0 + lax.erf(pre * (1.0 / math.sqrt(2.0))))
    density = jnp.exp(-0.5 * pre * pre) * (1.0 / math.sqrt(2.0 * math.pi))
    active_low = (pre * cumulative).astype(BF16)
    final = resid + dot(active_low, mlp_w2, ((1,), (0,))) + mlp_b2.astype(F32)
    places = position * block + jnp.arange(block, dtype=jnp.int32)
    valid = (places[None, :] < lengths[0][:, None]).astype(F32).reshape(rows, 1)
    output = (final * valid).astype(BF16).reshape(1, seqs, block, width)
    grad_final_low = (cotangent.reshape(rows, width).astype(F32) * valid).astype(BF16)
    grad_final = grad_final_low.astype(F32)
    grad_mlp_b2 = jnp.sum(grad_final, axis=0)
    grad_mlp_w2 = dot(active_low, grad_final_low, ((0,), (0,)))
    grad_active = dot(grad_final_low, mlp_w2, ((1,), (1,)))
    grad_pre_low = (grad_active * (cumulative + pre * density)).astype(BF16)
    grad_mlp_b1 = jnp.sum(grad_pre_low.astype(F32), axis=0)
    grad_mlp_w1 = dot(normed_two_low, grad_pre_low, ((0,), (0,)))
    grad_normed_two = dot(grad_pre_low, mlp_w1, ((1,), (1,)))
    grad_resid_norm, grad_norm2_gain, grad_norm2_bias = norm_backward(
        grad_normed_two, gain_two, unit_two, inverse_two
    )
    grad_resid = grad_final + grad_resid_norm
    grad_branch_low = grad_resid.astype(BF16)
    grad_b_out = jnp.sum(grad_branch_low.astype(F32), axis=0)
    grad_w_out = dot(gated_low, grad_branch_low, ((1,), (0,)))

    grad_gated = dot(w_out, grad_branch_low, ((1,), (1,)))
    grad_long_low = (grad_gated * gate_out).astype(BF16)
    grad_long = grad_long_low.astype(F32)
    grad_gate_out = grad_gated * long_out
    grad_skip_gain = jnp.sum(grad_long * signal, axis=1)
    grad_long_all = lax.all_to_all(grad_long_low, "seq", 0, 0, tiled=True)
    back_all, grad_filter = conv_backward(
        signal_all, grad_long_all, filt, tables, channels, blocks, block, seqs
    )
    grad_signal = lax.all_to_all(back_all, "seq", 0, 0, tiled=True).astype(F32)
    grad_signal = grad_signal + grad_long * skip
    grad_filter_w1, grad_filter_b1, grad_filter_w2, grad_filter_b2, own_w3 = filter_pull(
        grad_filter
    )
    grad_filter_w3 = lax.dynamic_update_slice_in_dim(
        jnp.zeros(filter_w3.shape, F32), own_w3, own, axis=1
    )
    grad_conv = jnp.concatenate(
        [grad_gate_out, grad_signal * values, grad_signal * gate_in], axis=0
    )
    grad_short_bias = jnp.sum(grad_conv, axis=1)
    grad_conv = grad_conv.reshape(3 * width, seqs, block)
    grad_short_weight = jnp.stack(
        [
            jnp.sum(grad_conv * extended[:, :, 2:], axis=(1, 2)),
            jnp.sum(grad_conv * extended[:, :, 1:-1], axis=(1, 2)),
            jnp.sum(grad_conv * extended[:, :, :-2], axis=(1, 2)),
        ]
    )
    after = shifted(grad_conv[:, :, :2].reshape(3 * width, 2 * seqs), "seq", -1)
    after = after.reshape(3 * width, seqs, 2)
    grown = jnp.concatenate([grad_conv, after], axis=2)
    grad_mixed = (
        taps[0] * grown[:, :, :-2] + taps[1] * grown[:, :, 1:-1] + taps[2] * grown[:, :, 2:]
    )
    grad_mixed_low = grad_mixed.astype(BF16).reshape(3 * width, rows)
    grad_b_in = jnp.sum(grad_mixed_low.astype(F32), axis=1)
    grad_w_in = dot(normed_low, grad_mixed_low, ((0,), (1,)))
    grad_normed = dot(grad_mixed_low, w_in, ((0,), (1,)))
    grad_input_norm, grad_norm1_gain, grad_norm1_bias = norm_backward(
        grad_normed, gain_one, unit_one, inverse_one
    )
    tokens_grad = (grad_resid + grad_input_norm).reshape(1, seqs, block, width)

    small = [
        grad_norm1_gain, grad_norm1_bias, grad_b_in, grad_short_weight, grad_short_bias,
        grad_filter_w1, grad_filter_b1, grad_filter_w2, grad_filter_b2, grad_filter_w3,
        grad_skip_gain, grad_b_out, grad_norm2_gain, grad_norm2_bias, grad_mlp_b1,
        grad_mlp_b2,
    ]
    flat = jnp.concatenate([part.reshape(-1) for part in small])
    padding = -flat.shape[0] % width
    flat = jnp.pad(flat, (0, padding)).reshape(-1, width)
    sums = lax.psum(
        tuple(
            part.astype(BF16)
            for part in (grad_w_in, grad_w_out, grad_mlp_w1, grad_mlp_w2, flat)
        ),
        ("bucket", "seq"),
    )
    sum_w_in, sum_w_out, sum_w1, sum_w2, sum_flat = (part.astype(F32) for part in sums)
    sum_flat = sum_flat.reshape(-1)
    pieces = []
    start = 0
    for part in small:
        pieces.append(sum_flat[start : start + part.size].reshape(part.shape))
        start += part.size
    return (
        output, tokens_grad, pieces[0], pieces[1], sum_w_in, pieces[2], pieces[3], pieces[4],
        pieces[5], pieces[6], pieces[7], pieces[8], pieces[9], pieces[10], sum_w_out,
        pieces[11], pieces[12], pieces[13], sum_w1, pieces[14], sum_w2, pieces[15],
    )


def solution(mesh):
    split = P("bucket", None, "seq", None)
    in_specs = (split, split, P("bucket", None)) + (P(),) * 21
    out_specs = (split, split) + (P(),) * 20
    return jax.shard_map(local, mesh=mesh, in_specs=in_specs, out_specs=out_specs, check_vma=False)
```

```python
import math

import jax
import jax.numpy as jnp
import numpy as np
from jax import lax
from jax.experimental import pallas as pl
from jax.experimental.pallas import tpu as pltpu
from jax.sharding import PartitionSpec as P

HIGH = lax.Precision.HIGHEST
EPSILON = 1e-05
F32 = jnp.float32
BF16 = jnp.bfloat16


def norm_forward(values, gain, bias):
    center = values - jnp.mean(values, axis=-1, keepdims=True)
    inverse = lax.rsqrt(jnp.mean(center * center, axis=-1, keepdims=True) + EPSILON)
    unit = center * inverse
    return (unit * gain + bias, unit, inverse)


def precise(formula, left, right):
    return jnp.einsum(formula, left, right, precision=HIGH, preferred_element_type=F32)


def position_features(length):
    steps = lax.broadcasted_iota(jnp.int32, (1, length), 1).astype(F32)
    bands = 0.0001 + lax.broadcasted_iota(jnp.int32, (16, 1), 0).astype(F32) * (
        (15.0 - 0.0001) / 15.0
    )
    phase = 2.0 * math.pi / length * steps * bands
    return jnp.concatenate([steps / length, jnp.cos(phase), -jnp.sin(phase)], axis=0)


def filter_layers(weight_one, bias_one, weight_two, bias_two, length):
    feats = position_features(length)
    first = precise("eh,ep->hp", weight_one, feats) + bias_one[:, None]
    hidden = jnp.sin(first)
    second = precise("hk,hp->kp", weight_two, hidden) + bias_two[:, None]
    return feats, hidden, jnp.cos(first), jnp.sin(second), jnp.cos(second)


def exact(left, right, dims):
    return lax.dot_general(
        left, right, (dims, ((), ())), precision=HIGH, preferred_element_type=F32
    )


def filter_back_kernel(
    channels, own_ref, grad_ref, window_ref, feats_ref, h1_ref, c1_ref, h2_ref, c2_ref, w2_ref, w3_ref,
    last_ref, net_ref,
):
    hidden = h1_ref.shape[0]
    features = feats_ref.shape[0]
    shaped = grad_ref[...] * window_ref[...]
    ones = jnp.ones((8, shaped.shape[1]), F32)
    last_ref[...] = jnp.zeros_like(last_ref)
    net_ref[...] = jnp.zeros_like(net_ref)
    rows = pl.ds(pl.multiple_of(own_ref[0], 16), channels)
    grad_w3 = exact(shaped, h2_ref[...], ((1,), (1,)))
    last_ref[rows, :] = jnp.concatenate([grad_w3, jnp.zeros_like(grad_w3)], axis=1).astype(BF16)
    second = exact(w3_ref[...], shaped, ((1,), (0,))) * c2_ref[...]
    first = exact(w2_ref[...], second, ((1,), (0,))) * c1_ref[...]
    place = 0
    for value in (
        exact(feats_ref[...], first, ((1,), (1,))), exact(ones, first, ((1,), (1,)))[:1],
        exact(h1_ref[...], second, ((1,), (1,))), exact(ones, second, ((1,), (1,)))[:1],
    ):
        net_ref[place : place + value.shape[0], :hidden] = value
        place += value.shape[0]


def filter_back(own, grad, window, feats, h1, c1, h2, c2, w2, w3, width):
    channels = grad.shape[0]
    return pl.pallas_call(
        lambda *refs: filter_back_kernel(channels, *refs),
        name="filter_back",
        out_shape=(
            jax.ShapeDtypeStruct((width, 128), BF16), jax.ShapeDtypeStruct((128, 128), F32),
        ),
        in_specs=[smem_spec()] + [vmem_spec()] * 9,
        out_specs=(vmem_spec(), vmem_spec()),
        compiler_params=pltpu.CompilerParams(vmem_limit_bytes=28 << 20),
    )(own, grad, window, feats, h1, c1, h2, c2, w2, w3)


def choose_kernel(side_ref, early_ref, late_ref, out_ref, last_ref, net_ref, *refs):
    low_side = side_ref[0] == 0
    width = early_ref.shape[1]
    parts = (
        (early_ref[...], late_ref[0], slice(0, width), 0), (late_ref[1], out_ref[...], slice(0, width), 1),
        (last_ref[...], net_ref[...].astype(BF16), slice(width, width + 128), 1),
    )
    for low_half, high_half, lanes, stream in parts:
        refs[2 * stream][:, lanes] = jnp.where(low_side, high_half, low_half)
        refs[2 * stream + 1][:, lanes] = jnp.where(low_side, low_half, high_half)


def choose(side, early, late, grad_out, last, net):
    width = early.shape[0]
    tile = 128
    part = lambda lanes: pl.BlockSpec((tile, lanes), lambda j: (j, 0))
    shape = lambda lanes: jax.ShapeDtypeStruct((width, lanes), BF16)
    given_s, kept_s, given_t, kept_t = pl.pallas_call(
        choose_kernel,
        name="choose",
        grid=(width // tile,),
        out_shape=(shape(width), shape(width), shape(width + 128), shape(width + 128)),
        in_specs=[
            smem_spec(), part(width), pl.BlockSpec((2, tile, width), lambda j: (0, j, 0)), part(width),
            part(128), part(128),
        ],
        out_specs=(part(width), part(width), part(width + 128), part(width + 128)),
        compiler_params=pltpu.CompilerParams(vmem_limit_bytes=28 << 20),
    )(side, early, late, grad_out, last, net)
    return [(given_s, kept_s), (given_t, kept_t)]


def vmem_spec():
    return pl.BlockSpec(memory_space=pltpu.VMEM)


def smem_spec():
    return pl.BlockSpec(memory_space=pltpu.SMEM)


def contract(left, right, dims):
    return lax.dot_general(left, right, (dims, ((), ())), preferred_element_type=F32)


def lane_sums(parts):
    ones = jnp.ones((8, 128), BF16)
    rows = []
    for part in parts:
        folded = part[:, :128]
        for lane in range(128, part.shape[1], 128):
            folded = folded + part[:, lane : lane + 128]
        head = folded.astype(BF16)
        tail = (folded - head.astype(F32)).astype(BF16)
        both = contract(ones, head, ((1,), (1,))) + contract(ones, tail, ((1,), (1,)))
        rows.append(both[:1])
    return rows


def short_filter(mixed, edge, cols, seqs, block):
    spots = lax.broadcasted_iota(jnp.int32, (1, block), 1)
    pieces = []
    for q in range(seqs):
        now = mixed[:, q * block : (q + 1) * block]
        near, far = edge[:, 2 * q + 1 : 2 * q + 2], edge[:, 2 * q : 2 * q + 1]
        once = jnp.where(spots == 0, near, pltpu.roll(now, 1, 1))
        twice = jnp.where(spots == 0, far, jnp.where(spots == 1, near, pltpu.roll(now, 2, 1)))
        pieces.append(
            cols[:, 2:3] * now + cols[:, 3:4] * once + cols[:, 4:5] * twice + cols[:, 1:2]
        )
    return jnp.concatenate(pieces, axis=1)


def project(weight, normed, edge_normed, cols, inside, seqs, block):
    mixed = (contract(weight, normed, ((0,), (1,))) + cols[:, 0:1]).astype(BF16)
    edge = (contract(weight, edge_normed, ((0,), (1,))) + cols[:, 0:1]).astype(BF16)
    edge = edge.astype(F32) * inside
    return mixed, short_filter(mixed.astype(F32), edge, cols, seqs, block)


def front_kernel(
    seqs, block, first_ref, tok_ref, edge_ref, norm_ref, cols_ref, wb_ref, wc_ref,
    normed_ref, edge_normed_ref, mixed_ref, factor_ref, signal_ref,
):
    @pl.when(pl.program_id(0) == 0)
    def _():
        gain, bias = norm_ref[0:1], norm_ref[1:2]
        normed_ref[...] = norm_forward(tok_ref[...].astype(F32), gain, bias)[0].astype(BF16)
        edge_normed_ref[...] = norm_forward(edge_ref[...].astype(F32), gain, bias)[0].astype(BF16)

    normed, edge_normed = normed_ref[...], edge_normed_ref[...]
    inside = (first_ref[0] > 0).astype(F32)
    mixed_ref[0], gate_in = project(
        wb_ref[...], normed, edge_normed, cols_ref[1].T, inside, seqs, block
    )
    mixed_ref[1], values = project(
        wc_ref[...], normed, edge_normed, cols_ref[2].T, inside, seqs, block
    )
    factor_ref[0] = values
    factor_ref[1] = gate_in
    signal_ref[...] = (gate_in * values).astype(BF16)


def front(position, tokens, edge, norm, cols, w_in, seqs, block):
    rows, width = tokens.shape
    tile = 256
    steps = width // tile
    fixed = lambda shape: pl.BlockSpec(shape, lambda j: (0,) * len(shape))
    weight = lambda part: pl.BlockSpec((width, tile), lambda j: (0, part * steps + j))
    both = pl.BlockSpec((2, tile, rows), lambda j: (0, j, 0))
    return pl.pallas_call(
        lambda *refs: front_kernel(seqs, block, *refs),
        name="front",
        grid=(steps,),
        out_shape=(
            jax.ShapeDtypeStruct((rows, width), BF16), jax.ShapeDtypeStruct(edge.shape, BF16),
            jax.ShapeDtypeStruct((2, width, rows), BF16), jax.ShapeDtypeStruct((2, width, rows), F32),
            jax.ShapeDtypeStruct((width, rows), BF16),
        ),
        in_specs=[
            smem_spec(), fixed((rows, width)), fixed(edge.shape), fixed(norm.shape),
            pl.BlockSpec((3, cols.shape[1], tile), lambda j: (0, 0, j)), weight(1), weight(2),
        ],
        out_specs=(
            fixed((rows, width)), fixed(edge.shape), both, both,
            pl.BlockSpec((tile, rows), lambda j: (j, 0)),
        ),
        compiler_params=pltpu.CompilerParams(vmem_limit_bytes=58 << 20),
    )(position, tokens, edge, norm, cols, w_in, w_in)


def gate_kernel(
    seqs, block, first_ref, normed_ref, edge_normed_ref, cols_ref, w_ref, turned_ref, mixed_ref, gate_ref
):
    normed = normed_ref[...]

    @pl.when(pl.program_id(0) == 0)
    def _():
        turned_ref[...] = normed.T

    inside = (first_ref[0] > 0).astype(F32)
    mixed_ref[...], gate_ref[...] = project(
        w_ref[...], normed, edge_normed_ref[...], cols_ref[0].T, inside, seqs, block
    )


def gate_part(position, normed, edge_normed, cols, w_in, seqs, block):
    rows, width = normed.shape
    tile = 256
    fixed = lambda shape: pl.BlockSpec(shape, lambda j: (0,) * len(shape))
    out = pl.BlockSpec((tile, rows), lambda j: (j, 0))
    return pl.pallas_call(
        lambda *refs: gate_kernel(seqs, block, *refs),
        name="gate_part",
        grid=(width // tile,),
        out_shape=(
            jax.ShapeDtypeStruct((width, rows), BF16), jax.ShapeDtypeStruct((width, rows), BF16),
            jax.ShapeDtypeStruct((width, rows), F32),
        ),
        in_specs=[
            smem_spec(), fixed((rows, width)), fixed(edge_normed.shape),
            pl.BlockSpec((1, cols.shape[1], tile), lambda j: (0, 0, j)),
            pl.BlockSpec((width, tile), lambda j: (0, j)),
        ],
        out_specs=(fixed((width, rows)), out, out),
        compiler_params=pltpu.CompilerParams(vmem_limit_bytes=58 << 20),
    )(position, normed, edge_normed, cols, w_in)


def row_mask(position, lengths_ref, seqs, block):
    spots = position * block + lax.broadcasted_iota(jnp.int32, (block, 1), 0)
    return jnp.concatenate([(spots < lengths_ref[q]).astype(F32) for q in range(seqs)], axis=0)


def middle_kernel(
    seqs, block, side_ref, position_ref, lengths_ref, conv_ref, signal_ref, gate_ref, skip_ref, tok_ref,
    cot_ref, w_out_ref, rows_ref, b1_ref, w1_ref, w2_ref,
    out_ref, resid_grad_ref, long_ref, gate_grad_ref, given1_ref, kept1_ref, given2_ref, kept2_ref,
    gwo_ref, sums_ref, edge_ref, gb1_ref,
    gated_ref, n2_ref, n2t_ref, unit_ref, inv_ref, final_ref, gf_ref, q_ref, lout_ref,
):
    step = pl.program_id(0)
    last = pl.num_programs(0) - 1
    b_out, gain, bias, b2 = (rows_ref[i : i + 1] for i in range(4))

    @pl.when(step == 0)
    def _():
        skip = skip_ref[...].T[:, 0:1]
        long_out = conv_ref[...].astype(F32) + signal_ref[...].astype(F32) * skip
        lout_ref[...] = long_out
        gated = (long_out * gate_ref[...]).astype(BF16)
        gated_ref[...] = gated
        branch = contract(gated, w_out_ref[...], ((0,), (0,))) + b_out
        resid = tok_ref[...].astype(F32) + branch
        normed, unit, inverse = norm_forward(resid, gain, bias)
        n2_ref[...] = normed.astype(BF16)
        n2t_ref[...] = normed.astype(BF16).T
        unit_ref[...] = unit
        inv_ref[...] = jnp.broadcast_to(inverse, inv_ref.shape)
        final_ref[...] = resid + b2
        valid = row_mask(position_ref[0], lengths_ref, seqs, block)
        gf_ref[...] = (cot_ref[...].astype(F32) * valid).astype(BF16)
        q_ref[...] = jnp.zeros_like(q_ref)

    w1, w2, gf = w1_ref[...], w2_ref[...], gf_ref[...]
    pre = contract(n2_ref[...], w1, ((1,), (0,))) + b1_ref[...]
    grad_active = contract(gf, w2, ((1,), (1,)))
    cumulative, slope = normal_terms(pre)
    active = (pre * cumulative).astype(BF16)
    grad_pre = grad_active * slope
    grad_low = grad_pre.astype(BF16)
    final_ref[...] += contract(active, w2, ((1,), (0,)))
    q_ref[...] += contract(grad_low, w1, ((1,), (1,)))
    grad_two = contract(active, gf, ((0,), (0,))).astype(BF16)
    grad_one = contract(n2t_ref[...], grad_low, ((1,), (0,))).astype(BF16)

    @pl.when(step <= last // 2)
    def _():
        given1_ref[...] = grad_one
        given2_ref[...] = grad_two

    @pl.when(step > last // 2)
    def _():
        kept1_ref[...] = grad_one
        kept2_ref[...] = grad_two

    gb1_ref[...] = jnp.sum(grad_low.astype(F32), axis=0, keepdims=True)

    @pl.when(step == last)
    def _():
        valid = row_mask(position_ref[0], lengths_ref, seqs, block)
        out_ref[...] = (final_ref[...] * valid).astype(BF16)
        grad_final = gf_ref[...].astype(F32)
        q, unit = q_ref[...], unit_ref[...]
        scaled = q * gain
        grad_resid = grad_final + inv_ref[:, 0:1] * (
            scaled
            - jnp.mean(scaled, axis=-1, keepdims=True)
            - unit * jnp.mean(scaled * unit, axis=-1, keepdims=True)
        )
        resid_grad_ref[...] = grad_resid
        grad_branch = grad_resid.astype(BF16)
        grad_gated = contract(w_out_ref[...], grad_branch, ((1,), (1,)))
        grad_long = (grad_gated * gate_ref[...]).astype(BF16)
        long_ref[...] = grad_long
        gate_grad = grad_gated * lout_ref[...]
        gate_grad_ref[...] = gate_grad
        heads = [gate_grad[:, q * block : q * block + 128] for q in range(seqs)]
        edge_ref[...] = first_spots(heads)
        gwo_ref[...] = contract(gated_ref[...], grad_branch, ((1,), (0,))).astype(BF16)
        skip_sum = lane_sums([grad_long.astype(F32) * signal_ref[...].astype(F32)])[0]
        total = lambda part: jnp.sum(part, axis=0, keepdims=True)
        sums_ref[0:1] = skip_sum
        sums_ref[1:2] = total(grad_branch.astype(F32))
        sums_ref[2:3] = total(q * unit)
        sums_ref[3:4] = total(q)
        sums_ref[4:5] = total(grad_final)
        sums_ref[5:8] = jnp.zeros((3, sums_ref.shape[1]), F32)


def normal_terms(pre):
    cumulative = 0.5 * (1.0 + lax.erf(pre * (1.0 / math.sqrt(2.0))))
    density = jnp.exp(-0.5 * pre * pre) * (1.0 / math.sqrt(2.0 * math.pi))
    return cumulative, cumulative + pre * density


def middle(side, position, lengths, conv, signal, gate, skip, tokens, cotangent, w_out, rows, b1, w1, w2, seqs, block):
    count, width = tokens.shape
    hidden = w1.shape[1]
    chunk = width
    steps = hidden // chunk
    half = steps // 2
    once = lambda shape: pl.BlockSpec(
        shape, lambda j, side_ref: (0,) * len(shape), pipeline_mode=pl.Buffered(1)
    )

    def which(j, side_ref):
        side = side_ref[0]
        return jnp.where(j < half, half * (1 - side) + j, half * side + j - half)

    across = lambda height: pl.BlockSpec((height, chunk), lambda j, side_ref: (0, which(j, side_ref)))
    given = pl.BlockSpec((width, chunk), lambda j, side_ref: (0, jnp.minimum(j, half - 1)))
    kept = pl.BlockSpec((width, chunk), lambda j, side_ref: (0, jnp.maximum(j - half, 0)))
    wide, tall = (count, width), (width, count)
    shape = jax.ShapeDtypeStruct
    scratch = pltpu.VMEM
    part = shape((width, half * chunk), BF16)
    return pl.pallas_call(
        lambda *refs: middle_kernel(seqs, block, *refs),
        name="middle",
        out_shape=(
            shape(wide, BF16), shape(wide, F32), shape(tall, BF16), shape(tall, F32),
            part, part, part, part, shape((width, width), BF16),
            shape((8, width), F32), shape((8, width), F32), shape((1, hidden), F32),
        ),
        grid_spec=pltpu.PrefetchScalarGridSpec(
            num_scalar_prefetch=1,
            grid=(steps,),
            in_specs=[
                smem_spec(), smem_spec(), once(tall), once(tall), once(tall), once(skip.shape),
                once(wide), once(wide), once((width, width)), once(rows.shape),
                across(1), across(width),
                pl.BlockSpec((chunk, width), lambda j, side_ref: (which(j, side_ref), 0)),
            ],
            out_specs=(
                once(wide), once(wide), once(tall), once(tall), given, kept, given, kept,
                once((width, width)), once((8, width)), once((8, width)), across(1),
            ),
            scratch_shapes=[
                scratch(tall, BF16), scratch(wide, BF16), scratch(tall, BF16), scratch(wide, F32),
                scratch((count, 128), F32), scratch(wide, F32), scratch(wide, BF16), scratch(wide, F32),
                scratch(tall, F32),
            ],
        ),
        compiler_params=pltpu.CompilerParams(vmem_limit_bytes=58 << 20),
    )(side, position, lengths, conv, signal, gate, skip, tokens, cotangent, w_out, rows, b1, w1, w2)


def first_spots(heads):
    lanes = lax.broadcasted_iota(jnp.int32, (1, 128), 1)
    edge = jnp.zeros(heads[0].shape, F32)
    for q, head in enumerate(heads):
        head = pltpu.roll(head, 2 * q, 1) if q else head
        edge = jnp.where((lanes >= 2 * q) & (lanes < 2 * q + 2), head, edge)
    return edge.T[:8]


def edges_kernel(seqs, skip_ref, *refs):
    skip = skip_ref[...].T[:, 0:1]
    out_ref = refs[-1]
    signals = [
        refs[3 * q][...].astype(F32) + refs[3 * q + 1][...].astype(F32) * skip for q in range(seqs)
    ]
    for part in range(2):
        out_ref[part] = first_spots([signals[q] * refs[3 * q + 2][part] for q in range(seqs)])


def late_edges(conv, grad_long, skip, factors, seqs, block):
    width = conv.shape[0]
    specs, args = [], []
    for q in range(seqs):
        place = q * block // 128
        flat = pl.BlockSpec((width, 128), lambda i, place=place: (0, place))
        specs += [flat, flat, pl.BlockSpec((2, width, 128), lambda i, place=place: (0, 0, place))]
        args += [conv, grad_long, factors]
    return pl.pallas_call(
        lambda *refs: edges_kernel(seqs, *refs),
        name="late_edges",
        grid=(1,),
        out_shape=jax.ShapeDtypeStruct((2, 8, width), F32),
        in_specs=[pl.BlockSpec(skip.shape, lambda i: (0, 0))] + specs,
        out_specs=pl.BlockSpec((2, 8, width), lambda i: (0, 0, 0)),
        compiler_params=pltpu.CompilerParams(vmem_limit_bytes=24 << 20),
    )(skip, *args)


def short_back_kernel(seqs, block, late, *refs):
    if late:
        conv_ref, long_ref, skip_ref, factor_ref, *refs = refs
        skip = skip_ref[...].T[:, 0:1]
        grad = (conv_ref[...].astype(F32) + long_ref[...].astype(F32) * skip) * factor_ref[0]
    else:
        grad_ref, *refs = refs
        grad = grad_ref[0]
    edge_ref, mixed_ref, cols_ref, turned_ref, out_ref, gw_ref, sums_ref = refs
    cols = cols_ref[0].T
    edge = edge_ref[0].T
    spots = lax.broadcasted_iota(jnp.int32, (1, block), 1)
    mixed = mixed_ref[0].astype(F32)
    once, twice = [], []
    for q in range(seqs):
        now = grad[:, q * block : (q + 1) * block]
        near, far = edge[:, 2 * q : 2 * q + 1], edge[:, 2 * q + 1 : 2 * q + 2]
        end = block - 1
        once.append(jnp.where(spots == end, near, pltpu.roll(now, block - 1, 1)))
        twice.append(
            jnp.where(
                spots == end, far, jnp.where(spots == end - 1, near, pltpu.roll(now, block - 2, 1))
            )
        )
    once, twice = jnp.concatenate(once, axis=1), jnp.concatenate(twice, axis=1)
    low = (cols[:, 2:3] * grad + cols[:, 3:4] * once + cols[:, 4:5] * twice).astype(BF16)
    out_ref[0] = low
    gw_ref[0] = contract(turned_ref[...], low, ((1,), (1,))).astype(BF16)
    parts = [low.astype(F32), grad, mixed * grad, mixed * once, mixed * twice]
    for row, total in enumerate(lane_sums(parts)):
        sums_ref[0, row : row + 1] = total
    sums_ref[0, 5:8] = jnp.zeros((3, sums_ref.shape[2]), F32)


def short_back(grads, edges, mixed, cols, turned, seqs, block):
    count, width, rows = mixed.shape
    late = len(grads) > 1
    tile = 256
    part = lambda lanes: pl.BlockSpec((1, tile, lanes), lambda i, j: (i, j, 0))
    flat = pl.BlockSpec((tile, rows), lambda i, j: (j, 0))
    across = lambda height: pl.BlockSpec((1, height, tile), lambda i, j: (i, 0, j))
    given = [flat, flat, pl.BlockSpec((8, tile), lambda i, j: (0, j)), part(rows)]
    return pl.pallas_call(
        lambda *refs: short_back_kernel(seqs, block, late, *refs),
        name="short_back",
        grid=(count, width // tile),
        out_shape=(
            jax.ShapeDtypeStruct((count, width, rows), BF16),
            jax.ShapeDtypeStruct((count, width, width), BF16),
            jax.ShapeDtypeStruct((count, 8, width), F32),
        ),
        in_specs=(given if late else [part(rows)])
        + [
            across(8), part(rows), across(cols.shape[1]),
            pl.BlockSpec((width, rows), lambda i, j: (0, 0)),
        ],
        out_specs=(part(rows), across(width), across(8)),
        compiler_params=pltpu.CompilerParams(vmem_limit_bytes=58 << 20),
    )(*grads, edges, mixed, cols, turned)


def back_kernel(ga_ref, gb_ref, w_ref, tok_ref, resid_ref, norm_ref, out_ref, sums_ref):
    width = tok_ref.shape[1]
    turned = contract(w_ref[:, :width], ga_ref[0], ((1,), (0,)))
    for part in range(2):
        turned += contract(w_ref[:, (part + 1) * width : (part + 2) * width], gb_ref[part], ((1,), (0,)))
    q = turned.T
    gain = norm_ref[0:1]
    _, unit, inverse = norm_forward(tok_ref[...].astype(F32), gain, norm_ref[1:2])
    scaled = q * gain
    out_ref[...] = resid_ref[...] + inverse * (
        scaled
        - jnp.mean(scaled, axis=-1, keepdims=True)
        - unit * jnp.mean(scaled * unit, axis=-1, keepdims=True)
    )
    sums_ref[0:1] = jnp.sum(q * unit, axis=0, keepdims=True)
    sums_ref[1:2] = jnp.sum(q, axis=0, keepdims=True)
    sums_ref[2:8] = jnp.zeros((6, width), F32)


def back(mixed_early, mixed_late, w_in, tokens, grad_resid, norm):
    return pl.pallas_call(
        back_kernel,
        name="back",
        out_shape=(
            jax.ShapeDtypeStruct(tokens.shape, F32), jax.ShapeDtypeStruct((8, tokens.shape[1]), F32),
        ),
        in_specs=[vmem_spec()] * 6,
        out_specs=(vmem_spec(), vmem_spec()),
        compiler_params=pltpu.CompilerParams(vmem_limit_bytes=48 << 20),
    )(mixed_early, mixed_late, w_in, tokens, grad_resid, norm)


def transform_tables(block):
    spots = np.arange(block, dtype=np.float64)
    angle = np.pi / block * (spots[None, :] + 0.5) * spots[:, None]
    table = np.concatenate([np.cos(angle), -np.sin(angle)], axis=1)
    high = table.astype(np.float32).astype(jnp.bfloat16)
    low = (table - high.astype(np.float64)).astype(np.float32).astype(jnp.bfloat16)
    return np.stack([high, low])


def mm(left, right):
    return contract(left, right, ((1,), (0,)))


def spectrum(block, high, low):
    return mm(block, high) + mm(block, low)


def invert(spec, high, low):
    head = spec.astype(BF16)
    tail = (spec - head.astype(F32)).astype(BF16)
    back = lambda part, table: contract(part, table, ((1,), (1,)))
    return (back(head, high) + (back(tail, high) + back(head, low))) * (1.0 / high.shape[0])


def filter_spectra(filt_ref, high, low, g_ref, channels, blocks, length):
    sign = (1 - 2 * (lax.broadcasted_iota(jnp.int32, (1, length), 1) % 2)).astype(F32)
    before = None
    for lag in range(blocks):
        now = spectrum(filt_ref[:, lag * length : (lag + 1) * length], high, low)
        rows = slice(lag * channels, (lag + 1) * channels)
        if before is None:
            g_ref[rows, :] = now
        else:
            g_ref[rows, :length] = now[:, :length] - sign * before[:, length:]
            g_ref[rows, length:] = now[:, length:] + sign * before[:, :length]
        before = now


def conv_forward_kernel(
    channels, blocks, length, seqs,
    x_ref, filt_ref, table_ref, out_ref, s_ref, g_ref,
):
    high, low = table_ref[0], table_ref[1]
    filter_spectra(filt_ref, high, low, g_ref, channels, blocks, length)
    for q in range(seqs):
        s_ref[q] = spectrum(x_ref[:, q * length : (q + 1) * length], high, low)

    def tile(step, carry):
        row = pl.multiple_of(step * 8, 8)
        for lane in range(0, length, 128):
            re, im = slice(lane, lane + 128), slice(length + lane, length + lane + 128)
            for q in range(seqs):
                for i in reversed(range(blocks)):
                    acc_re = acc_im = None
                    for j in range(i + 1):
                        s_rows = pl.ds(j * channels + row, 8)
                        g_rows = pl.ds((i - j) * channels + row, 8)
                        sr, si = s_ref[q, s_rows, re], s_ref[q, s_rows, im]
                        gr, gi = g_ref[g_rows, re], g_ref[g_rows, im]
                        new_re = sr * gr - si * gi
                        new_im = sr * gi + si * gr
                        acc_re = new_re if acc_re is None else acc_re + new_re
                        acc_im = new_im if acc_im is None else acc_im + new_im
                    rows = pl.ds(i * channels + row, 8)
                    s_ref[q, rows, re] = acc_re
                    s_ref[q, rows, im] = acc_im
        return carry

    lax.fori_loop(0, channels // 8, tile, 0)
    for q in range(seqs):
        out_ref[:, q * length : (q + 1) * length] = invert(s_ref[q], high, low).astype(BF16)


def conv_backward_kernel(
    channels, blocks, length, seqs,
    x_ref, y_ref, filt_ref, table_ref, out_ref, gfilt_ref, s_ref, q_ref, g_ref, l_ref,
):
    high, low = table_ref[0], table_ref[1]
    filter_spectra(filt_ref, high, low, g_ref, channels, blocks, length)
    for q in range(seqs):
        s_ref[q] = spectrum(x_ref[:, q * length : (q + 1) * length], high, low)
        q_ref[q] = spectrum(y_ref[:, q * length : (q + 1) * length], high, low)

    def tile(step, carry):
        row = pl.multiple_of(step * 8, 8)
        for lane in range(0, length, 128):
            re, im = slice(lane, lane + 128), slice(length + lane, length + lane + 128)
            for d in range(blocks):
                acc_re = acc_im = None
                for q in range(seqs):
                    for j in range(blocks - d):
                        s_rows = pl.ds(j * channels + row, 8)
                        y_rows = pl.ds((j + d) * channels + row, 8)
                        sr, si = s_ref[q, s_rows, re], s_ref[q, s_rows, im]
                        yr, yi = q_ref[q, y_rows, re], q_ref[q, y_rows, im]
                        new_re = sr * yr + si * yi
                        new_im = sr * yi - si * yr
                        acc_re = new_re if acc_re is None else acc_re + new_re
                        acc_im = new_im if acc_im is None else acc_im + new_im
                rows = pl.ds(d * channels + row, 8)
                l_ref[rows, re] = acc_re
                l_ref[rows, im] = acc_im
            for q in range(seqs):
                for j in range(blocks):
                    acc_re = acc_im = None
                    for i in range(j, blocks):
                        y_rows = pl.ds(i * channels + row, 8)
                        g_rows = pl.ds((i - j) * channels + row, 8)
                        yr, yi = q_ref[q, y_rows, re], q_ref[q, y_rows, im]
                        gr, gi = g_ref[g_rows, re], g_ref[g_rows, im]
                        new_re = gr * yr + gi * yi
                        new_im = gr * yi - gi * yr
                        acc_re = new_re if acc_re is None else acc_re + new_re
                        acc_im = new_im if acc_im is None else acc_im + new_im
                    rows = pl.ds(j * channels + row, 8)
                    q_ref[q, rows, re] = acc_re
                    q_ref[q, rows, im] = acc_im
        return carry

    lax.fori_loop(0, channels // 8, tile, 0)
    for q in range(seqs):
        out_ref[:, q * length : (q + 1) * length] = invert(q_ref[q], high, low).astype(BF16)
    sign = (1 - 2 * (lax.broadcasted_iota(jnp.int32, (1, length), 1) % 2)).astype(F32)
    for d in range(blocks):
        rows = slice(d * channels, (d + 1) * channels)
        real, imag = l_ref[rows, :length], l_ref[rows, length:]
        if d + 1 < blocks:
            after = slice((d + 1) * channels, (d + 2) * channels)
            real = real + sign * l_ref[after, length:]
            imag = imag - sign * l_ref[after, :length]
        both = jnp.concatenate([real, imag], axis=1)
        gfilt_ref[:, d * length : (d + 1) * length] = invert(both, high, low)


def conv_forward(x, filt, table, channels, blocks, length, seqs):
    rows = blocks * channels
    kernel = lambda *refs: conv_forward_kernel(channels, blocks, length, seqs, *refs)
    return pl.pallas_call(
        kernel,
        name="conv_forward",
        out_shape=jax.ShapeDtypeStruct((rows, seqs * length), BF16),
        in_specs=[vmem_spec()] * 3,
        out_specs=vmem_spec(),
        scratch_shapes=[
            pltpu.VMEM((seqs, rows, 2 * length), F32),
            pltpu.VMEM((rows, 2 * length), F32),
        ],
        compiler_params=pltpu.CompilerParams(vmem_limit_bytes=58 << 20),
    )(x, filt, table)


def conv_backward(x, y, filt, table, channels, blocks, length, seqs):
    rows = blocks * channels
    kernel = lambda *refs: conv_backward_kernel(channels, blocks, length, seqs, *refs)
    return pl.pallas_call(
        kernel,
        name="conv_backward",
        out_shape=(
            jax.ShapeDtypeStruct((rows, seqs * length), BF16),
            jax.ShapeDtypeStruct((channels, blocks * length), F32),
        ),
        in_specs=[vmem_spec()] * 4,
        out_specs=(vmem_spec(), vmem_spec()),
        scratch_shapes=[
            pltpu.VMEM((seqs, rows, 2 * length), F32),
            pltpu.VMEM((seqs, rows, 2 * length), F32),
            pltpu.VMEM((rows, 2 * length), F32),
            pltpu.VMEM((rows, 2 * length), F32),
        ],
        compiler_params=pltpu.CompilerParams(vmem_limit_bytes=58 << 20),
    )(x, y, filt, table)


def shifted(block, axis, distance):
    count = lax.axis_size(axis)
    route = [(i - distance, i) for i in range(count) if 0 <= i - distance < count]
    return lax.ppermute(block, axis, route)


def axis_bits(axis):
    size, bits, bit = lax.axis_size(axis), [], 1
    while bit < size:
        bits.append((axis, bit))
        bit *= 2
    return bits


def exchange(value, step):
    axis, bit = step
    return lax.ppermute(value, axis, [(i, i ^ bit) for i in range(lax.axis_size(axis))])


def side_of(step):
    axis, bit = step
    return (lax.axis_index(axis) // bit) % 2


def fold_kernel(count, ways, sides_ref, *refs):
    ins, outs = refs[: 2 * ways * count], refs[2 * ways * count :]
    for i in range(ways * count):
        outs[i][...] = (
            ins[2 * i][...].astype(F32) + ins[2 * i + 1][...].astype(F32)
        ).astype(BF16)


def fold(pairs, steps):
    count = len(pairs)
    half = [pair[0].shape[0] // 2 for pair in pairs]
    if any(size % 16 for size in half):
        sums = [(kept.astype(F32) + other.astype(F32)).astype(BF16) for kept, other in pairs]
        if steps is None:
            return sums
        cut = lambda value, place, size: lax.dynamic_slice_in_dim(value, place * size, size, 0)
        return [
            (cut(value, 1 - side_of(step), size), cut(value, side_of(step), size))
            for value, step, size in zip(sums, steps, half)
        ]
    ways = 2 if steps else 1
    most = max(half) if steps else 2 * max(half)
    grid = 3 if most >= 384 and all(size % 48 == 0 for size in half) else 1
    shapes, in_specs, out_specs, args = [], [], [], []
    for i, ((kept, other), size) in enumerate(zip(pairs, half)):
        lanes = kept.shape[1]
        tile = (size if steps else 2 * size) // grid
        for way in range(ways):
            if steps:
                place = lambda j, sides_ref, i=i, way=way: (
                    (1 - sides_ref[i] if way == 0 else sides_ref[i]) * grid + j, 0
                )
            else:
                place = lambda j, sides_ref: (j, 0)
            in_specs += [pl.BlockSpec((tile, lanes), place)] * 2
            args += [kept, other]
            out_specs.append(pl.BlockSpec((tile, lanes), lambda j, sides_ref: (j, 0)))
            shapes.append(jax.ShapeDtypeStruct((tile * grid, lanes), BF16))
    sides = jnp.stack([side_of(step) for step in steps] if steps else [jnp.zeros((), jnp.int32)])
    outs = pl.pallas_call(
        lambda *refs: fold_kernel(count, ways, *refs),
        name="fold",
        out_shape=shapes,
        grid_spec=pltpu.PrefetchScalarGridSpec(
            num_scalar_prefetch=1, grid=(grid,), in_specs=in_specs, out_specs=out_specs
        ),
        compiler_params=pltpu.CompilerParams(vmem_limit_bytes=(58 if most >= 192 else 24) << 20),
    )(sides.astype(jnp.int32), *args)
    return list(zip(outs[::2], outs[1::2])) if steps else list(outs)


def join_kernel(count, sides_ref, *refs):
    for i in range(count):
        out_ref = refs[2 * count + i]
        out_ref[sides_ref[i]] = refs[2 * i][...]
        out_ref[1 - sides_ref[i]] = refs[2 * i + 1][...]


def join(pairs, steps):
    count = len(pairs)
    if any(pair[0].shape[0] % 16 for pair in pairs):
        outs = []
        for (own, other), step in zip(pairs, steps):
            first = side_of(step) == 0
            outs.append(jnp.concatenate([jnp.where(first, own, other), jnp.where(first, other, own)]))
        return outs
    sides = jnp.stack([side_of(step) for step in steps]).astype(jnp.int32)
    grid = 3 if all(pair[0].shape[0] % 384 == 0 for pair in pairs) else 1
    in_specs, out_specs, shapes = [], [], []
    for own, _ in pairs:
        rows, lanes = own.shape
        in_specs += [pl.BlockSpec((rows // grid, lanes), lambda j: (j, 0))] * 2
        out_specs.append(pl.BlockSpec((2, rows // grid, lanes), lambda j: (0, j, 0)))
        shapes.append(jax.ShapeDtypeStruct((2, rows, lanes), BF16))
    outs = pl.pallas_call(
        lambda *refs: join_kernel(count, *refs),
        name="join",
        grid=(grid,),
        out_shape=shapes,
        in_specs=[smem_spec()] + in_specs,
        out_specs=out_specs,
        compiler_params=pltpu.CompilerParams(vmem_limit_bytes=(58 if grid > 1 else 24) << 20),
    )(sides, *[value for pair in pairs for value in pair])
    return [out.reshape(-1, out.shape[2]) for out in outs]


def widen_kernel(side_ref, own_ref, other_ref, out_ref):
    side = side_ref[0]
    blocks = out_ref.shape[1] if len(out_ref.shape) == 4 else 0
    for ref, place in ((own_ref, side), (other_ref, 1 - side)):
        value = ref[...].astype(F32)
        lanes = value.shape[1]
        if blocks:
            for k in range(blocks):
                width = lanes // blocks
                out_ref[place, k] = value[:, k * width : (k + 1) * width]
        else:
            for half in range(2):

                @pl.when(place == half)
                def _():
                    out_ref[:, half * lanes : (half + 1) * lanes] = value


def widen(own, other, side, stacked):
    rows, lanes = own.shape
    tile = 128
    given = pl.BlockSpec((tile, lanes), lambda j: (j, 0))
    if stacked:
        count = lanes // rows
        shape = (2, count, rows, rows)
        out = pl.BlockSpec((2, count, tile, rows), lambda j: (0, 0, j, 0))
    else:
        shape = (rows, 2 * lanes)
        out = pl.BlockSpec((tile, 2 * lanes), lambda j: (j, 0))
    wide = pl.pallas_call(
        widen_kernel,
        name="widen",
        grid=(rows // tile,),
        out_shape=jax.ShapeDtypeStruct(shape, F32),
        in_specs=[smem_spec(), given, given],
        out_specs=out,
        compiler_params=pltpu.CompilerParams(vmem_limit_bytes=28 << 20),
    )(side, own, other)
    return wide.reshape(2 * count * rows, rows) if stacked else wide


def widen_late_kernel(side_ref, s_own_ref, s_other_ref, t_own_ref, t_other_ref, in_ref, out_ref, last_ref):
    width = out_ref.shape[1]
    first = side_ref[0] == 0
    for part in range(2):
        mine = first if part == 0 else jnp.logical_not(first)
        s_part = jnp.where(mine, s_own_ref[...].astype(F32), s_other_ref[...].astype(F32))
        t_part = jnp.where(mine, t_own_ref[...].astype(F32), t_other_ref[...].astype(F32))
        in_ref[:, part * width : (part + 1) * width] = s_part
        if part == 0:
            in_ref[:, 2 * width :] = t_part[:, :width]
        else:
            out_ref[...] = t_part[:, :width]
        last_ref[part] = t_part[:, width:]


def widen_late(s_own, s_other, t_own, t_other, side):
    rows, width = s_own.shape
    more = t_own.shape[1] - width
    tile = 128
    part = lambda lanes: pl.BlockSpec((tile, lanes), lambda j: (j, 0))
    return pl.pallas_call(
        widen_late_kernel,
        name="widen_late",
        grid=(rows // tile,),
        out_shape=(
            jax.ShapeDtypeStruct((rows, 3 * width), F32), jax.ShapeDtypeStruct((rows, width), F32),
            jax.ShapeDtypeStruct((2, rows, more), F32),
        ),
        in_specs=[smem_spec(), part(width), part(width), part(width + more), part(width + more)],
        out_specs=(
            part(3 * width), part(width), pl.BlockSpec((2, tile, more), lambda j: (0, j, 0)),
        ),
        compiler_params=pltpu.CompilerParams(vmem_limit_bytes=28 << 20),
    )(side, s_own, s_other, t_own, t_other)


def orders():
    bits = axis_bits("bucket") + axis_bits("seq")
    first, rest = bits[0], bits[1:]
    if len(rest) == 4:
        y, x, near, far = rest
        turns = ([y, x, near, far], [x, y, near, far])
    else:
        turns = (rest, rest[1:] + rest[:1])
    return [[first] + turn for turn in turns]


def work_order(last):
    if last == 4:
        return [
            ("p", 4), ("s", 1), ("back", 0), ("p", 5), ("s", 2), ("small", 0), ("p", -4), ("s", 3),
            ("small", 0), ("p", -3), ("small", 0), ("s", 4), ("p", -2), ("s", 5), ("small", 0), ("s", -4),
            ("small", 0), ("s", -3), ("p", -1), ("s", -2), ("wide", 0), ("s", -1),
        ]
    order = [("p", index) for index in range(4, last + 2)] + [("back", 0)]
    order += [("s", index) for index in range(1, last + 2)]
    order += [("p", -index) for index in range(last, 0, -1)] + [("wide", 0)]
    return order + [("s", -index) for index in range(last, 0, -1)]


def held(value, *awaited):
    return lax.optimization_barrier((value,) + awaited)[0]


def local(
    tokens, cotangent, lengths, decay_rate, norm1_gain, norm1_bias, w_in, b_in,
    short_weight, short_bias, filter_w1, filter_b1, filter_w2, filter_b2, filter_w3,
    skip_gain, w_out, b_out, norm2_gain, norm2_bias, mlp_w1, mlp_b1, mlp_w2, mlp_b2,
):
    seqs, block, width = tokens.shape[1:]
    rows = seqs * block
    blocks = lax.axis_size("seq")
    full = blocks * block
    channels = width // blocks
    position = lax.axis_index("seq")
    place = position.reshape(1).astype(jnp.int32)
    table = jnp.asarray(transform_tables(block))
    flat_tokens = tokens.reshape(rows, width)

    edge_tokens = shifted(tokens[0, :, block - 2 :, :], "seq", 1).reshape(2 * seqs, width)
    edge_tokens = jnp.pad(edge_tokens, ((0, 16 - 2 * seqs), (0, 0)))
    norm_one = jnp.stack([norm1_gain, norm1_bias]).astype(F32)
    cols = jnp.concatenate(
        [b_in[None], short_bias[None], short_weight, jnp.zeros((3, 3 * width), BF16)], axis=0
    )
    cols = cols.astype(F32).reshape(8, 3, width).transpose(1, 0, 2)
    skip = jnp.broadcast_to(skip_gain.astype(F32)[None], (8, width))
    normed, edge_normed, mixed_late, factors, signal = front(
        place, flat_tokens, edge_tokens, norm_one, cols, w_in, seqs, block
    )
    signal_all = lax.all_to_all(signal, "seq", 0, 0, tiled=True)
    turned, mixed_early, gate_out = gate_part(
        place, normed, edge_normed, cols, w_in, seqs, block
    )

    own = position * channels
    rates = lax.dynamic_slice_in_dim(decay_rate, own, channels)
    weight_three = lax.dynamic_slice_in_dim(filter_w3.astype(F32), own, channels, axis=1)

    second_weight = filter_w2.astype(F32)
    feats, hidden_one, slope_one, hidden_two, slope_two = filter_layers(
        filter_w1.astype(F32), filter_b1.astype(F32), second_weight, filter_b2.astype(F32), full
    )
    times = lax.broadcasted_iota(jnp.int32, (1, full), 1).astype(F32) / full
    window = jnp.exp(-times * rates[:, None]) + 0.05
    filt = (precise("hd,hp->dp", weight_three, hidden_two) * window).astype(BF16)
    long_all = conv_forward(signal_all, filt, table, channels, blocks, block, seqs)
    conv_long = lax.all_to_all(long_all, "seq", 0, 0, tiled=True)

    row_params = jnp.stack([b_out, norm2_gain, norm2_bias, mlp_b2]).astype(F32)
    order_p, order_q = orders()
    core = order_p[0]
    side = side_of(core).reshape(1).astype(jnp.int32)
    (
        output, grad_resid, grad_long, grad_gate, given_p, kept_p, given_q, kept_q, grad_w_out, sums,
        gate_edges, grad_b1,
    ) = middle(
        side, place, lengths.reshape(seqs), conv_long, signal, gate_out, skip, flat_tokens,
        cotangent.reshape(rows, width), w_out, row_params, mlp_b1.astype(F32)[None], mlp_w1,
        mlp_w2, seqs, block,
    )
    grad_long_all = lax.all_to_all(grad_long, "seq", 0, 0, tiled=True)

    def turn(streams, index, *awaited):
        steps = (order_p[index], order_q[index])
        pairs = [(kept, exchange(given, step)) for (given, kept), step in zip(streams, steps)]
        if awaited:
            pairs[0] = (held(pairs[0][0], *awaited), pairs[0][1])
        if index + 1 == len(order_p):
            return fold(pairs, None)
        return fold(pairs, (order_p[index + 1], order_q[index + 1]))

    def turn_back(parts, index, *awaited):
        steps = (order_p[index], order_q[index])
        pairs = [(part, exchange(part, step)) for part, step in zip(parts, steps)]
        pairs[0] = (held(pairs[0][0], *awaited), pairs[0][1])
        return join(pairs, steps)

    last = len(order_p) - 1
    gate_edges = shifted(gate_edges[None], "seq", -1)
    parts = turn([(given_p, kept_p), (given_q, kept_q)], 0)
    grad_long_all = held(grad_long_all, parts[0][0])
    back_all, grad_filter = conv_backward(
        signal_all, grad_long_all, filt, table, channels, blocks, block, seqs
    )
    back_conv = lax.all_to_all(back_all, "seq", 0, 0, tiled=True)
    last_w3, net = filter_back(
        own.reshape(1).astype(jnp.int32), grad_filter, window, feats, hidden_one, slope_one, hidden_two,
        slope_two, second_weight, weight_three, width,
    )
    parts = turn(parts, 1, last_w3)
    gate_grads, w_in_early, sums_early = short_back(
        (held(grad_gate, parts[0][0])[None],), gate_edges, mixed_early[None], cols[:1], turned, seqs,
        block,
    )
    back_conv = held(back_conv, gate_grads)
    edges = late_edges(back_conv, grad_long, skip, factors, seqs, block)
    parts = turn(parts, 2, edges)
    edges = shifted(edges, "seq", -1)
    late_grads, w_in_late, sums_late = short_back(
        (held(back_conv, parts[0][0]), grad_long, skip, factors), edges, mixed_late, cols[1:], turned,
        seqs, block,
    )
    features, hidden = filter_w1.shape
    heads = features + hidden + 2
    net = jnp.pad(net, ((0, width - 128), (0, 0)))
    late_parts = choose(side, w_in_early[0], w_in_late, grad_w_out, last_w3, net)
    state = {"p": parts, "s": late_parts}
    token = late_parts[0][0]
    small = iter(axis_bits("bucket") + axis_bits("seq"))
    for piece, index in work_order(last):
        if piece == "back":
            tokens_grad, sums_norm = back(
                gate_grads, held(late_grads, token), w_in, flat_tokens, grad_resid, norm_one
            )
            shorts = jnp.concatenate([sums_early, sums_late], axis=0)
            late = jnp.concatenate(
                [
                    sums[:5], grad_b1.reshape(-1, width), sums_norm[:2],
                    shorts[:, :5].reshape(-1, width),
                ],
                axis=0,
            )
            token = tokens_grad
        elif piece == "small":
            late = held(late, token)
            late = late + exchange(late, next(small))
            token = late
        elif piece == "wide":
            parts = state["p"]
            sum_w1 = widen(held(parts[0], token), exchange(parts[0], core), side, False)
            sum_w2 = widen(held(parts[1], sum_w1), exchange(parts[1], core), side, True)
            token = sum_w2
        elif index > 0:
            state[piece] = turn(state[piece], index - 1, token)
            token = state[piece][0][0] if index - 1 < last else state[piece][0]
        else:
            state[piece] = turn_back(state[piece], -index, token)
            token = state[piece][0]
    for step in small:
        late = late + exchange(late, step)
    total = late
    late_parts = state["s"]
    sum_w_in, sum_w_out, sum_last = widen_late(
        late_parts[0], exchange(late_parts[0], core), late_parts[1], exchange(late_parts[1], core),
        side,
    )
    w3_s, net_s = sum_last[0, :, :hidden].T, sum_last[1, :heads, :hidden]
    wide = grad_b1.shape[1] // width
    shorts_s = total[7 + wide :].reshape(3, 5, width)
    strip = lambda row: shorts_s[:, row].reshape(3 * width)
    return (
        output.reshape(tokens.shape), tokens_grad.reshape(tokens.shape), total[5 + wide],
        total[6 + wide], sum_w_in, strip(0), jnp.stack([strip(2), strip(3), strip(4)]), strip(1),
        net_s[:features], net_s[features], net_s[features + 1 : heads - 1], net_s[heads - 1], w3_s,
        total[0], sum_w_out, total[1], total[2], total[3], sum_w1,
        total[5 : 5 + wide].reshape(-1), sum_w2, total[4],
    )


def solution(mesh):
    split = P("bucket", None, "seq", None)
    in_specs = (split, split, P("bucket", None)) + (P(),) * 21
    out_specs = (split, split) + (P(),) * 20
    return jax.shard_map(local, mesh=mesh, in_specs=in_specs, out_specs=out_specs, check_vma=False)
```

```python
import math

import jax
import jax.numpy as jnp
import numpy as np
from jax import lax
from jax.experimental import pallas as pl
from jax.experimental.pallas import tpu as pltpu
from jax.sharding import PartitionSpec as P

HIGH = lax.Precision.HIGHEST
EPSILON = 1e-05
F32 = jnp.float32
BF16 = jnp.bfloat16


def norm_forward(values, gain, bias):
    center = values - jnp.mean(values, axis=-1, keepdims=True)
    inverse = lax.rsqrt(jnp.mean(center * center, axis=-1, keepdims=True) + EPSILON)
    unit = center * inverse
    return (unit * gain + bias, unit, inverse)


def precise(formula, left, right):
    return jnp.einsum(formula, left, right, precision=HIGH, preferred_element_type=F32)


def position_features(length):
    steps = lax.broadcasted_iota(jnp.int32, (1, length), 1).astype(F32)
    bands = 0.0001 + lax.broadcasted_iota(jnp.int32, (16, 1), 0).astype(F32) * (
        (15.0 - 0.0001) / 15.0
    )
    phase = 2.0 * math.pi / length * steps * bands
    return jnp.concatenate([steps / length, jnp.cos(phase), -jnp.sin(phase)], axis=0)


def filter_layers(weight_one, bias_one, weight_two, bias_two, length):
    feats = position_features(length)
    first = precise("eh,ep->hp", weight_one, feats) + bias_one[:, None]
    hidden = jnp.sin(first)
    second = precise("hk,hp->kp", weight_two, hidden) + bias_two[:, None]
    return feats, hidden, jnp.cos(first), jnp.sin(second), jnp.cos(second)


def exact(left, right, dims):
    return lax.dot_general(
        left, right, (dims, ((), ())), precision=HIGH, preferred_element_type=F32
    )


def filter_back_kernel(
    channels, own_ref, grad_ref, window_ref, feats_ref, h1_ref, c1_ref, h2_ref, c2_ref, w2_ref, w3_ref,
    last_ref, net_ref,
):
    hidden = h1_ref.shape[0]
    features = feats_ref.shape[0]
    shaped = grad_ref[...] * window_ref[...]
    ones = jnp.ones((8, shaped.shape[1]), F32)
    last_ref[...] = jnp.zeros_like(last_ref)
    net_ref[...] = jnp.zeros_like(net_ref)
    rows = pl.ds(pl.multiple_of(own_ref[0], 16), channels)
    grad_w3 = exact(shaped, h2_ref[...], ((1,), (1,)))
    last_ref[rows, :] = jnp.concatenate([grad_w3, jnp.zeros_like(grad_w3)], axis=1).astype(BF16)
    second = exact(w3_ref[...], shaped, ((1,), (0,))) * c2_ref[...]
    first = exact(w2_ref[...], second, ((1,), (0,))) * c1_ref[...]
    place = 0
    for value in (
        exact(feats_ref[...], first, ((1,), (1,))), exact(ones, first, ((1,), (1,)))[:1],
        exact(h1_ref[...], second, ((1,), (1,))), exact(ones, second, ((1,), (1,)))[:1],
    ):
        net_ref[place : place + value.shape[0], :hidden] = value
        place += value.shape[0]


def filter_back(own, grad, window, feats, h1, c1, h2, c2, w2, w3, width):
    channels = grad.shape[0]
    return pl.pallas_call(
        lambda *refs: filter_back_kernel(channels, *refs),
        name="filter_back",
        out_shape=(
            jax.ShapeDtypeStruct((width, 128), BF16), jax.ShapeDtypeStruct((128, 128), F32),
        ),
        in_specs=[smem_spec()] + [vmem_spec()] * 9,
        out_specs=(vmem_spec(), vmem_spec()),
        compiler_params=pltpu.CompilerParams(vmem_limit_bytes=14 << 20),
    )(own, grad, window, feats, h1, c1, h2, c2, w2, w3)


def choose_kernel(side_ref, early_ref, last_ref, out_ref, net_ref, given_ref, kept_ref):
    low_side = side_ref[0] == 0
    width = early_ref.shape[1]
    parts = (
        (early_ref[...], out_ref[...], slice(0, width)),
        (last_ref[...], net_ref[...].astype(BF16), slice(width, width + 128)),
    )
    for low_half, high_half, lanes in parts:
        given_ref[:, lanes] = jnp.where(low_side, high_half, low_half)
        kept_ref[:, lanes] = jnp.where(low_side, low_half, high_half)


def choose(side, early, last, grad_out, net):
    width = early.shape[0]
    tile = 128
    part = lambda lanes: pl.BlockSpec((tile, lanes), lambda j: (j, 0))
    shape = jax.ShapeDtypeStruct((width, width + 128), BF16)
    return tuple(
        pl.pallas_call(
            choose_kernel,
            name="choose",
            grid=(width // tile,),
            out_shape=(shape, shape),
            in_specs=[smem_spec(), part(width), part(128), part(width), part(128)],
            out_specs=(part(width + 128), part(width + 128)),
            compiler_params=pltpu.CompilerParams(vmem_limit_bytes=8 << 20),
        )(side, early, last, grad_out, net)
    )


def outside(shape, dtype):
    return pltpu.HBM(shape, dtype)


def vmem_spec():
    return pl.BlockSpec(memory_space=pltpu.VMEM)


def smem_spec():
    return pl.BlockSpec(memory_space=pltpu.SMEM)


def contract(left, right, dims):
    return lax.dot_general(left, right, (dims, ((), ())), preferred_element_type=F32)


def lane_sums(parts):
    ones = jnp.ones((8, 128), BF16)
    rows = []
    for part in parts:
        folded = part[:, :128]
        for lane in range(128, part.shape[1], 128):
            folded = folded + part[:, lane : lane + 128]
        head = folded.astype(BF16)
        tail = (folded - head.astype(F32)).astype(BF16)
        both = contract(ones, head, ((1,), (1,))) + contract(ones, tail, ((1,), (1,)))
        rows.append(both[:1])
    return rows


def columns(*rows):
    parts = [row[...].astype(F32).reshape(-1, row.shape[-1]) for row in rows]
    count = sum(part.shape[0] for part in parts)
    parts.append(jnp.zeros((8 - count, parts[0].shape[1]), F32))
    return jnp.concatenate(parts, axis=0).T


def row(ref):
    return ref[...].astype(F32).reshape(1, ref.shape[0])


def short_filter(mixed, edge, cols, seqs, block):
    spots = lax.broadcasted_iota(jnp.int32, (1, block), 1)
    pieces = []
    for q in range(seqs):
        now = mixed[:, q * block : (q + 1) * block]
        near, far = edge[:, 2 * q + 1 : 2 * q + 2], edge[:, 2 * q : 2 * q + 1]
        once = jnp.where(spots == 0, near, pltpu.roll(now, 1, 1))
        twice = jnp.where(spots == 0, far, jnp.where(spots == 1, near, pltpu.roll(now, 2, 1)))
        pieces.append(
            cols[:, 2:3] * now + cols[:, 3:4] * once + cols[:, 4:5] * twice + cols[:, 1:2]
        )
    return jnp.concatenate(pieces, axis=1)


def project(weight, normed, edge_normed, cols, inside, seqs, block):
    mixed = (contract(weight, normed, ((0,), (1,))) + cols[:, 0:1]).astype(BF16)
    edge = (contract(weight, edge_normed, ((0,), (1,))) + cols[:, 0:1]).astype(BF16)
    edge = edge.astype(F32) * inside
    return mixed, short_filter(mixed.astype(F32), edge, cols, seqs, block)


def front_kernel(
    seqs, block, first_ref, tok_ref, edge_ref, gain_ref, bias_ref, bb_ref, bc_ref, sbb_ref, sbc_ref, swb_ref,
    swc_ref, wb_ref, wc_ref, normed_ref, edge_normed_ref, mixed_ref, factor_ref, signal_ref,
):
    @pl.when(pl.program_id(0) == 0)
    def _():
        gain, bias = row(gain_ref), row(bias_ref)
        normed_ref[...] = norm_forward(tok_ref[...].astype(F32), gain, bias)[0].astype(BF16)
        edge_normed_ref[...] = norm_forward(edge_ref[...].astype(F32), gain, bias)[0].astype(BF16)

    normed, edge_normed = normed_ref[...], edge_normed_ref[...]
    inside = (first_ref[0] > 0).astype(F32)
    mixed_ref[0], gate_in = project(
        wb_ref[...], normed, edge_normed, columns(bb_ref, sbb_ref, swb_ref), inside, seqs, block
    )
    mixed_ref[1], values = project(
        wc_ref[...], normed, edge_normed, columns(bc_ref, sbc_ref, swc_ref), inside, seqs, block
    )
    factor_ref[0] = values
    factor_ref[1] = gate_in
    signal_ref[...] = (gate_in * values).astype(BF16)


def front(position, tokens, edge, gain, bias, b_in, short_bias, short_weight, w_in, seqs, block):
    rows, width = tokens.shape
    tile = 256
    steps = width // tile
    fixed = lambda shape: pl.BlockSpec(shape, lambda j: (0,) * len(shape))
    weight = lambda part: pl.BlockSpec((width, tile), lambda j: (0, part * steps + j))
    flat = lambda part: pl.BlockSpec((tile,), lambda j: (part * steps + j,))
    taps = lambda part: pl.BlockSpec((3, tile), lambda j: (0, part * steps + j))
    both = pl.BlockSpec((2, tile, rows), lambda j: (0, j, 0))
    return pl.pallas_call(
        lambda *refs: front_kernel(seqs, block, *refs),
        name="front",
        grid=(steps,),
        out_shape=(
            jax.ShapeDtypeStruct((rows, width), BF16), jax.ShapeDtypeStruct(edge.shape, BF16),
            jax.ShapeDtypeStruct((2, width, rows), BF16), jax.ShapeDtypeStruct((2, width, rows), F32),
            jax.ShapeDtypeStruct((width, rows), BF16),
        ),
        in_specs=[
            smem_spec(), fixed((rows, width)), fixed(edge.shape), fixed(gain.shape), fixed(bias.shape),
            flat(1), flat(2), flat(1), flat(2), taps(1), taps(2), weight(1), weight(2),
        ],
        out_specs=(
            fixed((rows, width)), fixed(edge.shape), both, both,
            pl.BlockSpec((tile, rows), lambda j: (j, 0)),
        ),
        compiler_params=pltpu.CompilerParams(vmem_limit_bytes=58 << 20),
    )(
        position, tokens, edge, gain, bias, b_in, b_in, short_bias, short_bias, short_weight,
        short_weight, w_in, w_in,
    )


def gate_kernel(
    seqs, block, first_ref, normed_ref, edge_normed_ref, b_ref, sb_ref, sw_ref, w_ref, turned_ref,
    mixed_ref, gate_ref,
):
    normed = normed_ref[...]

    @pl.when(pl.program_id(0) == 0)
    def _():
        turned_ref[...] = normed.T

    inside = (first_ref[0] > 0).astype(F32)
    mixed_ref[...], gate_ref[...] = project(
        w_ref[...], normed, edge_normed_ref[...], columns(b_ref, sb_ref, sw_ref), inside, seqs, block
    )


def gate_part(position, normed, edge_normed, b_in, short_bias, short_weight, w_in, seqs, block):
    rows, width = normed.shape
    tile = 256
    fixed = lambda shape: pl.BlockSpec(shape, lambda j: (0,) * len(shape))
    flat = pl.BlockSpec((tile,), lambda j: (j,))
    out = pl.BlockSpec((tile, rows), lambda j: (j, 0))
    return pl.pallas_call(
        lambda *refs: gate_kernel(seqs, block, *refs),
        name="gate_part",
        grid=(width // tile,),
        out_shape=(
            jax.ShapeDtypeStruct((width, rows), BF16), jax.ShapeDtypeStruct((width, rows), BF16),
            jax.ShapeDtypeStruct((width, rows), F32),
        ),
        in_specs=[
            smem_spec(), fixed((rows, width)), fixed(edge_normed.shape), flat, flat,
            pl.BlockSpec((3, tile), lambda j: (0, j)), pl.BlockSpec((width, tile), lambda j: (0, j)),
        ],
        out_specs=(fixed((width, rows)), out, out),
        compiler_params=pltpu.CompilerParams(vmem_limit_bytes=58 << 20),
    )(position, normed, edge_normed, b_in, short_bias, short_weight, w_in)


def row_mask(position, lengths_ref, seqs, block):
    spots = position * block + lax.broadcasted_iota(jnp.int32, (block, 1), 0)
    return jnp.concatenate([(spots < lengths_ref[q]).astype(F32) for q in range(seqs)], axis=0)


def middle_kernel(
    seqs, block, side_ref, position_ref, lengths_ref, conv_ref, signal_ref, gate_ref, skip_ref, tok_ref,
    cot_ref, w_out_ref, b_out_ref, gain_ref, bias_ref, b2_ref, b1_ref, w1_ref, w2_ref,
    out_ref, resid_grad_ref, long_ref, gate_grad_ref, given1_ref, kept1_ref, given2_ref, kept2_ref,
    gwo_ref, sums_ref, gb1_ref,
    gated_ref, n2_ref, n2t_ref, unit_ref, inv_ref, final_ref, gf_ref, q_ref, lout_ref,
):
    step = pl.program_id(0)
    last = pl.num_programs(0) - 1
    b_out, gain, bias, b2 = row(b_out_ref), row(gain_ref), row(bias_ref), row(b2_ref)

    @pl.when(step == 0)
    def _():
        skip = columns(skip_ref)[:, 0:1]
        long_out = conv_ref[...].astype(F32) + signal_ref[...].astype(F32) * skip
        lout_ref[...] = long_out
        gated = (long_out * gate_ref[...]).astype(BF16)
        gated_ref[...] = gated
        branch = contract(gated, w_out_ref[...], ((0,), (0,))) + b_out
        resid = tok_ref[...].astype(F32) + branch
        normed, unit, inverse = norm_forward(resid, gain, bias)
        n2_ref[...] = normed.astype(BF16)
        n2t_ref[...] = normed.astype(BF16).T
        unit_ref[...] = unit
        inv_ref[...] = jnp.broadcast_to(inverse, inv_ref.shape)
        final_ref[...] = resid + b2
        valid = row_mask(position_ref[0], lengths_ref, seqs, block)
        gf_ref[...] = (cot_ref[...].astype(F32) * valid).astype(BF16)
        q_ref[...] = jnp.zeros_like(q_ref)

    w1, w2, gf = w1_ref[...], w2_ref[...], gf_ref[...]
    pre = contract(n2_ref[...], w1, ((1,), (0,))) + b1_ref[...].astype(F32)
    grad_active = contract(gf, w2, ((1,), (1,)))
    cumulative, slope = normal_terms(pre)
    active = (pre * cumulative).astype(BF16)
    grad_pre = grad_active * slope
    grad_low = grad_pre.astype(BF16)
    final_ref[...] += contract(active, w2, ((1,), (0,)))
    q_ref[...] += contract(grad_low, w1, ((1,), (1,)))
    grad_two = contract(active, gf, ((0,), (0,))).astype(BF16)
    grad_one = contract(n2t_ref[...], grad_low, ((1,), (0,))).astype(BF16)

    @pl.when(step <= last // 2)
    def _():
        given1_ref[...] = grad_one
        given2_ref[...] = grad_two

    @pl.when(step > last // 2)
    def _():
        kept1_ref[...] = grad_one
        kept2_ref[...] = grad_two

    gb1_ref[...] = jnp.sum(grad_low.astype(F32), axis=0, keepdims=True)

    @pl.when(step == last)
    def _():
        valid = row_mask(position_ref[0], lengths_ref, seqs, block)
        out_ref[...] = (final_ref[...] * valid).astype(BF16)
        grad_final = gf_ref[...].astype(F32)
        q, unit = q_ref[...], unit_ref[...]
        scaled = q * gain
        grad_resid = grad_final + inv_ref[:, 0:1] * (
            scaled
            - jnp.mean(scaled, axis=-1, keepdims=True)
            - unit * jnp.mean(scaled * unit, axis=-1, keepdims=True)
        )
        resid_grad_ref[...] = grad_resid
        grad_branch = grad_resid.astype(BF16)
        grad_gated = contract(w_out_ref[...], grad_branch, ((1,), (1,)))
        grad_long = (grad_gated * gate_ref[...]).astype(BF16)
        long_ref[...] = grad_long
        gate_grad_ref[...] = grad_gated * lout_ref[...]
        gwo_ref[...] = contract(gated_ref[...], grad_branch, ((1,), (0,))).astype(BF16)
        skip_sum = lane_sums([grad_long.astype(F32) * signal_ref[...].astype(F32)])[0]
        total = lambda part: jnp.sum(part, axis=0, keepdims=True)
        sums_ref[0:1] = skip_sum
        sums_ref[1:2] = total(grad_branch.astype(F32))
        sums_ref[2:3] = total(q * unit)
        sums_ref[3:4] = total(q)
        sums_ref[4:5] = total(grad_final)
        sums_ref[5:8] = jnp.zeros((3, sums_ref.shape[1]), F32)


def normal_terms(pre):
    cumulative = 0.5 * (1.0 + lax.erf(pre * (1.0 / math.sqrt(2.0))))
    density = jnp.exp(-0.5 * pre * pre) * (1.0 / math.sqrt(2.0 * math.pi))
    return cumulative, cumulative + pre * density


def middle(
    side, position, lengths, conv, signal, gate, skip, tokens, cotangent, w_out, b_out, gain, bias, b2, b1, w1,
    w2, seqs, block,
):
    count, width = tokens.shape
    hidden = w1.shape[1]
    chunk = width
    steps = hidden // chunk
    half = steps // 2
    once = lambda shape: pl.BlockSpec(
        shape, lambda j, side_ref: (0,) * len(shape), pipeline_mode=pl.Buffered(1)
    )

    def which(j, side_ref):
        side = side_ref[0]
        return jnp.where(j < half, half * (1 - side) + j, half * side + j - half)

    across = lambda height: pl.BlockSpec((height, chunk), lambda j, side_ref: (0, which(j, side_ref)))
    given = pl.BlockSpec((width, chunk), lambda j, side_ref: (0, jnp.minimum(j, half - 1)))
    kept = pl.BlockSpec((width, chunk), lambda j, side_ref: (0, jnp.maximum(j - half, 0)))
    wide, tall = (count, width), (width, count)
    shape = jax.ShapeDtypeStruct
    scratch = pltpu.VMEM
    part = shape((width, half * chunk), BF16)
    return pl.pallas_call(
        lambda *refs: middle_kernel(seqs, block, *refs),
        name="middle",
        out_shape=(
            shape(wide, BF16), shape(wide, F32), shape(tall, BF16), shape(tall, F32),
            part, part, part, part, shape((width, width), BF16),
            shape((8, width), F32), shape((1, hidden), F32),
        ),
        grid_spec=pltpu.PrefetchScalarGridSpec(
            num_scalar_prefetch=1,
            grid=(steps,),
            in_specs=[
                smem_spec(), smem_spec(), once(tall), once(tall), once(tall), once(skip.shape),
                once(wide), once(wide), once((width, width)), once(b_out.shape), once(gain.shape),
                once(bias.shape), once(b2.shape),
                across(1), across(width),
                pl.BlockSpec((chunk, width), lambda j, side_ref: (which(j, side_ref), 0)),
            ],
            out_specs=(
                once(wide), once(wide), once(tall), once(tall), given, kept, given, kept,
                once((width, width)), once((8, width)), across(1),
            ),
            scratch_shapes=[
                scratch(tall, BF16), scratch(wide, BF16), scratch(tall, BF16), scratch(wide, F32),
                scratch((count, 128), F32), scratch(wide, F32), scratch(wide, BF16), scratch(wide, F32),
                scratch(tall, F32),
            ],
        ),
        compiler_params=pltpu.CompilerParams(vmem_limit_bytes=58 << 20),
    )(
        side, position, lengths, conv, signal, gate, skip, tokens, cotangent, w_out, b_out, gain, bias, b2, b1,
        w1, w2,
    )


def first_spots(heads):
    lanes = lax.broadcasted_iota(jnp.int32, (1, 128), 1)
    edge = jnp.zeros(heads[0].shape, F32)
    for q, head in enumerate(heads):
        head = pltpu.roll(head, 2 * q, 1) if q else head
        edge = jnp.where((lanes >= 2 * q) & (lanes < 2 * q + 2), head, edge)
    return edge.T[:8]


def edges_kernel(seqs, skip_ref, *refs):
    skip = columns(skip_ref)[:, 0:1]
    out_ref = refs[-1]
    signals = [
        refs[4 * q][...].astype(F32) + refs[4 * q + 1][...].astype(F32) * skip for q in range(seqs)
    ]
    for part in range(2):
        out_ref[part] = first_spots([signals[q] * refs[4 * q + 2][part] for q in range(seqs)])
    out_ref[2] = first_spots([refs[4 * q + 3][...] for q in range(seqs)])


def all_edges(conv, grad_long, skip, factors, gate, seqs, block):
    width = conv.shape[0]
    specs, args = [], []
    for q in range(seqs):
        place = q * block // 128
        flat = pl.BlockSpec((width, 128), lambda i, place=place: (0, place))
        specs += [flat, flat, pl.BlockSpec((2, width, 128), lambda i, place=place: (0, 0, place)), flat]
        args += [conv, grad_long, factors, gate]
    return pl.pallas_call(
        lambda *refs: edges_kernel(seqs, *refs),
        name="all_edges",
        grid=(1,),
        out_shape=jax.ShapeDtypeStruct((3, 8, width), F32),
        in_specs=[pl.BlockSpec(skip.shape, lambda i: (0,))] + specs,
        out_specs=pl.BlockSpec((3, 8, width), lambda i: (0, 0, 0)),
        compiler_params=pltpu.CompilerParams(vmem_limit_bytes=14 << 20),
    )(skip, *args)


def short_back_body(grad, edge_ref, mixed_ref, sw_ref, turned_ref, out_ref, sums_ref, seqs, block):
    taps = columns(sw_ref)
    edge = edge_ref[0].T
    spots = lax.broadcasted_iota(jnp.int32, (1, block), 1)
    mixed = mixed_ref[0].astype(F32)
    once, twice = [], []
    for q in range(seqs):
        now = grad[:, q * block : (q + 1) * block]
        near, far = edge[:, 2 * q : 2 * q + 1], edge[:, 2 * q + 1 : 2 * q + 2]
        end = block - 1
        once.append(jnp.where(spots == end, near, pltpu.roll(now, block - 1, 1)))
        twice.append(
            jnp.where(
                spots == end, far, jnp.where(spots == end - 1, near, pltpu.roll(now, block - 2, 1))
            )
        )
    once, twice = jnp.concatenate(once, axis=1), jnp.concatenate(twice, axis=1)
    low = (taps[:, 0:1] * grad + taps[:, 1:2] * once + taps[:, 2:3] * twice).astype(BF16)
    out_ref[0] = low
    parts = [low.astype(F32), grad, mixed * grad, mixed * once, mixed * twice]
    for place, total in enumerate(lane_sums(parts)):
        sums_ref[0, place : place + 1] = total
    sums_ref[0, 5:8] = jnp.zeros((3, sums_ref.shape[2]), F32)
    return contract(turned_ref[...], low, ((1,), (1,))).astype(BF16)


def early_back_kernel(
    seqs, block, grad_ref, edge_ref, mixed_ref, sw_ref, turned_ref, out_ref, gw_ref, sums_ref
):
    gw_ref[...] = short_back_body(
        grad_ref[...], edge_ref, mixed_ref, sw_ref, turned_ref, out_ref, sums_ref, seqs, block
    )


def early_back(grad, edges, mixed, short_weight, turned, seqs, block):
    width, rows = grad.shape
    tile = 256
    flat = pl.BlockSpec((tile, rows), lambda j: (j, 0))
    part = pl.BlockSpec((1, tile, rows), lambda j: (0, j, 0))
    across = lambda height: pl.BlockSpec((1, height, tile), lambda j: (0, 0, j))
    return pl.pallas_call(
        lambda *refs: early_back_kernel(seqs, block, *refs),
        name="early_back",
        grid=(width // tile,),
        out_shape=(
            outside((1, width, rows), BF16), jax.ShapeDtypeStruct((width, width), BF16),
            jax.ShapeDtypeStruct((1, 8, width), F32),
        ),
        in_specs=[
            flat, pl.BlockSpec((1, 8, tile), lambda j: (2, 0, j)), part, pl.BlockSpec((3, tile), lambda j: (0, j)),
            pl.BlockSpec((width, rows), lambda j: (0, 0)),
        ],
        out_specs=(part, pl.BlockSpec((width, tile), lambda j: (0, j)), across(8)),
        compiler_params=pltpu.CompilerParams(vmem_limit_bytes=18 << 20),
    )(grad, edges, mixed[None], short_weight, turned)


def late_back_kernel(
    seqs, block, side_ref, conv_ref, long_ref, skip_ref, factor_ref, edge_ref, mixed_ref, sw_ref, turned_ref,
    out_ref, given_ref, kept_ref, sums_ref,
):
    skip = columns(skip_ref)[:, 0:1]
    grad = (conv_ref[...].astype(F32) + long_ref[...].astype(F32) * skip) * factor_ref[0]
    weight = short_back_body(
        grad, edge_ref, mixed_ref, sw_ref, turned_ref, out_ref, sums_ref, seqs, block
    )

    @pl.when(pl.program_id(0) == 0)
    def _():
        given_ref[...] = weight

    @pl.when(pl.program_id(0) == 1)
    def _():
        kept_ref[...] = weight


def late_back(side, conv, grad_long, skip, factors, edges, mixed, short_weight, turned, seqs, block):
    count, width, rows = mixed.shape
    tile = 256
    steps = width // tile
    group = lambda i, side_ref: jnp.where(i == 0, 1 - side_ref[0], side_ref[0])
    part = pl.BlockSpec((1, tile, rows), lambda i, j, side_ref: (group(i, side_ref), j, 0))
    flat = pl.BlockSpec((tile, rows), lambda i, j, side_ref: (j, 0))
    across = pl.BlockSpec((1, 8, tile), lambda i, j, side_ref: (group(i, side_ref), 0, j))
    given = pl.BlockSpec((width, tile), lambda i, j, side_ref: (0, jnp.where(i == 0, j, steps - 1)))
    kept = pl.BlockSpec((width, tile), lambda i, j, side_ref: (0, jnp.where(i == 0, 0, j)))
    return pl.pallas_call(
        lambda *refs: late_back_kernel(seqs, block, *refs),
        name="late_back",
        out_shape=(
            outside((count, width, rows), BF16), jax.ShapeDtypeStruct((width, width), BF16), jax.ShapeDtypeStruct((width, width), BF16),
            jax.ShapeDtypeStruct((count, 8, width), F32),
        ),
        grid_spec=pltpu.PrefetchScalarGridSpec(
            num_scalar_prefetch=1,
            grid=(2, steps),
            in_specs=[
                flat, flat, pl.BlockSpec((tile,), lambda i, j, side_ref: (j,)), part, across, part,
                pl.BlockSpec((3, tile), lambda i, j, side_ref: (0, (1 + group(i, side_ref)) * steps + j)),
                pl.BlockSpec((width, rows), lambda i, j, side_ref: (0, 0)),
            ],
            out_specs=(part, given, kept, across),
        ),
        compiler_params=pltpu.CompilerParams(vmem_limit_bytes=20 << 20),
    )(side, conv, grad_long, skip, factors, edges, mixed, short_weight, turned)


def back_kernel(ga_ref, gb_ref, w_ref, tok_ref, resid_ref, gain_ref, bias_ref, out_ref, sums_ref):
    width = tok_ref.shape[1]
    turned = contract(w_ref[:, :width], ga_ref[0], ((1,), (0,)))
    for part in range(2):
        turned += contract(w_ref[:, (part + 1) * width : (part + 2) * width], gb_ref[part], ((1,), (0,)))
    q = turned.T
    gain = row(gain_ref)
    _, unit, inverse = norm_forward(tok_ref[...].astype(F32), gain, row(bias_ref))
    scaled = q * gain
    out_ref[...] = resid_ref[...] + inverse * (
        scaled
        - jnp.mean(scaled, axis=-1, keepdims=True)
        - unit * jnp.mean(scaled * unit, axis=-1, keepdims=True)
    )
    sums_ref[0:1] = jnp.sum(q * unit, axis=0, keepdims=True)
    sums_ref[1:2] = jnp.sum(q, axis=0, keepdims=True)
    sums_ref[2:8] = jnp.zeros((6, width), F32)


def back(mixed_early, mixed_late, w_in, tokens, grad_resid, gain, bias):
    return pl.pallas_call(
        back_kernel,
        name="back",
        out_shape=(
            jax.ShapeDtypeStruct(tokens.shape, F32), jax.ShapeDtypeStruct((8, tokens.shape[1]), F32),
        ),
        in_specs=[vmem_spec()] * 7,
        out_specs=(vmem_spec(), vmem_spec()),
        compiler_params=pltpu.CompilerParams(vmem_limit_bytes=26 << 20),
    )(mixed_early, mixed_late, w_in, tokens, grad_resid, gain, bias)


def transform_tables(block):
    spots = np.arange(block, dtype=np.float64)
    angle = np.pi / block * (spots[None, :] + 0.5) * spots[:, None]
    table = np.concatenate([np.cos(angle), -np.sin(angle)], axis=1)
    high = table.astype(np.float32).astype(jnp.bfloat16)
    low = (table - high.astype(np.float64)).astype(np.float32).astype(jnp.bfloat16)
    return np.stack([high, low])


def mm(left, right):
    return contract(left, right, ((1,), (0,)))


def spectrum(block, high, low):
    return mm(block, high) + mm(block, low)


def invert(spec, high, low):
    head = spec.astype(BF16)
    tail = (spec - head.astype(F32)).astype(BF16)
    back = lambda part, table: contract(part, table, ((1,), (1,)))
    return (back(head, high) + (back(tail, high) + back(head, low))) * (1.0 / high.shape[0])


def filter_spectra(filt_ref, high, low, g_ref, channels, blocks, length):
    sign = (1 - 2 * (lax.broadcasted_iota(jnp.int32, (1, length), 1) % 2)).astype(F32)
    before = None
    for lag in range(blocks):
        now = spectrum(filt_ref[:, lag * length : (lag + 1) * length], high, low)
        rows = slice(lag * channels, (lag + 1) * channels)
        if before is None:
            g_ref[rows, :] = now
        else:
            g_ref[rows, :length] = now[:, :length] - sign * before[:, length:]
            g_ref[rows, length:] = now[:, length:] + sign * before[:, :length]
        before = now


def conv_forward_kernel(
    channels, blocks, length, seqs,
    x_ref, filt_ref, table_ref, out_ref, s_ref, g_ref,
):
    high, low = table_ref[0], table_ref[1]
    filter_spectra(filt_ref, high, low, g_ref, channels, blocks, length)
    for q in range(seqs):
        s_ref[q] = spectrum(x_ref[:, q * length : (q + 1) * length], high, low)

    def tile(step, carry):
        row = pl.multiple_of(step * 8, 8)
        for lane in range(0, length, 128):
            re, im = slice(lane, lane + 128), slice(length + lane, length + lane + 128)
            for q in range(seqs):
                for i in reversed(range(blocks)):
                    acc_re = acc_im = None
                    for j in range(i + 1):
                        s_rows = pl.ds(j * channels + row, 8)
                        g_rows = pl.ds((i - j) * channels + row, 8)
                        sr, si = s_ref[q, s_rows, re], s_ref[q, s_rows, im]
                        gr, gi = g_ref[g_rows, re], g_ref[g_rows, im]
                        new_re = sr * gr - si * gi
                        new_im = sr * gi + si * gr
                        acc_re = new_re if acc_re is None else acc_re + new_re
                        acc_im = new_im if acc_im is None else acc_im + new_im
                    rows = pl.ds(i * channels + row, 8)
                    s_ref[q, rows, re] = acc_re
                    s_ref[q, rows, im] = acc_im
        return carry

    lax.fori_loop(0, channels // 8, tile, 0)
    for q in range(seqs):
        out_ref[:, q * length : (q + 1) * length] = invert(s_ref[q], high, low).astype(BF16)


def conv_backward_kernel(
    channels, blocks, length, seqs,
    x_ref, y_ref, filt_ref, table_ref, out_ref, gfilt_ref, s_ref, q_ref, g_ref, l_ref,
):
    high, low = table_ref[0], table_ref[1]
    filter_spectra(filt_ref, high, low, g_ref, channels, blocks, length)
    for q in range(seqs):
        s_ref[q] = spectrum(x_ref[:, q * length : (q + 1) * length], high, low)
        q_ref[q] = spectrum(y_ref[:, q * length : (q + 1) * length], high, low)

    def tile(step, carry):
        row = pl.multiple_of(step * 8, 8)
        for lane in range(0, length, 128):
            re, im = slice(lane, lane + 128), slice(length + lane, length + lane + 128)
            for d in range(blocks):
                acc_re = acc_im = None
                for q in range(seqs):
                    for j in range(blocks - d):
                        s_rows = pl.ds(j * channels + row, 8)
                        y_rows = pl.ds((j + d) * channels + row, 8)
                        sr, si = s_ref[q, s_rows, re], s_ref[q, s_rows, im]
                        yr, yi = q_ref[q, y_rows, re], q_ref[q, y_rows, im]
                        new_re = sr * yr + si * yi
                        new_im = sr * yi - si * yr
                        acc_re = new_re if acc_re is None else acc_re + new_re
                        acc_im = new_im if acc_im is None else acc_im + new_im
                rows = pl.ds(d * channels + row, 8)
                l_ref[rows, re] = acc_re
                l_ref[rows, im] = acc_im
            for q in range(seqs):
                for j in range(blocks):
                    acc_re = acc_im = None
                    for i in range(j, blocks):
                        y_rows = pl.ds(i * channels + row, 8)
                        g_rows = pl.ds((i - j) * channels + row, 8)
                        yr, yi = q_ref[q, y_rows, re], q_ref[q, y_rows, im]
                        gr, gi = g_ref[g_rows, re], g_ref[g_rows, im]
                        new_re = gr * yr + gi * yi
                        new_im = gr * yi - gi * yr
                        acc_re = new_re if acc_re is None else acc_re + new_re
                        acc_im = new_im if acc_im is None else acc_im + new_im
                    rows = pl.ds(j * channels + row, 8)
                    q_ref[q, rows, re] = acc_re
                    q_ref[q, rows, im] = acc_im
        return carry

    lax.fori_loop(0, channels // 8, tile, 0)
    for q in range(seqs):
        out_ref[:, q * length : (q + 1) * length] = invert(q_ref[q], high, low).astype(BF16)
    sign = (1 - 2 * (lax.broadcasted_iota(jnp.int32, (1, length), 1) % 2)).astype(F32)
    for d in range(blocks):
        rows = slice(d * channels, (d + 1) * channels)
        real, imag = l_ref[rows, :length], l_ref[rows, length:]
        if d + 1 < blocks:
            after = slice((d + 1) * channels, (d + 2) * channels)
            real = real + sign * l_ref[after, length:]
            imag = imag - sign * l_ref[after, :length]
        both = jnp.concatenate([real, imag], axis=1)
        gfilt_ref[:, d * length : (d + 1) * length] = invert(both, high, low)


def conv_forward(x, filt, table, channels, blocks, length, seqs):
    rows = blocks * channels
    kernel = lambda *refs: conv_forward_kernel(channels, blocks, length, seqs, *refs)
    return pl.pallas_call(
        kernel,
        name="conv_forward",
        out_shape=jax.ShapeDtypeStruct((rows, seqs * length), BF16),
        in_specs=[vmem_spec()] * 3,
        out_specs=vmem_spec(),
        scratch_shapes=[
            pltpu.VMEM((seqs, rows, 2 * length), F32),
            pltpu.VMEM((rows, 2 * length), F32),
        ],
        compiler_params=pltpu.CompilerParams(vmem_limit_bytes=18 << 20),
    )(x, filt, table)


def conv_backward(x, y, filt, table, channels, blocks, length, seqs):
    rows = blocks * channels
    kernel = lambda *refs: conv_backward_kernel(channels, blocks, length, seqs, *refs)
    return pl.pallas_call(
        kernel,
        name="conv_backward",
        out_shape=(
            outside((rows, seqs * length), BF16),
            jax.ShapeDtypeStruct((channels, blocks * length), F32),
        ),
        in_specs=[vmem_spec()] * 4,
        out_specs=(vmem_spec(), vmem_spec()),
        scratch_shapes=[
            pltpu.VMEM((seqs, rows, 2 * length), F32),
            pltpu.VMEM((seqs, rows, 2 * length), F32),
            pltpu.VMEM((rows, 2 * length), F32),
            pltpu.VMEM((rows, 2 * length), F32),
        ],
        compiler_params=pltpu.CompilerParams(vmem_limit_bytes=26 << 20),
    )(x, y, filt, table)


def shifted(block, axis, distance):
    count = lax.axis_size(axis)
    route = [(i - distance, i) for i in range(count) if 0 <= i - distance < count]
    return lax.ppermute(block, axis, route)


def axis_bits(axis):
    size, bits, bit = lax.axis_size(axis), [], 1
    while bit < size:
        bits.append((axis, bit))
        bit *= 2
    return bits


def exchange(value, step):
    axis, bit = step
    return lax.ppermute(value, axis, [(i, i ^ bit) for i in range(lax.axis_size(axis))])


def side_of(step):
    axis, bit = step
    return (lax.axis_index(axis) // bit) % 2


def fold_kernel(count, ways, sides_ref, *refs):
    ins, outs = refs[: 2 * ways * count], refs[2 * ways * count :]
    for i in range(ways * count):
        outs[i][...] = (
            ins[2 * i][...].astype(F32) + ins[2 * i + 1][...].astype(F32)
        ).astype(BF16)


def fold(pairs, steps):
    count = len(pairs)
    half = [pair[0].shape[0] // 2 for pair in pairs]
    if any(size % 16 for size in half):
        sums = [(kept.astype(F32) + other.astype(F32)).astype(BF16) for kept, other in pairs]
        if steps is None:
            return sums
        cut = lambda value, place, size: lax.dynamic_slice_in_dim(value, place * size, size, 0)
        return [
            (cut(value, 1 - side_of(step), size), cut(value, side_of(step), size))
            for value, step, size in zip(sums, steps, half)
        ]
    ways = 2 if steps else 1
    most = max(half) if steps else 2 * max(half)
    grid = most // 64 if most >= 192 and all(size == most for size in half) and most % 64 == 0 else 1
    shapes, in_specs, out_specs, args = [], [], [], []
    for i, ((kept, other), size) in enumerate(zip(pairs, half)):
        lanes = kept.shape[1]
        tile = (size if steps else 2 * size) // grid
        for way in range(ways):
            if steps:
                place = lambda j, sides_ref, i=i, way=way: (
                    (1 - sides_ref[i] if way == 0 else sides_ref[i]) * grid + j, 0
                )
            else:
                place = lambda j, sides_ref: (j, 0)
            in_specs += [pl.BlockSpec((tile, lanes), place)] * 2
            args += [kept, other]
            out_specs.append(pl.BlockSpec((tile, lanes), lambda j, sides_ref: (j, 0)))
            shapes.append(outside((tile * grid, lanes), BF16) if most >= 192 else jax.ShapeDtypeStruct((tile * grid, lanes), BF16))
    sides = jnp.stack([side_of(step) for step in steps] if steps else [jnp.zeros((), jnp.int32)])
    outs = pl.pallas_call(
        lambda *refs: fold_kernel(count, ways, *refs),
        name="fold",
        out_shape=shapes,
        grid_spec=pltpu.PrefetchScalarGridSpec(
            num_scalar_prefetch=1, grid=(grid,), in_specs=in_specs, out_specs=out_specs
        ),
        compiler_params=pltpu.CompilerParams(vmem_limit_bytes=14 << 20),
    )(sides.astype(jnp.int32), *args)
    return list(zip(outs[::2], outs[1::2])) if steps else list(outs)


def join_kernel(count, sides_ref, *refs):
    for i in range(count):
        out_ref = refs[2 * count + i]
        out_ref[sides_ref[i]] = refs[2 * i][...]
        out_ref[1 - sides_ref[i]] = refs[2 * i + 1][...]


def join(pairs, steps):
    count = len(pairs)
    if any(pair[0].shape[0] % 16 for pair in pairs):
        outs = []
        for (own, other), step in zip(pairs, steps):
            first = side_of(step) == 0
            outs.append(jnp.concatenate([jnp.where(first, own, other), jnp.where(first, other, own)]))
        return outs
    sides = jnp.stack([side_of(step) for step in steps]).astype(jnp.int32)
    grid = 3 if all(pair[0].shape[0] % 384 == 0 for pair in pairs) else 1
    in_specs, out_specs, shapes = [], [], []
    for own, _ in pairs:
        rows, lanes = own.shape
        in_specs += [pl.BlockSpec((rows // grid, lanes), lambda j: (j, 0))] * 2
        out_specs.append(pl.BlockSpec((2, rows // grid, lanes), lambda j: (0, j, 0)))
        shapes.append(jax.ShapeDtypeStruct((2, rows, lanes), BF16))
    outs = pl.pallas_call(
        lambda *refs: join_kernel(count, *refs),
        name="join",
        grid=(grid,),
        out_shape=shapes,
        in_specs=[smem_spec()] + in_specs,
        out_specs=out_specs,
        compiler_params=pltpu.CompilerParams(vmem_limit_bytes=8 << 20),
    )(sides, *[value for pair in pairs for value in pair])
    return [out.reshape(-1, out.shape[2]) for out in outs]


def quarters_do(row_side, lane_side, refs, put):
    for place, ref in enumerate(refs):
        h = row_side if place % 2 == 0 else 1 - row_side
        for l in range(2):

            @pl.when((lane_side == l) if place < 2 else (lane_side != l))
            def _():
                put(h, l, ref[...].astype(F32))


def widen_kernel(stacked, sides_ref, *refs):
    pieces, out_ref = refs[:4], refs[4]
    lanes = pieces[0].shape[1]

    def put(h, l, value):
        if stacked:
            width = lanes // out_ref.shape[1]
            for k in range(out_ref.shape[1]):
                out_ref[l, k, h] = value[:, k * width : (k + 1) * width]
        else:
            out_ref[h, :, l * lanes : (l + 1) * lanes] = value

    quarters_do(sides_ref[0], sides_ref[1], pieces, put)


def widen(sides, pieces, width, stacked):
    rows, lanes = pieces[0].shape
    tile = 64
    if stacked:
        count = lanes // width
        shape = (2, count, 2, rows, width)
        out = pl.BlockSpec((2, count, 2, tile, width), lambda j: (0, 0, 0, j, 0))
    else:
        shape = (2, rows, 2 * lanes)
        out = pl.BlockSpec((2, tile, 2 * lanes), lambda j: (0, j, 0))
    wide = pl.pallas_call(
        lambda *refs: widen_kernel(stacked, *refs),
        name="widen",
        grid=(rows // tile,),
        out_shape=jax.ShapeDtypeStruct(shape, F32),
        in_specs=[smem_spec()] + [pl.BlockSpec((tile, lanes), lambda j: (j, 0))] * 4,
        out_specs=out,
        compiler_params=pltpu.CompilerParams(vmem_limit_bytes=14 << 20),
    )(sides, *pieces)
    return wide.reshape(-1, shape[-1])


def widen_late_kernel(sides_ref, *refs):
    s_pieces, t_pieces, (in_ref, out_ref, last_ref) = refs[:4], refs[4:8], refs[8:]
    width = out_ref.shape[2]

    def put_s(h, l, value):
        in_ref[h, :, (l + 1) * width : (l + 2) * width] = value

    def put_t(h, l, value):
        if l == 0:
            in_ref[h, :, :width] = value[:, :width]
        else:
            out_ref[h] = value[:, :width]
        last_ref[l, h] = value[:, width:]

    quarters_do(sides_ref[0], sides_ref[1], s_pieces, put_s)
    quarters_do(sides_ref[2], sides_ref[1], t_pieces, put_t)


def widen_late(sides, s_pieces, t_pieces):
    rows, width = s_pieces[0].shape
    more = t_pieces[0].shape[1] - width
    tile = 64
    part = lambda lanes: pl.BlockSpec((tile, lanes), lambda j: (j, 0))
    both = lambda lanes: pl.BlockSpec((2, tile, lanes), lambda j: (0, j, 0))
    grad_in, grad_out, last = pl.pallas_call(
        widen_late_kernel,
        name="widen_late",
        grid=(rows // tile,),
        out_shape=(
            jax.ShapeDtypeStruct((2, rows, 3 * width), F32), jax.ShapeDtypeStruct((2, rows, width), F32),
            jax.ShapeDtypeStruct((2, 2, rows, more), F32),
        ),
        in_specs=[smem_spec()] + [part(width)] * 4 + [part(width + more)] * 4,
        out_specs=(
            both(3 * width), both(width), pl.BlockSpec((2, 2, tile, more), lambda j: (0, 0, j, 0)),
        ),
        compiler_params=pltpu.CompilerParams(vmem_limit_bytes=14 << 20),
    )(sides, *s_pieces, *t_pieces)
    return grad_in.reshape(-1, 3 * width), grad_out.reshape(-1, width), last.reshape(2, -1, more)


def unpack_kernel(features, hidden, wide, last_ref, net_ref, *refs):
    (g1, b1, b_in, sw, sb, fw1, fb1, fw2, fb2, fw3, skip, b_out, g2, b2, mb1, mb2) = refs
    width = g1.shape[0]
    fw3[...] = last_ref[0].T[:hidden]
    fw1[...] = net_ref[0, :features, :hidden]
    fb1[...] = net_ref[0, features : features + 1, :hidden].reshape(hidden)
    fw2[...] = net_ref[0, features + 1 : features + 1 + hidden, :hidden]
    fb2[...] = net_ref[0, features + 1 + hidden : features + 2 + hidden, :hidden].reshape(hidden)
    pieces = width // 128

    def put(ref, place, lane, row=None):
        for k in range(pieces):
            at = 128 + place * pieces + k
            value = net_ref[0, at : at + 1, :]
            lanes = slice(lane + k * 128, lane + (k + 1) * 128)
            if row is None:
                ref[lanes] = value.reshape(128)
            else:
                ref[row : row + 1, lanes] = value

    for place, ref in enumerate((skip, b_out, g2, b2, mb2)):
        put(ref, place, 0)
    for k in range(wide):
        put(mb1, 5 + k, k * width)
    put(g1, 5 + wide, 0)
    put(b1, 6 + wide, 0)
    for group in range(3):
        first = 7 + wide + 5 * group
        put(b_in, first, group * width)
        put(sb, first + 1, group * width)
        for tap in range(3):
            put(sw, first + 2 + tap, group * width, tap)


def unpack(last, features, hidden, wide, width):
    flat = lambda size: jax.ShapeDtypeStruct((size,), F32)
    grid = lambda *shape: jax.ShapeDtypeStruct(shape, F32)
    part = lambda h: pl.BlockSpec((1, width, 128), lambda i: (h, 0, 0))
    shapes = (
        flat(width), flat(width), flat(3 * width), grid(3, 3 * width), flat(3 * width),
        grid(features, hidden), flat(hidden), grid(hidden, hidden), flat(hidden), grid(hidden, width),
        flat(width), flat(width), flat(width), flat(width), flat(wide * width), flat(width),
    )
    whole = lambda shape: pl.BlockSpec(shape, lambda i: (0,) * len(shape))
    return pl.pallas_call(
        lambda *refs: unpack_kernel(features, hidden, wide, *refs),
        name="unpack",
        grid=(1,),
        out_shape=shapes,
        in_specs=[part(0), part(1)],
        out_specs=[whole(shape.shape) for shape in shapes],
        compiler_params=pltpu.CompilerParams(vmem_limit_bytes=14 << 20),
    )(last, last)


def orders():
    bits = axis_bits("bucket") + axis_bits("seq")
    first, rest = bits[0], bits[1:]
    if len(rest) == 4:
        y, x, near, far = rest
        turns = ([y, x, near, far], [x, y, near, far])
    else:
        turns = (rest, rest[1:] + rest[:1])
    return [[first] + turn for turn in turns]


def work_order(last):
    if last == 4:
        return [
            ("p", -3), ("s", 3), ("s", 4), ("s", 5), ("p", -2), ("s", -4), ("s", -3),
            ("last", 0), ("s", -2), ("wide", 0),
        ]
    order = [("p", index) for index in range(5, last + 2)]
    order += [("s", index) for index in range(2, last + 2)]
    order += [("p", -index) for index in range(last, 1, -1)]
    order += [("s", -index) for index in range(last, 1, -1)]
    return order + [("last", 0), ("wide", 0)]


def held(value, *awaited):
    return lax.optimization_barrier((value,) + awaited)[0]


def local(
    tokens, cotangent, lengths, decay_rate, norm1_gain, norm1_bias, w_in, b_in,
    short_weight, short_bias, filter_w1, filter_b1, filter_w2, filter_b2, filter_w3,
    skip_gain, w_out, b_out, norm2_gain, norm2_bias, mlp_w1, mlp_b1, mlp_w2, mlp_b2,
):
    seqs, block, width = tokens.shape[1:]
    rows = seqs * block
    blocks = lax.axis_size("seq")
    full = blocks * block
    channels = width // blocks
    position = lax.axis_index("seq")
    place = position.reshape(1).astype(jnp.int32)
    table = jnp.asarray(transform_tables(block))
    flat_tokens = tokens.reshape(rows, width)

    edge_tokens = shifted(tokens[0, :, block - 2 :, :], "seq", 1).reshape(2 * seqs, width)
    normed, edge_normed, mixed_late, factors, signal = front(
        place, flat_tokens, edge_tokens, norm1_gain, norm1_bias, b_in, short_bias, short_weight, w_in,
        seqs, block,
    )
    signal_all = lax.all_to_all(signal, "seq", 0, 0, tiled=True)
    turned, mixed_early, gate_out = gate_part(
        place, normed, edge_normed, b_in, short_bias, short_weight, w_in, seqs, block
    )

    own = position * channels
    rates = lax.dynamic_slice_in_dim(decay_rate, own, channels)
    weight_three = lax.dynamic_slice_in_dim(filter_w3.astype(F32), own, channels, axis=1)

    second_weight = filter_w2.astype(F32)
    feats, hidden_one, slope_one, hidden_two, slope_two = filter_layers(
        filter_w1.astype(F32), filter_b1.astype(F32), second_weight, filter_b2.astype(F32), full
    )
    times = lax.broadcasted_iota(jnp.int32, (1, full), 1).astype(F32) / full
    window = jnp.exp(-times * rates[:, None]) + 0.05
    filt = (precise("hd,hp->dp", weight_three, hidden_two) * window).astype(BF16)
    long_all = conv_forward(signal_all, filt, table, channels, blocks, block, seqs)
    conv_long = lax.all_to_all(long_all, "seq", 0, 0, tiled=True)

    order_p, order_q = orders()
    core = order_p[0]
    side = side_of(core).reshape(1).astype(jnp.int32)
    (
        output, grad_resid, grad_long, grad_gate, given_p, kept_p, given_q, kept_q, grad_w_out, sums,
        grad_b1,
    ) = middle(
        side, place, lengths.reshape(seqs), conv_long, signal, gate_out, skip_gain, flat_tokens,
        cotangent.reshape(rows, width), w_out, b_out, norm2_gain, norm2_bias, mlp_b2, mlp_b1[None], mlp_w1,
        mlp_w2, seqs, block,
    )
    grad_long_all = lax.all_to_all(grad_long, "seq", 0, 0, tiled=True)

    def turn(streams, index, *awaited):
        pairs, after = [], []
        for (given, kept), order in streams:
            if awaited:
                kept, awaited = held(kept, *awaited), ()
            pairs.append((kept, exchange(given, order[index])))
            after.append(order[index + 1] if index + 1 < len(order) else None)
        parts = fold(pairs, after if after[0] else None)
        return [(part, order) for part, (_, order) in zip(parts, streams)]

    def turn_back(streams, index, *awaited):
        pairs = []
        for part, order in streams:
            other = exchange(part, order[index])
            if awaited:
                part, awaited = held(part, *awaited), ()
            pairs.append((part, other))
        parts = join(pairs, [order[index] for _, order in streams])
        return [(part, order) for part, (_, order) in zip(parts, streams)]

    def quarters(streams, *awaited):
        others = [exchange(part, order[1]) for part, order in streams]
        if awaited:
            others = lax.optimization_barrier(tuple(others) + awaited)[: len(others)]
        return [
            [part, other, exchange(part, core), exchange(other, core)]
            for (part, _), other in zip(streams, others)
        ]

    def first_of(streams):
        value = streams[0][0]
        return value[0] if isinstance(value, tuple) else value

    last = len(order_p) - 1
    parts = turn([((given_p, kept_p), order_p), ((given_q, kept_q), order_q)], 0)
    grad_long_all = held(grad_long_all, first_of(parts))
    back_all, grad_filter = conv_backward(
        signal_all, grad_long_all, filt, table, channels, blocks, block, seqs
    )
    back_conv = lax.all_to_all(back_all, "seq", 0, 0, tiled=True)
    last_w3, net = filter_back(
        own.reshape(1).astype(jnp.int32), grad_filter, window, feats, hidden_one, slope_one, hidden_two,
        slope_two, second_weight, weight_three, width,
    )
    features, hidden = filter_w1.shape
    heads = features + hidden + 2
    parts = turn(parts, 1, last_w3)
    back_conv = held(back_conv, first_of(parts))
    edges = all_edges(back_conv, grad_long, skip_gain, factors, grad_gate, seqs, block)
    edges = shifted(edges, "seq", -1)
    parts = turn(parts, 2, edges)
    late_grads, given_s, kept_s, sums_late = late_back(
        side, held(back_conv, first_of(parts)), grad_long, skip_gain, factors, edges, mixed_late,
        short_weight, turned, seqs, block,
    )
    parts = turn(parts, 3, late_grads)
    gate_grads, w_in_early, sums_early = early_back(
        held(grad_gate, first_of(parts)), edges, mixed_early, short_weight, turned, seqs, block
    )
    stream_s = turn([((held(given_s, first_of(parts)), kept_s), order_p)], 0, gate_grads)
    if last == 4:
        parts = turn(parts, 4, first_of(stream_s))
    tokens_grad, sums_norm = back(
        gate_grads, held(late_grads, first_of(parts)), w_in, flat_tokens, grad_resid, norm1_gain,
        norm1_bias,
    )
    wide = grad_b1.shape[1] // width
    shorts = jnp.concatenate([sums_early, sums_late], axis=0)
    small = jnp.concatenate(
        [sums[:5], grad_b1.reshape(-1, width), sums_norm[:2], shorts[:, :5].reshape(-1, width)], axis=0
    )
    more = small.size // 128
    net = jnp.concatenate(
        [net, small.reshape(more, 128), jnp.zeros((width - 128 - more, 128), F32)], axis=0
    )
    part_t = choose(side, w_in_early, last_w3, grad_w_out, net)
    stream_t = turn([(part_t, order_q)], 0)
    token = first_of(stream_t)
    if last == 4:
        stream_s = turn(stream_s, 1, token)
        parts = turn_back(parts, 4, first_of(stream_s))
        stream_t = turn(stream_t, 1, first_of(parts))
        token = first_of(stream_t)
    state = {"p": parts, "s": stream_s + stream_t}
    for piece, index in work_order(last):
        if piece == "last":
            last_p, last_q = quarters(state["p"], token)
            token = last_q[1]
        elif piece == "wide":
            sides_of = lambda order: jnp.stack([side_of(order[1]), side_of(core)]).astype(jnp.int32)
            last_p[0] = held(last_p[0], token)
            sum_w1 = widen(sides_of(order_p), last_p, width, False)
            last_q[0] = held(last_q[0], sum_w1)
            sum_w2 = widen(sides_of(order_q), last_q, width, True)
            token = sum_w2
        elif index > 0:
            state[piece] = turn(state[piece], index - 1, token)
            token = first_of(state[piece])
        else:
            state[piece] = turn_back(state[piece], -index, token)
            token = first_of(state[piece])
    last_s, last_t = quarters(state["s"], token)
    sides = jnp.stack([side_of(order_p[1]), side_of(core), side_of(order_q[1])]).astype(jnp.int32)
    sum_w_in, sum_w_out, sum_last = widen_late(sides, last_s, last_t)
    small = unpack(sum_last, features, hidden, wide, width)
    return (
        output.reshape(tokens.shape), tokens_grad.reshape(tokens.shape), *small[:2], sum_w_in, *small[2:11],
        sum_w_out, *small[11:14], sum_w1, small[14], sum_w2, small[15],
    )


def solution(mesh):
    split = P("bucket", None, "seq", None)
    in_specs = (split, split, P("bucket", None)) + (P(),) * 21
    out_specs = (split, split) + (P(),) * 20
    return jax.shard_map(local, mesh=mesh, in_specs=in_specs, out_specs=out_specs, check_vma=False)
```

```python
import math

import jax
import jax.numpy as jnp
import numpy as np
from jax import lax
from jax.experimental import pallas as pl
from jax.experimental.pallas import tpu as pltpu
from jax.sharding import PartitionSpec as P

HIGH = lax.Precision.HIGHEST
EPSILON = 1e-05
F32 = jnp.float32
BF16 = jnp.bfloat16


def norm_forward(values, gain, bias):
    center = values - jnp.mean(values, axis=-1, keepdims=True)
    inverse = lax.rsqrt(jnp.mean(center * center, axis=-1, keepdims=True) + EPSILON)
    unit = center * inverse
    return (unit * gain + bias, unit, inverse)


def precise(formula, left, right):
    return jnp.einsum(formula, left, right, precision=HIGH, preferred_element_type=F32)


def position_features(length):
    steps = lax.broadcasted_iota(jnp.int32, (1, length), 1).astype(F32)
    bands = 0.0001 + lax.broadcasted_iota(jnp.int32, (16, 1), 0).astype(F32) * (
        (15.0 - 0.0001) / 15.0
    )
    phase = 2.0 * math.pi / length * steps * bands
    return jnp.concatenate([steps / length, jnp.cos(phase), -jnp.sin(phase)], axis=0)


def filter_layers(weight_one, bias_one, weight_two, bias_two, length):
    feats = position_features(length)
    first = precise("eh,ep->hp", weight_one, feats) + bias_one[:, None]
    hidden = jnp.sin(first)
    second = precise("hk,hp->kp", weight_two, hidden) + bias_two[:, None]
    return feats, hidden, jnp.cos(first), jnp.sin(second), jnp.cos(second)


def exact(left, right, dims):
    return lax.dot_general(
        left, right, (dims, ((), ())), precision=HIGH, preferred_element_type=F32
    )


def filter_back_kernel(
    channels, own_ref, grad_ref, window_ref, feats_ref, h1_ref, c1_ref, h2_ref, c2_ref, w2_ref, w3_ref,
    last_ref, net_ref,
):
    hidden = h1_ref.shape[0]
    features = feats_ref.shape[0]
    shaped = grad_ref[...] * window_ref[...]
    ones = jnp.ones((8, shaped.shape[1]), F32)
    last_ref[...] = jnp.zeros_like(last_ref)
    net_ref[...] = jnp.zeros_like(net_ref)
    rows = pl.ds(pl.multiple_of(own_ref[0], 16), channels)
    grad_w3 = exact(shaped, h2_ref[...], ((1,), (1,)))
    last_ref[rows, :] = jnp.concatenate([grad_w3, jnp.zeros_like(grad_w3)], axis=1).astype(BF16)
    second = exact(w3_ref[...], shaped, ((1,), (0,))) * c2_ref[...]
    first = exact(w2_ref[...], second, ((1,), (0,))) * c1_ref[...]
    place = 0
    for value in (
        exact(feats_ref[...], first, ((1,), (1,))), exact(ones, first, ((1,), (1,)))[:1],
        exact(h1_ref[...], second, ((1,), (1,))), exact(ones, second, ((1,), (1,)))[:1],
    ):
        net_ref[place : place + value.shape[0], :hidden] = value
        place += value.shape[0]


def filter_back(own, grad, window, feats, h1, c1, h2, c2, w2, w3, width):
    channels = grad.shape[0]
    return pl.pallas_call(
        lambda *refs: filter_back_kernel(channels, *refs),
        name="filter_back",
        out_shape=(
            jax.ShapeDtypeStruct((width, 128), BF16), jax.ShapeDtypeStruct((128, 128), F32),
        ),
        in_specs=[smem_spec()] + [vmem_spec()] * 9,
        out_specs=(vmem_spec(), vmem_spec()),
        compiler_params=pltpu.CompilerParams(vmem_limit_bytes=14 << 20),
    )(own, grad, window, feats, h1, c1, h2, c2, w2, w3)


def choose_kernel(side_ref, early_ref, last_ref, out_ref, net_ref, given_ref, kept_ref):
    low_side = side_ref[0] == 0
    width = early_ref.shape[1]
    parts = (
        (early_ref[...], out_ref[...], slice(0, width)),
        (last_ref[...], net_ref[...].astype(BF16), slice(width, width + 128)),
    )
    for low_half, high_half, lanes in parts:
        given_ref[:, lanes] = jnp.where(low_side, high_half, low_half)
        kept_ref[:, lanes] = jnp.where(low_side, low_half, high_half)


def choose(side, early, last, grad_out, net):
    width = early.shape[0]
    tile = 128
    part = lambda lanes: pl.BlockSpec((tile, lanes), lambda j: (j, 0))
    shape = jax.ShapeDtypeStruct((width, width + 128), BF16)
    return tuple(
        pl.pallas_call(
            choose_kernel,
            name="choose",
            grid=(width // tile,),
            out_shape=(shape, shape),
            in_specs=[smem_spec(), part(width), part(128), part(width), part(128)],
            out_specs=(part(width + 128), part(width + 128)),
            compiler_params=pltpu.CompilerParams(vmem_limit_bytes=8 << 20),
        )(side, early, last, grad_out, net)
    )


def outside(shape, dtype):
    return pltpu.HBM(shape, dtype)


def vmem_spec():
    return pl.BlockSpec(memory_space=pltpu.VMEM)


def smem_spec():
    return pl.BlockSpec(memory_space=pltpu.SMEM)


def contract(left, right, dims):
    return lax.dot_general(left, right, (dims, ((), ())), preferred_element_type=F32)


def lane_sums(parts):
    ones = jnp.ones((8, 128), BF16)
    rows = []
    for part in parts:
        folded = part[:, :128]
        for lane in range(128, part.shape[1], 128):
            folded = folded + part[:, lane : lane + 128]
        head = folded.astype(BF16)
        tail = (folded - head.astype(F32)).astype(BF16)
        both = contract(ones, head, ((1,), (1,))) + contract(ones, tail, ((1,), (1,)))
        rows.append(both[:1])
    return rows


def columns(*rows):
    parts = [row[...].astype(F32).reshape(-1, row.shape[-1]) for row in rows]
    count = sum(part.shape[0] for part in parts)
    parts.append(jnp.zeros((8 - count, parts[0].shape[1]), F32))
    return jnp.concatenate(parts, axis=0).T


def row(ref):
    return ref[...].astype(F32).reshape(1, ref.shape[0])


def short_filter(mixed, edge, cols, seqs, block):
    spots = lax.broadcasted_iota(jnp.int32, (1, block), 1)
    pieces = []
    for q in range(seqs):
        now = mixed[:, q * block : (q + 1) * block]
        near, far = edge[:, 2 * q + 1 : 2 * q + 2], edge[:, 2 * q : 2 * q + 1]
        once = jnp.where(spots == 0, near, pltpu.roll(now, 1, 1))
        twice = jnp.where(spots == 0, far, jnp.where(spots == 1, near, pltpu.roll(now, 2, 1)))
        pieces.append(
            cols[:, 2:3] * now + cols[:, 3:4] * once + cols[:, 4:5] * twice + cols[:, 1:2]
        )
    return jnp.concatenate(pieces, axis=1)


def project(weight, normed, edge_normed, cols, inside, seqs, block):
    mixed = (contract(weight, normed, ((0,), (1,))) + cols[:, 0:1]).astype(BF16)
    edge = (contract(weight, edge_normed, ((0,), (1,))) + cols[:, 0:1]).astype(BF16)
    edge = edge.astype(F32) * inside
    return mixed, short_filter(mixed.astype(F32), edge, cols, seqs, block)


def front_kernel(
    seqs, block, first_ref, tok_ref, edge_ref, gain_ref, bias_ref, bb_ref, bc_ref, sbb_ref, sbc_ref, swb_ref,
    swc_ref, wb_ref, wc_ref, normed_ref, edge_normed_ref, mixed_ref, factor_ref, signal_ref,
):
    @pl.when(pl.program_id(0) == 0)
    def _():
        gain, bias = row(gain_ref), row(bias_ref)
        normed_ref[...] = norm_forward(tok_ref[...].astype(F32), gain, bias)[0].astype(BF16)
        edge_normed_ref[...] = norm_forward(edge_ref[...].astype(F32), gain, bias)[0].astype(BF16)

    normed, edge_normed = normed_ref[...], edge_normed_ref[...]
    inside = (first_ref[0] > 0).astype(F32)
    mixed_ref[0], gate_in = project(
        wb_ref[...], normed, edge_normed, columns(bb_ref, sbb_ref, swb_ref), inside, seqs, block
    )
    mixed_ref[1], values = project(
        wc_ref[...], normed, edge_normed, columns(bc_ref, sbc_ref, swc_ref), inside, seqs, block
    )
    factor_ref[0] = values
    factor_ref[1] = gate_in
    signal_ref[...] = (gate_in * values).astype(BF16)


def front(position, tokens, edge, gain, bias, b_in, short_bias, short_weight, w_in, seqs, block):
    rows, width = tokens.shape
    tile = 256
    steps = width // tile
    fixed = lambda shape: pl.BlockSpec(shape, lambda j: (0,) * len(shape))
    weight = lambda part: pl.BlockSpec((width, tile), lambda j: (0, part * steps + j))
    flat = lambda part: pl.BlockSpec((tile,), lambda j: (part * steps + j,))
    taps = lambda part: pl.BlockSpec((3, tile), lambda j: (0, part * steps + j))
    both = pl.BlockSpec((2, tile, rows), lambda j: (0, j, 0))
    return pl.pallas_call(
        lambda *refs: front_kernel(seqs, block, *refs),
        name="front",
        grid=(steps,),
        out_shape=(
            jax.ShapeDtypeStruct((rows, width), BF16), jax.ShapeDtypeStruct(edge.shape, BF16),
            jax.ShapeDtypeStruct((2, width, rows), BF16), jax.ShapeDtypeStruct((2, width, rows), F32),
            jax.ShapeDtypeStruct((width, rows), BF16),
        ),
        in_specs=[
            smem_spec(), fixed((rows, width)), fixed(edge.shape), fixed(gain.shape), fixed(bias.shape),
            flat(1), flat(2), flat(1), flat(2), taps(1), taps(2), weight(1), weight(2),
        ],
        out_specs=(
            fixed((rows, width)), fixed(edge.shape), both, both,
            pl.BlockSpec((tile, rows), lambda j: (j, 0)),
        ),
        compiler_params=pltpu.CompilerParams(vmem_limit_bytes=58 << 20),
    )(
        position, tokens, edge, gain, bias, b_in, b_in, short_bias, short_bias, short_weight,
        short_weight, w_in, w_in,
    )


def gate_kernel(
    seqs, block, first_ref, normed_ref, edge_normed_ref, b_ref, sb_ref, sw_ref, w_ref, turned_ref,
    mixed_ref, gate_ref,
):
    normed = normed_ref[...]

    @pl.when(pl.program_id(0) == 0)
    def _():
        turned_ref[...] = normed.T

    inside = (first_ref[0] > 0).astype(F32)
    mixed_ref[...], gate_ref[...] = project(
        w_ref[...], normed, edge_normed_ref[...], columns(b_ref, sb_ref, sw_ref), inside, seqs, block
    )


def gate_part(position, normed, edge_normed, b_in, short_bias, short_weight, w_in, seqs, block):
    rows, width = normed.shape
    tile = 256
    fixed = lambda shape: pl.BlockSpec(shape, lambda j: (0,) * len(shape))
    flat = pl.BlockSpec((tile,), lambda j: (j,))
    out = pl.BlockSpec((tile, rows), lambda j: (j, 0))
    return pl.pallas_call(
        lambda *refs: gate_kernel(seqs, block, *refs),
        name="gate_part",
        grid=(width // tile,),
        out_shape=(
            jax.ShapeDtypeStruct((width, rows), BF16), jax.ShapeDtypeStruct((width, rows), BF16),
            jax.ShapeDtypeStruct((width, rows), F32),
        ),
        in_specs=[
            smem_spec(), fixed((rows, width)), fixed(edge_normed.shape), flat, flat,
            pl.BlockSpec((3, tile), lambda j: (0, j)), pl.BlockSpec((width, tile), lambda j: (0, j)),
        ],
        out_specs=(fixed((width, rows)), out, out),
        compiler_params=pltpu.CompilerParams(vmem_limit_bytes=58 << 20),
    )(position, normed, edge_normed, b_in, short_bias, short_weight, w_in)


def row_mask(position, lengths_ref, seqs, block):
    spots = position * block + lax.broadcasted_iota(jnp.int32, (block, 1), 0)
    return jnp.concatenate([(spots < lengths_ref[q]).astype(F32) for q in range(seqs)], axis=0)


def middle_kernel(
    seqs, block, side_ref, position_ref, lengths_ref, conv_ref, signal_ref, gate_ref, skip_ref, tok_ref,
    cot_ref, w_out_ref, b_out_ref, gain_ref, bias_ref, b2_ref, b1_ref, w1_ref, w2_ref,
    out_ref, resid_grad_ref, long_ref, gate_grad_ref, given1_ref, kept1_ref, given2_ref, kept2_ref,
    gwo_ref, sums_ref, gb1_ref,
    gated_ref, n2_ref, n2t_ref, unit_ref, inv_ref, final_ref, gf_ref, q_ref, lout_ref,
):
    step = pl.program_id(0)
    last = pl.num_programs(0) - 1
    b_out, gain, bias, b2 = row(b_out_ref), row(gain_ref), row(bias_ref), row(b2_ref)

    @pl.when(step == 0)
    def _():
        skip = columns(skip_ref)[:, 0:1]
        long_out = conv_ref[...].astype(F32) + signal_ref[...].astype(F32) * skip
        lout_ref[...] = long_out
        gated = (long_out * gate_ref[...]).astype(BF16)
        gated_ref[...] = gated
        branch = contract(gated, w_out_ref[...], ((0,), (0,))) + b_out
        resid = tok_ref[...].astype(F32) + branch
        normed, unit, inverse = norm_forward(resid, gain, bias)
        n2_ref[...] = normed.astype(BF16)
        n2t_ref[...] = normed.astype(BF16).T
        unit_ref[...] = unit
        inv_ref[...] = jnp.broadcast_to(inverse, inv_ref.shape)
        final_ref[...] = resid + b2
        valid = row_mask(position_ref[0], lengths_ref, seqs, block)
        gf_ref[...] = (cot_ref[...].astype(F32) * valid).astype(BF16)
        q_ref[...] = jnp.zeros_like(q_ref)

    w1, w2, gf = w1_ref[...], w2_ref[...], gf_ref[...]
    pre = contract(n2_ref[...], w1, ((1,), (0,))) + b1_ref[...].astype(F32)
    grad_active = contract(gf, w2, ((1,), (1,)))
    cumulative, slope = normal_terms(pre)
    active = (pre * cumulative).astype(BF16)
    grad_pre = grad_active * slope
    grad_low = grad_pre.astype(BF16)
    final_ref[...] += contract(active, w2, ((1,), (0,)))
    q_ref[...] += contract(grad_low, w1, ((1,), (1,)))
    grad_two = contract(active, gf, ((0,), (0,))).astype(BF16)
    grad_one = contract(n2t_ref[...], grad_low, ((1,), (0,))).astype(BF16)

    @pl.when(step <= last // 2)
    def _():
        given1_ref[...] = grad_one
        given2_ref[...] = grad_two

    @pl.when(step > last // 2)
    def _():
        kept1_ref[...] = grad_one
        kept2_ref[...] = grad_two

    gb1_ref[...] = jnp.sum(grad_low.astype(F32), axis=0, keepdims=True)

    @pl.when(step == last)
    def _():
        valid = row_mask(position_ref[0], lengths_ref, seqs, block)
        out_ref[...] = (final_ref[...] * valid).astype(BF16)
        grad_final = gf_ref[...].astype(F32)
        q, unit = q_ref[...], unit_ref[...]
        scaled = q * gain
        grad_resid = grad_final + inv_ref[:, 0:1] * (
            scaled
            - jnp.mean(scaled, axis=-1, keepdims=True)
            - unit * jnp.mean(scaled * unit, axis=-1, keepdims=True)
        )
        resid_grad_ref[...] = grad_resid
        grad_branch = grad_resid.astype(BF16)
        grad_gated = contract(w_out_ref[...], grad_branch, ((1,), (1,)))
        grad_long = (grad_gated * gate_ref[...]).astype(BF16)
        long_ref[...] = grad_long
        gate_grad_ref[...] = grad_gated * lout_ref[...]
        gwo_ref[...] = contract(gated_ref[...], grad_branch, ((1,), (0,))).astype(BF16)
        skip_sum = lane_sums([grad_long.astype(F32) * signal_ref[...].astype(F32)])[0]
        total = lambda part: jnp.sum(part, axis=0, keepdims=True)
        sums_ref[0:1] = skip_sum
        sums_ref[1:2] = total(grad_branch.astype(F32))
        sums_ref[2:3] = total(q * unit)
        sums_ref[3:4] = total(q)
        sums_ref[4:5] = total(grad_final)
        sums_ref[5:8] = jnp.zeros((3, sums_ref.shape[1]), F32)


def normal_terms(pre):
    cumulative = 0.5 * (1.0 + lax.erf(pre * (1.0 / math.sqrt(2.0))))
    density = jnp.exp(-0.5 * pre * pre) * (1.0 / math.sqrt(2.0 * math.pi))
    return cumulative, cumulative + pre * density


def middle(
    side, position, lengths, conv, signal, gate, skip, tokens, cotangent, w_out, b_out, gain, bias, b2, b1, w1,
    w2, seqs, block,
):
    count, width = tokens.shape
    hidden = w1.shape[1]
    chunk = width
    steps = hidden // chunk
    half = steps // 2
    once = lambda shape: pl.BlockSpec(
        shape, lambda j, side_ref: (0,) * len(shape), pipeline_mode=pl.Buffered(1)
    )

    def which(j, side_ref):
        side = side_ref[0]
        return jnp.where(j < half, half * (1 - side) + j, half * side + j - half)

    across = lambda height: pl.BlockSpec((height, chunk), lambda j, side_ref: (0, which(j, side_ref)))
    given = pl.BlockSpec((width, chunk), lambda j, side_ref: (0, jnp.minimum(j, half - 1)))
    kept = pl.BlockSpec((width, chunk), lambda j, side_ref: (0, jnp.maximum(j - half, 0)))
    wide, tall = (count, width), (width, count)
    shape = jax.ShapeDtypeStruct
    scratch = pltpu.VMEM
    part = shape((width, half * chunk), BF16)
    return pl.pallas_call(
        lambda *refs: middle_kernel(seqs, block, *refs),
        name="middle",
        out_shape=(
            shape(wide, BF16), shape(wide, F32), shape(tall, BF16), shape(tall, F32),
            part, part, part, part, shape((width, width), BF16),
            shape((8, width), F32), shape((1, hidden), F32),
        ),
        grid_spec=pltpu.PrefetchScalarGridSpec(
            num_scalar_prefetch=1,
            grid=(steps,),
            in_specs=[
                smem_spec(), smem_spec(), once(tall), once(tall), once(tall), once(skip.shape),
                once(wide), once(wide), once((width, width)), once(b_out.shape), once(gain.shape),
                once(bias.shape), once(b2.shape),
                across(1), across(width),
                pl.BlockSpec((chunk, width), lambda j, side_ref: (which(j, side_ref), 0)),
            ],
            out_specs=(
                once(wide), once(wide), once(tall), once(tall), given, kept, given, kept,
                once((width, width)), once((8, width)), across(1),
            ),
            scratch_shapes=[
                scratch(tall, BF16), scratch(wide, BF16), scratch(tall, BF16), scratch(wide, F32),
                scratch((count, 128), F32), scratch(wide, F32), scratch(wide, BF16), scratch(wide, F32),
                scratch(tall, F32),
            ],
        ),
        compiler_params=pltpu.CompilerParams(vmem_limit_bytes=58 << 20),
    )(
        side, position, lengths, conv, signal, gate, skip, tokens, cotangent, w_out, b_out, gain, bias, b2, b1,
        w1, w2,
    )


def first_spots(heads):
    lanes = lax.broadcasted_iota(jnp.int32, (1, 128), 1)
    edge = jnp.zeros(heads[0].shape, F32)
    for q, head in enumerate(heads):
        head = pltpu.roll(head, 2 * q, 1) if q else head
        edge = jnp.where((lanes >= 2 * q) & (lanes < 2 * q + 2), head, edge)
    return edge.T[:8]


def edges_kernel(seqs, skip_ref, *refs):
    skip = columns(skip_ref)[:, 0:1]
    out_ref = refs[-1]
    signals = [
        refs[4 * q][...].astype(F32) + refs[4 * q + 1][...].astype(F32) * skip for q in range(seqs)
    ]
    for part in range(2):
        out_ref[part] = first_spots([signals[q] * refs[4 * q + 2][part] for q in range(seqs)])
    out_ref[2] = first_spots([refs[4 * q + 3][...] for q in range(seqs)])


def all_edges(conv, grad_long, skip, factors, gate, seqs, block):
    width = conv.shape[0]
    specs, args = [], []
    for q in range(seqs):
        place = q * block // 128
        flat = pl.BlockSpec((width, 128), lambda i, place=place: (0, place))
        specs += [flat, flat, pl.BlockSpec((2, width, 128), lambda i, place=place: (0, 0, place)), flat]
        args += [conv, grad_long, factors, gate]
    return pl.pallas_call(
        lambda *refs: edges_kernel(seqs, *refs),
        name="all_edges",
        grid=(1,),
        out_shape=jax.ShapeDtypeStruct((3, 8, width), F32),
        in_specs=[pl.BlockSpec(skip.shape, lambda i: (0,))] + specs,
        out_specs=pl.BlockSpec((3, 8, width), lambda i: (0, 0, 0)),
        compiler_params=pltpu.CompilerParams(vmem_limit_bytes=14 << 20),
    )(skip, *args)


def short_back_body(grad, edge_ref, mixed_ref, sw_ref, turned_ref, out_ref, sums_ref, seqs, block):
    taps = columns(sw_ref)
    edge = edge_ref[0].T
    spots = lax.broadcasted_iota(jnp.int32, (1, block), 1)
    mixed = mixed_ref[0].astype(F32)
    once, twice = [], []
    for q in range(seqs):
        now = grad[:, q * block : (q + 1) * block]
        near, far = edge[:, 2 * q : 2 * q + 1], edge[:, 2 * q + 1 : 2 * q + 2]
        end = block - 1
        once.append(jnp.where(spots == end, near, pltpu.roll(now, block - 1, 1)))
        twice.append(
            jnp.where(
                spots == end, far, jnp.where(spots == end - 1, near, pltpu.roll(now, block - 2, 1))
            )
        )
    once, twice = jnp.concatenate(once, axis=1), jnp.concatenate(twice, axis=1)
    low = (taps[:, 0:1] * grad + taps[:, 1:2] * once + taps[:, 2:3] * twice).astype(BF16)
    out_ref[0] = low
    parts = [low.astype(F32), grad, mixed * grad, mixed * once, mixed * twice]
    for place, total in enumerate(lane_sums(parts)):
        sums_ref[0, place : place + 1] = total
    sums_ref[0, 5:8] = jnp.zeros((3, sums_ref.shape[2]), F32)
    return contract(turned_ref[...], low, ((1,), (1,))).astype(BF16)


def early_back_kernel(
    seqs, block, grad_ref, edge_ref, mixed_ref, sw_ref, turned_ref, out_ref, gw_ref, sums_ref
):
    gw_ref[...] = short_back_body(
        grad_ref[...], edge_ref, mixed_ref, sw_ref, turned_ref, out_ref, sums_ref, seqs, block
    )


def early_back(grad, edges, mixed, short_weight, turned, seqs, block):
    width, rows = grad.shape
    tile = 256
    flat = pl.BlockSpec((tile, rows), lambda j: (j, 0))
    part = pl.BlockSpec((1, tile, rows), lambda j: (0, j, 0))
    across = lambda height: pl.BlockSpec((1, height, tile), lambda j: (0, 0, j))
    return pl.pallas_call(
        lambda *refs: early_back_kernel(seqs, block, *refs),
        name="early_back",
        grid=(width // tile,),
        out_shape=(
            outside((1, width, rows), BF16), jax.ShapeDtypeStruct((width, width), BF16),
            jax.ShapeDtypeStruct((1, 8, width), F32),
        ),
        in_specs=[
            flat, pl.BlockSpec((1, 8, tile), lambda j: (2, 0, j)), part, pl.BlockSpec((3, tile), lambda j: (0, j)),
            pl.BlockSpec((width, rows), lambda j: (0, 0)),
        ],
        out_specs=(part, pl.BlockSpec((width, tile), lambda j: (0, j)), across(8)),
        compiler_params=pltpu.CompilerParams(vmem_limit_bytes=18 << 20),
    )(grad, edges, mixed[None], short_weight, turned)


def late_back_kernel(
    seqs, block, side_ref, conv_ref, long_ref, skip_ref, factor_ref, edge_ref, mixed_ref, sw_ref, turned_ref,
    out_ref, given_ref, kept_ref, sums_ref,
):
    skip = columns(skip_ref)[:, 0:1]
    grad = (conv_ref[...].astype(F32) + long_ref[...].astype(F32) * skip) * factor_ref[0]
    weight = short_back_body(
        grad, edge_ref, mixed_ref, sw_ref, turned_ref, out_ref, sums_ref, seqs, block
    )

    @pl.when(pl.program_id(0) == 0)
    def _():
        given_ref[...] = weight

    @pl.when(pl.program_id(0) == 1)
    def _():
        kept_ref[...] = weight


def late_back(side, conv, grad_long, skip, factors, edges, mixed, short_weight, turned, seqs, block):
    count, width, rows = mixed.shape
    tile = 256
    steps = width // tile
    group = lambda i, side_ref: jnp.where(i == 0, 1 - side_ref[0], side_ref[0])
    part = pl.BlockSpec((1, tile, rows), lambda i, j, side_ref: (group(i, side_ref), j, 0))
    flat = pl.BlockSpec((tile, rows), lambda i, j, side_ref: (j, 0))
    across = pl.BlockSpec((1, 8, tile), lambda i, j, side_ref: (group(i, side_ref), 0, j))
    given = pl.BlockSpec((width, tile), lambda i, j, side_ref: (0, jnp.where(i == 0, j, steps - 1)))
    kept = pl.BlockSpec((width, tile), lambda i, j, side_ref: (0, jnp.where(i == 0, 0, j)))
    return pl.pallas_call(
        lambda *refs: late_back_kernel(seqs, block, *refs),
        name="late_back",
        out_shape=(
            outside((count, width, rows), BF16), jax.ShapeDtypeStruct((width, width), BF16), jax.ShapeDtypeStruct((width, width), BF16),
            jax.ShapeDtypeStruct((count, 8, width), F32),
        ),
        grid_spec=pltpu.PrefetchScalarGridSpec(
            num_scalar_prefetch=1,
            grid=(2, steps),
            in_specs=[
                flat, flat, pl.BlockSpec((tile,), lambda i, j, side_ref: (j,)), part, across, part,
                pl.BlockSpec((3, tile), lambda i, j, side_ref: (0, (1 + group(i, side_ref)) * steps + j)),
                pl.BlockSpec((width, rows), lambda i, j, side_ref: (0, 0)),
            ],
            out_specs=(part, given, kept, across),
        ),
        compiler_params=pltpu.CompilerParams(vmem_limit_bytes=20 << 20),
    )(side, conv, grad_long, skip, factors, edges, mixed, short_weight, turned)


def back_kernel(ga_ref, gb_ref, w_ref, tok_ref, resid_ref, gain_ref, bias_ref, out_ref, sums_ref):
    width = tok_ref.shape[1]
    turned = contract(w_ref[:, :width], ga_ref[0], ((1,), (0,)))
    for part in range(2):
        turned += contract(w_ref[:, (part + 1) * width : (part + 2) * width], gb_ref[part], ((1,), (0,)))
    q = turned.T
    gain = row(gain_ref)
    _, unit, inverse = norm_forward(tok_ref[...].astype(F32), gain, row(bias_ref))
    scaled = q * gain
    out_ref[...] = resid_ref[...] + inverse * (
        scaled
        - jnp.mean(scaled, axis=-1, keepdims=True)
        - unit * jnp.mean(scaled * unit, axis=-1, keepdims=True)
    )
    sums_ref[0:1] = jnp.sum(q * unit, axis=0, keepdims=True)
    sums_ref[1:2] = jnp.sum(q, axis=0, keepdims=True)
    sums_ref[2:8] = jnp.zeros((6, width), F32)


def back(mixed_early, mixed_late, w_in, tokens, grad_resid, gain, bias):
    return pl.pallas_call(
        back_kernel,
        name="back",
        out_shape=(
            jax.ShapeDtypeStruct(tokens.shape, F32), jax.ShapeDtypeStruct((8, tokens.shape[1]), F32),
        ),
        in_specs=[vmem_spec()] * 7,
        out_specs=(vmem_spec(), vmem_spec()),
        compiler_params=pltpu.CompilerParams(vmem_limit_bytes=26 << 20),
    )(mixed_early, mixed_late, w_in, tokens, grad_resid, gain, bias)


def transform_tables(block):
    spots = np.arange(block, dtype=np.float64)
    angle = np.pi / block * (spots[None, :] + 0.5) * spots[:, None]
    table = np.concatenate([np.cos(angle), -np.sin(angle)], axis=1)
    high = table.astype(np.float32).astype(jnp.bfloat16)
    low = (table - high.astype(np.float64)).astype(np.float32).astype(jnp.bfloat16)
    return np.stack([high, low])


def mm(left, right):
    return contract(left, right, ((1,), (0,)))


def spectrum(block, high, low):
    return mm(block, high) + mm(block, low)


def invert(spec, high, low):
    head = spec.astype(BF16)
    tail = (spec - head.astype(F32)).astype(BF16)
    back = lambda part, table: contract(part, table, ((1,), (1,)))
    return (back(head, high) + (back(tail, high) + back(head, low))) * (1.0 / high.shape[0])


def filter_spectra(filt_ref, high, low, g_ref, channels, blocks, length):
    sign = (1 - 2 * (lax.broadcasted_iota(jnp.int32, (1, length), 1) % 2)).astype(F32)
    before = None
    for lag in range(blocks):
        now = spectrum(filt_ref[:, lag * length : (lag + 1) * length], high, low)
        rows = slice(lag * channels, (lag + 1) * channels)
        if before is None:
            g_ref[rows, :] = now
        else:
            g_ref[rows, :length] = now[:, :length] - sign * before[:, length:]
            g_ref[rows, length:] = now[:, length:] + sign * before[:, :length]
        before = now


def conv_forward_kernel(
    channels, blocks, length, seqs,
    x_ref, filt_ref, table_ref, out_ref, s_ref, g_ref,
):
    high, low = table_ref[0], table_ref[1]
    filter_spectra(filt_ref, high, low, g_ref, channels, blocks, length)
    for q in range(seqs):
        s_ref[q] = spectrum(x_ref[:, q * length : (q + 1) * length], high, low)

    def tile(step, carry):
        row = pl.multiple_of(step * 8, 8)
        for lane in range(0, length, 128):
            re, im = slice(lane, lane + 128), slice(length + lane, length + lane + 128)
            for q in range(seqs):
                for i in reversed(range(blocks)):
                    acc_re = acc_im = None
                    for j in range(i + 1):
                        s_rows = pl.ds(j * channels + row, 8)
                        g_rows = pl.ds((i - j) * channels + row, 8)
                        sr, si = s_ref[q, s_rows, re], s_ref[q, s_rows, im]
                        gr, gi = g_ref[g_rows, re], g_ref[g_rows, im]
                        new_re = sr * gr - si * gi
                        new_im = sr * gi + si * gr
                        acc_re = new_re if acc_re is None else acc_re + new_re
                        acc_im = new_im if acc_im is None else acc_im + new_im
                    rows = pl.ds(i * channels + row, 8)
                    s_ref[q, rows, re] = acc_re
                    s_ref[q, rows, im] = acc_im
        return carry

    lax.fori_loop(0, channels // 8, tile, 0)
    for q in range(seqs):
        out_ref[:, q * length : (q + 1) * length] = invert(s_ref[q], high, low).astype(BF16)


def conv_backward_kernel(
    channels, blocks, length, seqs,
    x_ref, y_ref, filt_ref, table_ref, out_ref, gfilt_ref, s_ref, q_ref, g_ref, l_ref,
):
    high, low = table_ref[0], table_ref[1]
    filter_spectra(filt_ref, high, low, g_ref, channels, blocks, length)
    for q in range(seqs):
        s_ref[q] = spectrum(x_ref[:, q * length : (q + 1) * length], high, low)
        q_ref[q] = spectrum(y_ref[:, q * length : (q + 1) * length], high, low)

    def tile(step, carry):
        row = pl.multiple_of(step * 8, 8)
        for lane in range(0, length, 128):
            re, im = slice(lane, lane + 128), slice(length + lane, length + lane + 128)
            for d in range(blocks):
                acc_re = acc_im = None
                for q in range(seqs):
                    for j in range(blocks - d):
                        s_rows = pl.ds(j * channels + row, 8)
                        y_rows = pl.ds((j + d) * channels + row, 8)
                        sr, si = s_ref[q, s_rows, re], s_ref[q, s_rows, im]
                        yr, yi = q_ref[q, y_rows, re], q_ref[q, y_rows, im]
                        new_re = sr * yr + si * yi
                        new_im = sr * yi - si * yr
                        acc_re = new_re if acc_re is None else acc_re + new_re
                        acc_im = new_im if acc_im is None else acc_im + new_im
                rows = pl.ds(d * channels + row, 8)
                l_ref[rows, re] = acc_re
                l_ref[rows, im] = acc_im
            for q in range(seqs):
                for j in range(blocks):
                    acc_re = acc_im = None
                    for i in range(j, blocks):
                        y_rows = pl.ds(i * channels + row, 8)
                        g_rows = pl.ds((i - j) * channels + row, 8)
                        yr, yi = q_ref[q, y_rows, re], q_ref[q, y_rows, im]
                        gr, gi = g_ref[g_rows, re], g_ref[g_rows, im]
                        new_re = gr * yr + gi * yi
                        new_im = gr * yi - gi * yr
                        acc_re = new_re if acc_re is None else acc_re + new_re
                        acc_im = new_im if acc_im is None else acc_im + new_im
                    rows = pl.ds(j * channels + row, 8)
                    q_ref[q, rows, re] = acc_re
                    q_ref[q, rows, im] = acc_im
        return carry

    lax.fori_loop(0, channels // 8, tile, 0)
    for q in range(seqs):
        out_ref[:, q * length : (q + 1) * length] = invert(q_ref[q], high, low).astype(BF16)
    sign = (1 - 2 * (lax.broadcasted_iota(jnp.int32, (1, length), 1) % 2)).astype(F32)
    for d in range(blocks):
        rows = slice(d * channels, (d + 1) * channels)
        real, imag = l_ref[rows, :length], l_ref[rows, length:]
        if d + 1 < blocks:
            after = slice((d + 1) * channels, (d + 2) * channels)
            real = real + sign * l_ref[after, length:]
            imag = imag - sign * l_ref[after, :length]
        both = jnp.concatenate([real, imag], axis=1)
        gfilt_ref[:, d * length : (d + 1) * length] = invert(both, high, low)


def conv_forward(x, filt, table, channels, blocks, length, seqs):
    rows = blocks * channels
    kernel = lambda *refs: conv_forward_kernel(channels, blocks, length, seqs, *refs)
    return pl.pallas_call(
        kernel,
        name="conv_forward",
        out_shape=jax.ShapeDtypeStruct((rows, seqs * length), BF16),
        in_specs=[vmem_spec()] * 3,
        out_specs=vmem_spec(),
        scratch_shapes=[
            pltpu.VMEM((seqs, rows, 2 * length), F32),
            pltpu.VMEM((rows, 2 * length), F32),
        ],
        compiler_params=pltpu.CompilerParams(vmem_limit_bytes=18 << 20),
    )(x, filt, table)


def conv_backward(x, y, filt, table, channels, blocks, length, seqs):
    rows = blocks * channels
    kernel = lambda *refs: conv_backward_kernel(channels, blocks, length, seqs, *refs)
    return pl.pallas_call(
        kernel,
        name="conv_backward",
        out_shape=(
            outside((rows, seqs * length), BF16),
            jax.ShapeDtypeStruct((channels, blocks * length), F32),
        ),
        in_specs=[vmem_spec()] * 4,
        out_specs=(vmem_spec(), vmem_spec()),
        scratch_shapes=[
            pltpu.VMEM((seqs, rows, 2 * length), F32),
            pltpu.VMEM((seqs, rows, 2 * length), F32),
            pltpu.VMEM((rows, 2 * length), F32),
            pltpu.VMEM((rows, 2 * length), F32),
        ],
        compiler_params=pltpu.CompilerParams(vmem_limit_bytes=26 << 20),
    )(x, y, filt, table)


def shifted(block, axis, distance):
    count = lax.axis_size(axis)
    route = [(i - distance, i) for i in range(count) if 0 <= i - distance < count]
    return lax.ppermute(block, axis, route)


def axis_bits(axis):
    size, bits, bit = lax.axis_size(axis), [], 1
    while bit < size:
        bits.append((axis, bit))
        bit *= 2
    return bits


def exchange(value, step):
    axis, bit = step
    return lax.ppermute(value, axis, [(i, i ^ bit) for i in range(lax.axis_size(axis))])


def side_of(step):
    axis, bit = step
    return (lax.axis_index(axis) // bit) % 2


class Route(list):
    twin = None
    lanes = 0


def total_of(kept, other):
    return (kept.astype(F32) + other.astype(F32)).astype(BF16)


def fold_kernel(count, ways, merged, _, *refs):
    ins, outs = refs[: 2 * ways * count], refs[2 * ways * count :]
    for i in range(ways * count):
        value = total_of(ins[2 * i][...], ins[2 * i + 1][...])
        if merged and i < ways:
            outs[i][:, : value.shape[1]] = value
        elif merged:
            outs[i - ways][:, outs[i - ways].shape[1] - value.shape[1] :] = value
        else:
            outs[i][...] = value


def fold(pairs, steps, merged=False):
    count = len(pairs)
    ways = 2 if steps else 1
    sizes = [pair[0].shape[0] // ways for pair in pairs]
    if any(size % 16 for size in sizes):
        sums = [total_of(*pair) for pair in pairs]
        if steps is None:
            return sums
        cut = lambda value, place, size: lax.dynamic_slice_in_dim(value, place * size, size, 0)
        pieces = [
            (cut(value, 1 - side_of(step), size), cut(value, side_of(step), size))
            for value, step, size in zip(sums, steps, sizes)
        ]
        if merged:
            return [tuple(jnp.concatenate(parts, axis=1) for parts in zip(*pieces))]
        return pieces
    most = max(sizes)
    grid = most // 64 if most >= 192 and all(size == most for size in sizes) and most % 64 == 0 else 1
    shapes, in_specs, args = [], [], []
    for i, ((kept, other), size) in enumerate(zip(pairs, sizes)):
        lanes = kept.shape[1]
        for way in range(ways):
            if steps:
                place = lambda j, sides_ref, i=i, way=way: (
                    (1 - sides_ref[i] if way == 0 else sides_ref[i]) * grid + j, 0
                )
            else:
                place = lambda j, sides_ref: (j, 0)
            in_specs += [pl.BlockSpec((size // grid, lanes), place)] * 2
            args += [kept, other]
            make = outside if most >= 384 and lanes >= 1536 else jax.ShapeDtypeStruct
            shapes.append(make((size, lanes), BF16))
    if merged:
        lanes = sum(pair[0].shape[1] for pair in pairs)
        shapes = [jax.ShapeDtypeStruct((most, lanes), BF16)] * ways
    out_specs = [
        pl.BlockSpec((shape.shape[0] // grid, shape.shape[1]), lambda j, sides_ref: (j, 0)) for shape in shapes
    ]
    sides = jnp.stack([side_of(step) for step in steps] if steps else [jnp.zeros((), jnp.int32)])
    outs = pl.pallas_call(
        lambda *refs: fold_kernel(count, ways, merged, *refs),
        name="fold",
        out_shape=shapes,
        grid_spec=pltpu.PrefetchScalarGridSpec(
            num_scalar_prefetch=1, grid=(grid,), in_specs=in_specs, out_specs=out_specs
        ),
        compiler_params=pltpu.CompilerParams(vmem_limit_bytes=14 << 20),
    )(sides.astype(jnp.int32), *args)
    return list(zip(outs[::2], outs[1::2])) if steps else list(outs)


def join_kernel(count, lanes, sides_ref, *refs):
    for i in range(count):
        for ref, place in ((refs[2 * i], sides_ref[i]), (refs[2 * i + 1], 1 - sides_ref[i])):
            if lanes:
                refs[2 * count][place] = ref[:, :lanes]
                refs[2 * count + 1][place] = ref[:, lanes:]
            else:
                refs[2 * count + i][place] = ref[...]


def join(pairs, steps, lanes=0):
    count = len(pairs)
    if any(pair[0].shape[0] % 16 for pair in pairs):
        outs = []
        for (own, other), step in zip(pairs, steps):
            first = side_of(step) == 0
            outs.append(jnp.concatenate([jnp.where(first, own, other), jnp.where(first, other, own)]))
        return [outs[0][:, :lanes], outs[0][:, lanes:]] if lanes else outs
    sides = jnp.stack([side_of(step) for step in steps]).astype(jnp.int32)
    in_specs, shapes = [], []
    for own, _ in pairs:
        rows, width = own.shape
        in_specs += [pl.BlockSpec((rows, width), lambda j: (0, 0))] * 2
        for part in (lanes, width - lanes) if lanes else (width,):
            shapes.append(jax.ShapeDtypeStruct((2, rows, part), BF16))
    outs = pl.pallas_call(
        lambda *refs: join_kernel(count, lanes, *refs),
        name="join",
        grid=(1,),
        out_shape=shapes,
        in_specs=[smem_spec()] + in_specs,
        out_specs=[pl.BlockSpec(shape.shape, lambda j: (0, 0, 0)) for shape in shapes],
        compiler_params=pltpu.CompilerParams(vmem_limit_bytes=8 << 20),
    )(sides, *[value for pair in pairs for value in pair])
    return [out.reshape(-1, out.shape[2]) for out in outs]


def quarters_do(row_side, lane_side, refs, put):
    for place, ref in enumerate(refs):
        h = row_side if place % 2 == 0 else 1 - row_side
        for l in range(2):

            @pl.when((lane_side == l) if place < 2 else (lane_side != l))
            def _():
                put(h, l, ref[...].astype(F32))


def widen_kernel(stacked, sides_ref, *refs):
    pieces, out_ref = refs[:4], refs[4]
    lanes = pieces[0].shape[1]

    def put(h, l, value):
        if stacked:
            width = lanes // out_ref.shape[1]
            for k in range(out_ref.shape[1]):
                out_ref[l, k, h] = value[:, k * width : (k + 1) * width]
        else:
            out_ref[h, :, l * lanes : (l + 1) * lanes] = value

    quarters_do(sides_ref[0], sides_ref[1], pieces, put)


def widen(sides, pieces, width, stacked):
    rows, lanes = pieces[0].shape
    tile = 64
    if stacked:
        count = lanes // width
        shape = (2, count, 2, rows, width)
        out = pl.BlockSpec((2, count, 2, tile, width), lambda j: (0, 0, 0, j, 0))
    else:
        shape = (2, rows, 2 * lanes)
        out = pl.BlockSpec((2, tile, 2 * lanes), lambda j: (0, j, 0))
    wide = pl.pallas_call(
        lambda *refs: widen_kernel(stacked, *refs),
        name="widen",
        grid=(rows // tile,),
        out_shape=jax.ShapeDtypeStruct(shape, F32),
        in_specs=[smem_spec()] + [pl.BlockSpec((tile, lanes), lambda j: (j, 0))] * 4,
        out_specs=out,
        compiler_params=pltpu.CompilerParams(vmem_limit_bytes=14 << 20),
    )(sides, *pieces)
    return wide.reshape(-1, shape[-1])


def widen_late_kernel(sides_ref, *refs):
    s_pieces, t_pieces, (in_ref, out_ref, last_ref) = refs[:4], refs[4:8], refs[8:]
    width = out_ref.shape[2]

    def put_s(h, l, value):
        in_ref[h, :, (l + 1) * width : (l + 2) * width] = value

    def put_t(h, l, value):
        if l == 0:
            in_ref[h, :, :width] = value[:, :width]
        else:
            out_ref[h] = value[:, :width]
        last_ref[l, h] = value[:, width:]

    quarters_do(sides_ref[0], sides_ref[1], s_pieces, put_s)
    quarters_do(sides_ref[2], sides_ref[1], t_pieces, put_t)


def widen_late(sides, s_pieces, t_pieces):
    rows, width = s_pieces[0].shape
    more = t_pieces[0].shape[1] - width
    tile = 64
    part = lambda lanes: pl.BlockSpec((tile, lanes), lambda j: (j, 0))
    both = lambda lanes: pl.BlockSpec((2, tile, lanes), lambda j: (0, j, 0))
    grad_in, grad_out, last = pl.pallas_call(
        widen_late_kernel,
        name="widen_late",
        grid=(rows // tile,),
        out_shape=(
            jax.ShapeDtypeStruct((2, rows, 3 * width), F32), jax.ShapeDtypeStruct((2, rows, width), F32),
            jax.ShapeDtypeStruct((2, 2, rows, more), F32),
        ),
        in_specs=[smem_spec()] + [part(width)] * 4 + [part(width + more)] * 4,
        out_specs=(
            both(3 * width), both(width), pl.BlockSpec((2, 2, tile, more), lambda j: (0, 0, j, 0)),
        ),
        compiler_params=pltpu.CompilerParams(vmem_limit_bytes=14 << 20),
    )(sides, *s_pieces, *t_pieces)
    return grad_in.reshape(-1, 3 * width), grad_out.reshape(-1, width), last.reshape(2, -1, more)


def unpack_kernel(features, hidden, wide, last_ref, net_ref, *refs):
    (g1, b1, b_in, sw, sb, fw1, fb1, fw2, fb2, fw3, skip, b_out, g2, b2, mb1, mb2) = refs
    width = g1.shape[0]
    fw3[...] = last_ref[0].T[:hidden]
    fw1[...] = net_ref[0, :features, :hidden]
    fb1[...] = net_ref[0, features : features + 1, :hidden].reshape(hidden)
    fw2[...] = net_ref[0, features + 1 : features + 1 + hidden, :hidden]
    fb2[...] = net_ref[0, features + 1 + hidden : features + 2 + hidden, :hidden].reshape(hidden)
    pieces = width // 128

    def put(ref, place, lane, row=None):
        for k in range(pieces):
            at = 128 + place * pieces + k
            value = net_ref[0, at : at + 1, :]
            lanes = slice(lane + k * 128, lane + (k + 1) * 128)
            if row is None:
                ref[lanes] = value.reshape(128)
            else:
                ref[row : row + 1, lanes] = value

    for place, ref in enumerate((skip, b_out, g2, b2, mb2)):
        put(ref, place, 0)
    for k in range(wide):
        put(mb1, 5 + k, k * width)
    put(g1, 5 + wide, 0)
    put(b1, 6 + wide, 0)
    for group in range(3):
        first = 7 + wide + 5 * group
        put(b_in, first, group * width)
        put(sb, first + 1, group * width)
        for tap in range(3):
            put(sw, first + 2 + tap, group * width, tap)


def unpack(last, features, hidden, wide, width):
    flat = lambda size: jax.ShapeDtypeStruct((size,), F32)
    grid = lambda *shape: jax.ShapeDtypeStruct(shape, F32)
    part = lambda h: pl.BlockSpec((1, width, 128), lambda i: (h, 0, 0))
    shapes = (
        flat(width), flat(width), flat(3 * width), grid(3, 3 * width), flat(3 * width),
        grid(features, hidden), flat(hidden), grid(hidden, hidden), flat(hidden), grid(hidden, width),
        flat(width), flat(width), flat(width), flat(width), flat(wide * width), flat(width),
    )
    whole = lambda shape: pl.BlockSpec(shape, lambda i: (0,) * len(shape))
    return pl.pallas_call(
        lambda *refs: unpack_kernel(features, hidden, wide, *refs),
        name="unpack",
        grid=(1,),
        out_shape=shapes,
        in_specs=[part(0), part(1)],
        out_specs=[whole(shape.shape) for shape in shapes],
        compiler_params=pltpu.CompilerParams(vmem_limit_bytes=14 << 20),
    )(last, last)


def orders():
    bits = axis_bits("bucket") + axis_bits("seq")
    first, rest = bits[0], bits[1:]
    if len(rest) == 4:
        y, x, near, far = rest
        turns = ([y, x, near, far], [x, y, near, far])
    else:
        turns = (rest, rest[1:] + rest[:1])
    return [Route([first] + turn) for turn in turns]


def work_order(last):
    if last == 4:
        return [
            ("s", 3), ("p", -3), ("s", 4), ("s", 5), ("p", -2), ("s", -4), ("s", -3), ("s", -2),
            ("last", 0), ("wide", 0),
        ]
    order = [("p", index) for index in range(5, last + 2)]
    order += [("s", index) for index in range(2, last + 2)]
    order += [("p", -index) for index in range(last, 1, -1)]
    order += [("s", -index) for index in range(last, 1, -1)]
    return order + [("last", 0), ("wide", 0)]


def held(value, *awaited):
    return lax.optimization_barrier((value,) + awaited)[0]


def local(
    tokens, cotangent, lengths, decay_rate, norm1_gain, norm1_bias, w_in, b_in,
    short_weight, short_bias, filter_w1, filter_b1, filter_w2, filter_b2, filter_w3,
    skip_gain, w_out, b_out, norm2_gain, norm2_bias, mlp_w1, mlp_b1, mlp_w2, mlp_b2,
):
    seqs, block, width = tokens.shape[1:]
    rows = seqs * block
    blocks = lax.axis_size("seq")
    full = blocks * block
    channels = width // blocks
    position = lax.axis_index("seq")
    place = position.reshape(1).astype(jnp.int32)
    table = jnp.asarray(transform_tables(block))
    flat_tokens = tokens.reshape(rows, width)

    edge_tokens = shifted(tokens[0, :, block - 2 :, :], "seq", 1).reshape(2 * seqs, width)
    normed, edge_normed, mixed_late, factors, signal = front(
        place, flat_tokens, edge_tokens, norm1_gain, norm1_bias, b_in, short_bias, short_weight, w_in,
        seqs, block,
    )
    signal_all = lax.all_to_all(signal, "seq", 0, 0, tiled=True)
    turned, mixed_early, gate_out = gate_part(
        place, normed, edge_normed, b_in, short_bias, short_weight, w_in, seqs, block
    )

    own = position * channels
    rates = lax.dynamic_slice_in_dim(decay_rate, own, channels)
    weight_three = lax.dynamic_slice_in_dim(filter_w3.astype(F32), own, channels, axis=1)

    second_weight = filter_w2.astype(F32)
    feats, hidden_one, slope_one, hidden_two, slope_two = filter_layers(
        filter_w1.astype(F32), filter_b1.astype(F32), second_weight, filter_b2.astype(F32), full
    )
    times = lax.broadcasted_iota(jnp.int32, (1, full), 1).astype(F32) / full
    window = jnp.exp(-times * rates[:, None]) + 0.05
    filt = (precise("hd,hp->dp", weight_three, hidden_two) * window).astype(BF16)
    long_all = conv_forward(signal_all, filt, table, channels, blocks, block, seqs)
    conv_long = lax.all_to_all(long_all, "seq", 0, 0, tiled=True)

    order_p, order_q = orders()
    core = order_p[0]
    side = side_of(core).reshape(1).astype(jnp.int32)
    (
        output, grad_resid, grad_long, grad_gate, given_p, kept_p, given_q, kept_q, grad_w_out, sums,
        grad_b1,
    ) = middle(
        side, place, lengths.reshape(seqs), conv_long, signal, gate_out, skip_gain, flat_tokens,
        cotangent.reshape(rows, width), w_out, b_out, norm2_gain, norm2_bias, mlp_b2, mlp_b1[None], mlp_w1,
        mlp_w2, seqs, block,
    )
    grad_long_all = lax.all_to_all(grad_long, "seq", 0, 0, tiled=True)

    def turn(streams, index, *awaited):
        pairs, after = [], []
        for (given, kept), order in streams:
            other = exchange(given, order[index])
            if awaited:
                kept, awaited = held(kept, *awaited), ()
            pairs.append((kept, other))
            after.append(order[index + 1] if index + 1 < len(order) else None)
        routes = [order for _, order in streams]
        merged = len(streams) == 2 and after[0] is not None and after[0] == after[1]
        parts = fold(pairs, after if after[0] else None, merged)
        if merged:
            route = Route(routes[0])
            route.twin, route.lanes = routes[1], pairs[0][0].shape[1]
            routes = [route]
        return list(zip(parts, routes))

    def turn_back(streams, index, *awaited):
        pairs = []
        for part, order in streams:
            other = exchange(part, order[index])
            if awaited:
                part, awaited = held(part, *awaited), ()
            pairs.append((part, other))
        routes = [order for _, order in streams]
        route = routes[0]
        lanes = route.lanes if route.twin and route[index - 1] != route.twin[index - 1] else 0
        parts = join(pairs, [order[index] for order in routes], lanes)
        return list(zip(parts, [Route(route), route.twin] if lanes else routes))

    def quarters(streams, *awaited):
        others = [exchange(part, order[1]) for part, order in streams]
        if awaited:
            others = lax.optimization_barrier(tuple(others) + awaited)[: len(others)]
        return [
            [part, other, exchange(part, core), exchange(other, core)]
            for (part, _), other in zip(streams, others)
        ]

    def first_of(streams):
        value = streams[0][0]
        return value[0] if isinstance(value, tuple) else value

    last = len(order_p) - 1
    parts = turn([((given_p, kept_p), order_p), ((given_q, kept_q), order_q)], 0)
    grad_long_all = held(grad_long_all, first_of(parts))
    back_all, grad_filter = conv_backward(
        signal_all, grad_long_all, filt, table, channels, blocks, block, seqs
    )
    back_conv = lax.all_to_all(back_all, "seq", 0, 0, tiled=True)
    last_w3, net = filter_back(
        own.reshape(1).astype(jnp.int32), grad_filter, window, feats, hidden_one, slope_one, hidden_two,
        slope_two, second_weight, weight_three, width,
    )
    features, hidden = filter_w1.shape
    heads = features + hidden + 2
    parts = turn(parts, 1, last_w3)
    back_conv = held(back_conv, first_of(parts))
    edges = all_edges(back_conv, grad_long, skip_gain, factors, grad_gate, seqs, block)
    edges = shifted(edges, "seq", -1)
    late_grads, given_s, kept_s, sums_late = late_back(
        side, back_conv, grad_long, skip_gain, factors, edges, mixed_late, short_weight, turned, seqs,
        block,
    )
    parts = turn(parts, 2, late_grads)
    stream_s = turn([((held(given_s, first_of(parts)), kept_s), order_p)], 0)
    gate_grads, w_in_early, sums_early = early_back(
        held(grad_gate, first_of(stream_s)), edges, mixed_early, short_weight, turned, seqs, block
    )
    parts = turn(parts, 3, gate_grads)
    tokens_grad, sums_norm = back(
        gate_grads, held(late_grads, first_of(parts)), w_in, flat_tokens, grad_resid, norm1_gain,
        norm1_bias,
    )
    if last == 4:
        stream_s = turn(stream_s, 1, tokens_grad)
        parts = turn(parts, 4, first_of(stream_s))
    wide = grad_b1.shape[1] // width
    shorts = jnp.concatenate([sums_early, sums_late], axis=0)
    small = jnp.concatenate(
        [sums[:5], grad_b1.reshape(-1, width), sums_norm[:2], shorts[:, :5].reshape(-1, width)], axis=0
    )
    more = small.size // 128
    net = jnp.concatenate(
        [net, small.reshape(more, 128), jnp.zeros((width - 128 - more, 128), F32)], axis=0
    )
    part_t = choose(side, held(w_in_early, first_of(parts)), last_w3, grad_w_out, net)
    stream_t = turn([(part_t, order_q)], 0)
    token = first_of(stream_t)
    if last == 4:
        parts = turn_back(parts, 4, token)
        stream_t = turn(stream_t, 1, first_of(parts))
        token = first_of(stream_t)
    state = {"p": parts, "s": stream_s + stream_t}
    for piece, index in work_order(last):
        if piece == "last":
            last_p, last_q = quarters(state["p"], token)
            token = last_q[1]
        elif piece == "wide":
            sides_of = lambda order: jnp.stack([side_of(order[1]), side_of(core)]).astype(jnp.int32)
            last_p[0] = held(last_p[0], token)
            sum_w1 = widen(sides_of(order_p), last_p, width, False)
            last_q[0] = held(last_q[0], sum_w1)
            sum_w2 = widen(sides_of(order_q), last_q, width, True)
            token = sum_w2
        elif index > 0:
            state[piece] = turn(state[piece], index - 1, token)
            token = first_of(state[piece])
        else:
            state[piece] = turn_back(state[piece], -index, token)
            token = first_of(state[piece])
    last_s, last_t = quarters(state["s"], token)
    sides = jnp.stack([side_of(order_p[1]), side_of(core), side_of(order_q[1])]).astype(jnp.int32)
    sum_w_in, sum_w_out, sum_last = widen_late(sides, last_s, last_t)
    small = unpack(sum_last, features, hidden, wide, width)
    return (
        output.reshape(tokens.shape), tokens_grad.reshape(tokens.shape), *small[:2], sum_w_in, *small[2:11],
        sum_w_out, *small[11:14], sum_w1, small[14], sum_w2, small[15],
    )


def solution(mesh):
    split = P("bucket", None, "seq", None)
    in_specs = (split, split, P("bucket", None)) + (P(),) * 21
    out_specs = (split, split) + (P(),) * 20
    return jax.shard_map(local, mesh=mesh, in_specs=in_specs, out_specs=out_specs, check_vma=False)
```

```python
import math

import jax
import jax.numpy as jnp
import numpy as np
from jax import lax
from jax.experimental import pallas as pl
from jax.experimental.pallas import tpu as pltpu
from jax.sharding import PartitionSpec as P

HIGH = lax.Precision.HIGHEST
EPSILON = 1e-05
F32 = jnp.float32
BF16 = jnp.bfloat16


def norm_forward(values, gain, bias):
    center = values - jnp.mean(values, axis=-1, keepdims=True)
    inverse = lax.rsqrt(jnp.mean(center * center, axis=-1, keepdims=True) + EPSILON)
    unit = center * inverse
    return (unit * gain + bias, unit, inverse)


def precise(formula, left, right):
    return jnp.einsum(formula, left, right, precision=HIGH, preferred_element_type=F32)


def position_features(length):
    steps = lax.broadcasted_iota(jnp.int32, (1, length), 1).astype(F32)
    bands = 0.0001 + lax.broadcasted_iota(jnp.int32, (16, 1), 0).astype(F32) * (
        (15.0 - 0.0001) / 15.0
    )
    phase = 2.0 * math.pi / length * steps * bands
    return jnp.concatenate([steps / length, jnp.cos(phase), -jnp.sin(phase)], axis=0)


def filter_layers(weight_one, bias_one, weight_two, bias_two, length):
    feats = position_features(length)
    first = precise("eh,ep->hp", weight_one, feats) + bias_one[:, None]
    hidden = jnp.sin(first)
    second = precise("hk,hp->kp", weight_two, hidden) + bias_two[:, None]
    return feats, hidden, jnp.cos(first), jnp.sin(second), jnp.cos(second)


def exact(left, right, dims):
    return lax.dot_general(
        left, right, (dims, ((), ())), precision=HIGH, preferred_element_type=F32
    )


def filter_back_kernel(
    channels, own_ref, grad_ref, window_ref, feats_ref, h1_ref, c1_ref, h2_ref, c2_ref, w2_ref, w3_ref,
    last_ref, net_ref,
):
    hidden = h1_ref.shape[0]
    features = feats_ref.shape[0]
    shaped = grad_ref[...] * window_ref[...]
    ones = jnp.ones((8, shaped.shape[1]), F32)
    last_ref[...] = jnp.zeros_like(last_ref)
    net_ref[...] = jnp.zeros_like(net_ref)
    rows = pl.ds(pl.multiple_of(own_ref[0], 16), channels)
    grad_w3 = exact(shaped, h2_ref[...], ((1,), (1,)))
    last_ref[rows, :] = jnp.concatenate([grad_w3, jnp.zeros_like(grad_w3)], axis=1).astype(BF16)
    second = exact(w3_ref[...], shaped, ((1,), (0,))) * c2_ref[...]
    first = exact(w2_ref[...], second, ((1,), (0,))) * c1_ref[...]
    place = 0
    for value in (
        exact(feats_ref[...], first, ((1,), (1,))), exact(ones, first, ((1,), (1,)))[:1],
        exact(h1_ref[...], second, ((1,), (1,))), exact(ones, second, ((1,), (1,)))[:1],
    ):
        net_ref[place : place + value.shape[0], :hidden] = value
        place += value.shape[0]


def filter_back(own, grad, window, feats, h1, c1, h2, c2, w2, w3, width):
    channels = grad.shape[0]
    return pl.pallas_call(
        lambda *refs: filter_back_kernel(channels, *refs),
        name="filter_back",
        out_shape=(
            jax.ShapeDtypeStruct((width, 128), BF16), jax.ShapeDtypeStruct((128, 128), F32),
        ),
        in_specs=[smem_spec()] + [vmem_spec()] * 9,
        out_specs=(vmem_spec(), vmem_spec()),
        compiler_params=pltpu.CompilerParams(vmem_limit_bytes=14 << 20),
    )(own, grad, window, feats, h1, c1, h2, c2, w2, w3)


def choose_kernel(side_ref, early_ref, last_ref, out_ref, net_ref, given_ref, kept_ref):
    low_side = side_ref[0] == 0
    width = early_ref.shape[1]
    parts = (
        (early_ref[...], out_ref[...], slice(0, width)),
        (last_ref[...], net_ref[...].astype(BF16), slice(width, width + 128)),
    )
    for low_half, high_half, lanes in parts:
        given_ref[:, lanes] = jnp.where(low_side, high_half, low_half)
        kept_ref[:, lanes] = jnp.where(low_side, low_half, high_half)


def choose(side, early, last, grad_out, net):
    width = early.shape[0]
    tile = 128
    part = lambda lanes: pl.BlockSpec((tile, lanes), lambda j: (j, 0))
    shape = jax.ShapeDtypeStruct((width, width + 128), BF16)
    return tuple(
        pl.pallas_call(
            choose_kernel,
            name="choose",
            grid=(width // tile,),
            out_shape=(shape, shape),
            in_specs=[smem_spec(), part(width), part(128), part(width), part(128)],
            out_specs=(part(width + 128), part(width + 128)),
            compiler_params=pltpu.CompilerParams(vmem_limit_bytes=8 << 20),
        )(side, early, last, grad_out, net)
    )


def outside(shape, dtype):
    return pltpu.HBM(shape, dtype)


def vmem_spec():
    return pl.BlockSpec(memory_space=pltpu.VMEM)


def smem_spec():
    return pl.BlockSpec(memory_space=pltpu.SMEM)


def contract(left, right, dims):
    return lax.dot_general(left, right, (dims, ((), ())), preferred_element_type=F32)


def lane_sums(parts):
    ones = jnp.ones((8, 128), BF16)
    heads, tails = [], []
    for part in parts:
        folded = part[:, :128]
        for lane in range(128, part.shape[1], 128):
            folded = folded + part[:, lane : lane + 128]
        head = folded.astype(BF16)
        heads.append(head)
        tails.append((folded - head.astype(F32)).astype(BF16))
    both = contract(ones, jnp.concatenate(heads + tails, axis=0), ((1,), (1,)))
    count = parts[0].shape[0]
    half = count * len(parts)
    return [
        both[:1, k * count : (k + 1) * count] + both[:1, half + k * count : half + (k + 1) * count]
        for k in range(len(parts))
    ]


def columns(*rows):
    parts = [row[...].astype(F32).reshape(-1, row.shape[-1]) for row in rows]
    count = sum(part.shape[0] for part in parts)
    parts.append(jnp.zeros((8 - count, parts[0].shape[1]), F32))
    return jnp.concatenate(parts, axis=0).T


def row(ref):
    return ref[...].astype(F32).reshape(1, ref.shape[0])


def short_filter(mixed, edge, cols, seqs, block):
    spots = lax.broadcasted_iota(jnp.int32, (1, block), 1)
    pieces = []
    for q in range(seqs):
        now = mixed[:, q * block : (q + 1) * block]
        near, far = edge[:, 2 * q + 1 : 2 * q + 2], edge[:, 2 * q : 2 * q + 1]
        once = jnp.where(spots == 0, near, pltpu.roll(now, 1, 1))
        twice = jnp.where(spots == 0, far, jnp.where(spots == 1, near, pltpu.roll(now, 2, 1)))
        pieces.append(
            cols[:, 2:3] * now + cols[:, 3:4] * once + cols[:, 4:5] * twice + cols[:, 1:2]
        )
    return jnp.concatenate(pieces, axis=1)


def project(weight, normed, edge_normed, cols, inside, seqs, block):
    mixed = (contract(weight, normed, ((0,), (1,))) + cols[:, 0:1]).astype(BF16)
    edge = (contract(weight, edge_normed, ((0,), (1,))) + cols[:, 0:1]).astype(BF16)
    edge = edge.astype(F32) * inside
    return mixed, short_filter(mixed.astype(F32), edge, cols, seqs, block)


def front_kernel(
    seqs, block, first_ref, tok_ref, edge_ref, gain_ref, bias_ref, bb_ref, bc_ref, sbb_ref, sbc_ref, swb_ref,
    swc_ref, wb_ref, wc_ref, normed_ref, edge_normed_ref, mixed_ref, factor_ref, signal_ref,
):
    @pl.when(pl.program_id(0) == 0)
    def _():
        gain, bias = row(gain_ref), row(bias_ref)
        normed_ref[...] = norm_forward(tok_ref[...].astype(F32), gain, bias)[0].astype(BF16)
        edge_normed_ref[...] = norm_forward(edge_ref[...].astype(F32), gain, bias)[0].astype(BF16)

    normed, edge_normed = normed_ref[...], edge_normed_ref[...]
    inside = (first_ref[0] > 0).astype(F32)
    mixed_ref[0], gate_in = project(
        wb_ref[...], normed, edge_normed, columns(bb_ref, sbb_ref, swb_ref), inside, seqs, block
    )
    mixed_ref[1], values = project(
        wc_ref[...], normed, edge_normed, columns(bc_ref, sbc_ref, swc_ref), inside, seqs, block
    )
    factor_ref[0] = values
    factor_ref[1] = gate_in
    signal_ref[...] = (gate_in * values).astype(BF16)


def front(position, tokens, edge, gain, bias, b_in, short_bias, short_weight, w_in, seqs, block):
    rows, width = tokens.shape
    tile = 256
    steps = width // tile
    fixed = lambda shape: pl.BlockSpec(shape, lambda j: (0,) * len(shape))
    weight = lambda part: pl.BlockSpec((width, tile), lambda j: (0, part * steps + j))
    flat = lambda part: pl.BlockSpec((tile,), lambda j: (part * steps + j,))
    taps = lambda part: pl.BlockSpec((3, tile), lambda j: (0, part * steps + j))
    both = pl.BlockSpec((2, tile, rows), lambda j: (0, j, 0))
    return pl.pallas_call(
        lambda *refs: front_kernel(seqs, block, *refs),
        name="front",
        grid=(steps,),
        out_shape=(
            jax.ShapeDtypeStruct((rows, width), BF16), jax.ShapeDtypeStruct(edge.shape, BF16),
            jax.ShapeDtypeStruct((2, width, rows), BF16), jax.ShapeDtypeStruct((2, width, rows), F32),
            jax.ShapeDtypeStruct((width, rows), BF16),
        ),
        in_specs=[
            smem_spec(), fixed((rows, width)), fixed(edge.shape), fixed(gain.shape), fixed(bias.shape),
            flat(1), flat(2), flat(1), flat(2), taps(1), taps(2), weight(1), weight(2),
        ],
        out_specs=(
            fixed((rows, width)), fixed(edge.shape), both, both,
            pl.BlockSpec((tile, rows), lambda j: (j, 0)),
        ),
        compiler_params=pltpu.CompilerParams(vmem_limit_bytes=58 << 20),
    )(
        position, tokens, edge, gain, bias, b_in, b_in, short_bias, short_bias, short_weight,
        short_weight, w_in, w_in,
    )


def gate_kernel(
    seqs, block, first_ref, normed_ref, edge_normed_ref, b_ref, sb_ref, sw_ref, w_ref, turned_ref,
    mixed_ref, gate_ref,
):
    normed = normed_ref[...]

    @pl.when(pl.program_id(0) == 0)
    def _():
        turned_ref[...] = normed.T

    inside = (first_ref[0] > 0).astype(F32)
    mixed_ref[...], gate_ref[...] = project(
        w_ref[...], normed, edge_normed_ref[...], columns(b_ref, sb_ref, sw_ref), inside, seqs, block
    )


def gate_part(position, normed, edge_normed, b_in, short_bias, short_weight, w_in, seqs, block):
    rows, width = normed.shape
    tile = 256
    fixed = lambda shape: pl.BlockSpec(shape, lambda j: (0,) * len(shape))
    flat = pl.BlockSpec((tile,), lambda j: (j,))
    out = pl.BlockSpec((tile, rows), lambda j: (j, 0))
    return pl.pallas_call(
        lambda *refs: gate_kernel(seqs, block, *refs),
        name="gate_part",
        grid=(width // tile,),
        out_shape=(
            jax.ShapeDtypeStruct((width, rows), BF16), jax.ShapeDtypeStruct((width, rows), BF16),
            jax.ShapeDtypeStruct((width, rows), F32),
        ),
        in_specs=[
            smem_spec(), fixed((rows, width)), fixed(edge_normed.shape), flat, flat,
            pl.BlockSpec((3, tile), lambda j: (0, j)), pl.BlockSpec((width, tile), lambda j: (0, j)),
        ],
        out_specs=(fixed((width, rows)), out, out),
        compiler_params=pltpu.CompilerParams(vmem_limit_bytes=58 << 20),
    )(position, normed, edge_normed, b_in, short_bias, short_weight, w_in)


def row_mask(position, lengths_ref, seqs, block):
    spots = position * block + lax.broadcasted_iota(jnp.int32, (block, 1), 0)
    return jnp.concatenate([(spots < lengths_ref[q]).astype(F32) for q in range(seqs)], axis=0)


def middle_kernel(
    seqs, block, side_ref, position_ref, lengths_ref, conv_ref, signal_ref, gate_ref, skip_ref, tok_ref,
    cot_ref, w_out_ref, b_out_ref, gain_ref, bias_ref, b2_ref, b1_ref, w1_ref, w2_ref,
    out_ref, resid_grad_ref, long_ref, gate_grad_ref, given1_ref, kept1_ref, given2_ref, kept2_ref,
    gwo_ref, sums_ref,
    gated_ref, n2_ref, n2t_ref, unit_ref, inv_ref, final_ref, gf_ref, q_ref, lout_ref,
):
    step = pl.program_id(0)
    last = pl.num_programs(0) - 1
    b_out, gain, bias, b2 = row(b_out_ref), row(gain_ref), row(bias_ref), row(b2_ref)

    @pl.when(step == 0)
    def _():
        skip = columns(skip_ref)[:, 0:1]
        long_out = conv_ref[...].astype(F32) + signal_ref[...].astype(F32) * skip
        lout_ref[...] = long_out
        gated = (long_out * gate_ref[...]).astype(BF16)
        gated_ref[...] = gated
        branch = contract(gated, w_out_ref[...], ((0,), (0,))) + b_out
        resid = tok_ref[...].astype(F32) + branch
        normed, unit, inverse = norm_forward(resid, gain, bias)
        n2_ref[...] = normed.astype(BF16)
        n2t_ref[...] = normed.astype(BF16).T
        unit_ref[...] = unit
        inv_ref[...] = jnp.broadcast_to(inverse, inv_ref.shape)
        final_ref[...] = resid + b2
        valid = row_mask(position_ref[0], lengths_ref, seqs, block)
        gf_ref[...] = (cot_ref[...].astype(F32) * valid).astype(BF16)
        q_ref[...] = jnp.zeros_like(q_ref)

    w1, w2, gf = w1_ref[...], w2_ref[...], gf_ref[...]
    pre = contract(n2_ref[...], w1, ((1,), (0,))) + b1_ref[...].astype(F32)
    grad_active = contract(gf, w2, ((1,), (1,)))
    cumulative, slope = normal_terms(pre)
    active = (pre * cumulative).astype(BF16)
    grad_pre = grad_active * slope
    grad_low = grad_pre.astype(BF16)
    final_ref[...] += contract(active, w2, ((1,), (0,)))
    q_ref[...] += contract(grad_low, w1, ((1,), (1,)))
    grad_two = contract(active, gf, ((0,), (0,))).astype(BF16)
    grad_one = contract(n2t_ref[...], grad_low, ((1,), (0,))).astype(BF16)

    @pl.when(step <= last // 2)
    def _():
        given1_ref[...] = grad_one
        given2_ref[...] = grad_two

    @pl.when(step > last // 2)
    def _():
        kept1_ref[...] = grad_one
        kept2_ref[...] = grad_two

    half = pl.num_programs(0) // 2
    chunk = jnp.where(step < half, half * (1 - side_ref[0]) + step, half * side_ref[0] + step - half)
    sums_ref[pl.ds(8 + chunk, 1)] = jnp.sum(grad_low.astype(F32), axis=0, keepdims=True)

    @pl.when(step == last)
    def _():
        valid = row_mask(position_ref[0], lengths_ref, seqs, block)
        out_ref[...] = (final_ref[...] * valid).astype(BF16)
        grad_final = gf_ref[...].astype(F32)
        q, unit = q_ref[...], unit_ref[...]
        scaled = q * gain
        grad_resid = grad_final + inv_ref[:, 0:1] * (
            scaled
            - jnp.mean(scaled, axis=-1, keepdims=True)
            - unit * jnp.mean(scaled * unit, axis=-1, keepdims=True)
        )
        resid_grad_ref[...] = grad_resid
        grad_branch = grad_resid.astype(BF16)
        grad_gated = contract(w_out_ref[...], grad_branch, ((1,), (1,)))
        grad_long = (grad_gated * gate_ref[...]).astype(BF16)
        long_ref[...] = grad_long
        gate_grad_ref[...] = grad_gated * lout_ref[...]
        gwo_ref[...] = contract(gated_ref[...], grad_branch, ((1,), (0,))).astype(BF16)
        skip_sum = lane_sums([grad_long.astype(F32) * signal_ref[...].astype(F32)])[0]
        total = lambda part: jnp.sum(part, axis=0, keepdims=True)
        sums_ref[0:1] = skip_sum
        sums_ref[1:2] = total(grad_branch.astype(F32))
        sums_ref[2:3] = total(q * unit)
        sums_ref[3:4] = total(q)
        sums_ref[4:5] = total(grad_final)
        sums_ref[5:8] = jnp.zeros((3, sums_ref.shape[1]), F32)


def normal_terms(pre):
    cumulative = 0.5 * (1.0 + lax.erf(pre * (1.0 / math.sqrt(2.0))))
    density = jnp.exp(-0.5 * pre * pre) * (1.0 / math.sqrt(2.0 * math.pi))
    return cumulative, cumulative + pre * density


def middle(
    side, position, lengths, conv, signal, gate, skip, tokens, cotangent, w_out, b_out, gain, bias, b2, b1, w1,
    w2, seqs, block,
):
    count, width = tokens.shape
    hidden = w1.shape[1]
    chunk = width
    steps = hidden // chunk
    half = steps // 2
    once = lambda shape: pl.BlockSpec(
        shape, lambda j, side_ref: (0,) * len(shape), pipeline_mode=pl.Buffered(1)
    )

    def which(j, side_ref):
        side = side_ref[0]
        return jnp.where(j < half, half * (1 - side) + j, half * side + j - half)

    across = lambda height: pl.BlockSpec((height, chunk), lambda j, side_ref: (0, which(j, side_ref)))
    given = pl.BlockSpec((width, chunk), lambda j, side_ref: (0, jnp.minimum(j, half - 1)))
    kept = pl.BlockSpec((width, chunk), lambda j, side_ref: (0, jnp.maximum(j - half, 0)))
    wide, tall = (count, width), (width, count)
    shape = jax.ShapeDtypeStruct
    scratch = pltpu.VMEM
    part = shape((width, half * chunk), BF16)
    return pl.pallas_call(
        lambda *refs: middle_kernel(seqs, block, *refs),
        name="middle",
        out_shape=(
            shape(wide, BF16), shape(wide, F32), shape(tall, BF16), shape(tall, F32),
            part, part, part, part, shape((width, width), BF16),
            shape((8 + steps, width), F32),
        ),
        grid_spec=pltpu.PrefetchScalarGridSpec(
            num_scalar_prefetch=1,
            grid=(steps,),
            in_specs=[
                smem_spec(), smem_spec(), once(tall), once(tall), once(tall), once(skip.shape),
                once(wide), once(wide), once((width, width)), once(b_out.shape), once(gain.shape),
                once(bias.shape), once(b2.shape),
                across(1), across(width),
                pl.BlockSpec((chunk, width), lambda j, side_ref: (which(j, side_ref), 0)),
            ],
            out_specs=(
                once(wide), once(wide), once(tall), once(tall), given, kept, given, kept,
                once((width, width)), once((8 + steps, width)),
            ),
            scratch_shapes=[
                scratch(tall, BF16), scratch(wide, BF16), scratch(tall, BF16), scratch(wide, F32),
                scratch((count, 128), F32), scratch(wide, F32), scratch(wide, BF16), scratch(wide, F32),
                scratch(tall, F32),
            ],
        ),
        compiler_params=pltpu.CompilerParams(vmem_limit_bytes=58 << 20),
    )(
        side, position, lengths, conv, signal, gate, skip, tokens, cotangent, w_out, b_out, gain, bias, b2, b1,
        w1, w2,
    )


def first_spots(heads):
    lanes = lax.broadcasted_iota(jnp.int32, (1, 128), 1)
    edge = jnp.zeros(heads[0].shape, F32)
    for q, head in enumerate(heads):
        head = pltpu.roll(head, 2 * q, 1) if q else head
        edge = jnp.where((lanes >= 2 * q) & (lanes < 2 * q + 2), head, edge)
    return edge.T[:8]


def edges_kernel(seqs, skip_ref, *refs):
    skip = columns(skip_ref)[:, 0:1]
    out_ref = refs[-1]
    signals = [
        refs[4 * q][...].astype(F32) + refs[4 * q + 1][...].astype(F32) * skip for q in range(seqs)
    ]
    for part in range(2):
        out_ref[part] = first_spots([signals[q] * refs[4 * q + 2][part] for q in range(seqs)])
    out_ref[2] = first_spots([refs[4 * q + 3][...] for q in range(seqs)])


def all_edges(conv, grad_long, skip, factors, gate, seqs, block):
    width = conv.shape[0]
    specs, args = [], []
    for q in range(seqs):
        place = q * block // 128
        flat = pl.BlockSpec((width, 128), lambda i, place=place: (0, place))
        specs += [flat, flat, pl.BlockSpec((2, width, 128), lambda i, place=place: (0, 0, place)), flat]
        args += [conv, grad_long, factors, gate]
    return pl.pallas_call(
        lambda *refs: edges_kernel(seqs, *refs),
        name="all_edges",
        grid=(1,),
        out_shape=jax.ShapeDtypeStruct((3, 8, width), F32),
        in_specs=[pl.BlockSpec(skip.shape, lambda i: (0,))] + specs,
        out_specs=pl.BlockSpec((3, 8, width), lambda i: (0, 0, 0)),
        compiler_params=pltpu.CompilerParams(vmem_limit_bytes=14 << 20),
    )(skip, *args)


def short_back_body(grad, edge_ref, mixed_ref, sw_ref, turned_ref, out_ref, sums_ref, seqs, block):
    taps = columns(sw_ref)
    edge = edge_ref[0].T
    spots = lax.broadcasted_iota(jnp.int32, (1, block), 1)
    mixed = mixed_ref[0].astype(F32)
    once, twice = [], []
    for q in range(seqs):
        now = grad[:, q * block : (q + 1) * block]
        near, far = edge[:, 2 * q : 2 * q + 1], edge[:, 2 * q + 1 : 2 * q + 2]
        end = block - 1
        once.append(jnp.where(spots == end, near, pltpu.roll(now, block - 1, 1)))
        twice.append(
            jnp.where(
                spots == end, far, jnp.where(spots == end - 1, near, pltpu.roll(now, block - 2, 1))
            )
        )
    once, twice = jnp.concatenate(once, axis=1), jnp.concatenate(twice, axis=1)
    low = (taps[:, 0:1] * grad + taps[:, 1:2] * once + taps[:, 2:3] * twice).astype(BF16)
    out_ref[0] = low
    sums_ref[0, 0:1] = contract(jnp.ones((8, low.shape[1]), BF16), low, ((1,), (1,)))[:1]
    for place, total in enumerate(lane_sums([grad, mixed * grad, mixed * once, mixed * twice])):
        sums_ref[0, place + 1 : place + 2] = total
    sums_ref[0, 5:8] = jnp.zeros((3, sums_ref.shape[2]), F32)
    return contract(turned_ref[...], low, ((1,), (1,))).astype(BF16)


def early_back_kernel(
    seqs, block, grad_ref, edge_ref, mixed_ref, sw_ref, turned_ref, out_ref, gw_ref, sums_ref
):
    gw_ref[...] = short_back_body(
        grad_ref[...], edge_ref, mixed_ref, sw_ref, turned_ref, out_ref, sums_ref, seqs, block
    )


def early_back(grad, edges, mixed, short_weight, turned, seqs, block):
    width, rows = grad.shape
    tile = 256
    flat = pl.BlockSpec((tile, rows), lambda j: (j, 0))
    part = pl.BlockSpec((1, tile, rows), lambda j: (0, j, 0))
    across = lambda height: pl.BlockSpec((1, height, tile), lambda j: (0, 0, j))
    return pl.pallas_call(
        lambda *refs: early_back_kernel(seqs, block, *refs),
        name="early_back",
        grid=(width // tile,),
        out_shape=(
            outside((1, width, rows), BF16), jax.ShapeDtypeStruct((width, width), BF16),
            jax.ShapeDtypeStruct((1, 8, width), F32),
        ),
        in_specs=[
            flat, pl.BlockSpec((1, 8, tile), lambda j: (2, 0, j)), part, pl.BlockSpec((3, tile), lambda j: (0, j)),
            pl.BlockSpec((width, rows), lambda j: (0, 0)),
        ],
        out_specs=(part, pl.BlockSpec((width, tile), lambda j: (0, j)), across(8)),
        compiler_params=pltpu.CompilerParams(vmem_limit_bytes=18 << 20),
    )(grad, edges, mixed[None], short_weight, turned)


def late_back_kernel(
    seqs, block, side_ref, conv_ref, long_ref, skip_ref, factor_ref, edge_ref, mixed_ref, sw_ref, turned_ref,
    out_ref, given_ref, kept_ref, sums_ref,
):
    skip = columns(skip_ref)[:, 0:1]
    grad = (conv_ref[...].astype(F32) + long_ref[...].astype(F32) * skip) * factor_ref[0]
    weight = short_back_body(
        grad, edge_ref, mixed_ref, sw_ref, turned_ref, out_ref, sums_ref, seqs, block
    )

    @pl.when(pl.program_id(0) == 0)
    def _():
        given_ref[...] = weight

    @pl.when(pl.program_id(0) == 1)
    def _():
        kept_ref[...] = weight


def late_back(side, conv, grad_long, skip, factors, edges, mixed, short_weight, turned, seqs, block):
    count, width, rows = mixed.shape
    tile = 256
    steps = width // tile
    group = lambda i, side_ref: jnp.where(i == 0, 1 - side_ref[0], side_ref[0])
    part = pl.BlockSpec((1, tile, rows), lambda i, j, side_ref: (group(i, side_ref), j, 0))
    flat = pl.BlockSpec((tile, rows), lambda i, j, side_ref: (j, 0))
    across = pl.BlockSpec((1, 8, tile), lambda i, j, side_ref: (group(i, side_ref), 0, j))
    given = pl.BlockSpec((width, tile), lambda i, j, side_ref: (0, jnp.where(i == 0, j, steps - 1)))
    kept = pl.BlockSpec((width, tile), lambda i, j, side_ref: (0, jnp.where(i == 0, 0, j)))
    return pl.pallas_call(
        lambda *refs: late_back_kernel(seqs, block, *refs),
        name="late_back",
        out_shape=(
            outside((count, width, rows), BF16), jax.ShapeDtypeStruct((width, width), BF16), jax.ShapeDtypeStruct((width, width), BF16),
            jax.ShapeDtypeStruct((count, 8, width), F32),
        ),
        grid_spec=pltpu.PrefetchScalarGridSpec(
            num_scalar_prefetch=1,
            grid=(2, steps),
            in_specs=[
                flat, flat, pl.BlockSpec((tile,), lambda i, j, side_ref: (j,)), part, across, part,
                pl.BlockSpec((3, tile), lambda i, j, side_ref: (0, (1 + group(i, side_ref)) * steps + j)),
                pl.BlockSpec((width, rows), lambda i, j, side_ref: (0, 0)),
            ],
            out_specs=(part, given, kept, across),
        ),
        compiler_params=pltpu.CompilerParams(vmem_limit_bytes=20 << 20),
    )(side, conv, grad_long, skip, factors, edges, mixed, short_weight, turned)


def back_kernel(ga_ref, gb_ref, w_ref, tok_ref, resid_ref, gain_ref, bias_ref, out_ref, sums_ref):
    width = tok_ref.shape[1]
    turned = contract(w_ref[:, :width], ga_ref[0], ((1,), (0,)))
    for part in range(2):
        turned += contract(w_ref[:, (part + 1) * width : (part + 2) * width], gb_ref[part], ((1,), (0,)))
    q = turned.T
    gain = row(gain_ref)
    _, unit, inverse = norm_forward(tok_ref[...].astype(F32), gain, row(bias_ref))
    scaled = q * gain
    out_ref[...] = resid_ref[...] + inverse * (
        scaled
        - jnp.mean(scaled, axis=-1, keepdims=True)
        - unit * jnp.mean(scaled * unit, axis=-1, keepdims=True)
    )
    sums_ref[0:1] = jnp.sum(q * unit, axis=0, keepdims=True)
    sums_ref[1:2] = jnp.sum(q, axis=0, keepdims=True)
    sums_ref[2:8] = jnp.zeros((6, width), F32)


def back(mixed_early, mixed_late, w_in, tokens, grad_resid, gain, bias):
    return pl.pallas_call(
        back_kernel,
        name="back",
        out_shape=(
            jax.ShapeDtypeStruct(tokens.shape, F32), jax.ShapeDtypeStruct((8, tokens.shape[1]), F32),
        ),
        in_specs=[vmem_spec()] * 7,
        out_specs=(vmem_spec(), vmem_spec()),
        compiler_params=pltpu.CompilerParams(vmem_limit_bytes=26 << 20),
    )(mixed_early, mixed_late, w_in, tokens, grad_resid, gain, bias)


def transform_tables(block):
    spots = np.arange(block, dtype=np.float64)
    angle = np.pi / block * (spots[None, :] + 0.5) * spots[:, None]
    table = np.concatenate([np.cos(angle), -np.sin(angle)], axis=1)
    high = table.astype(np.float32).astype(jnp.bfloat16)
    low = (table - high.astype(np.float64)).astype(np.float32).astype(jnp.bfloat16)
    return np.stack([high, low])


def mm(left, right):
    return contract(left, right, ((1,), (0,)))


def spectrum(block, high, low):
    return mm(block, high) + mm(block, low)


def invert(spec, high, low):
    head = spec.astype(BF16)
    tail = (spec - head.astype(F32)).astype(BF16)
    back = lambda part, table: contract(part, table, ((1,), (1,)))
    return (back(head, high) + (back(tail, high) + back(head, low))) * (1.0 / high.shape[0])


def filter_spectra(filt_ref, high, low, g_ref, channels, blocks, length):
    sign = (1 - 2 * (lax.broadcasted_iota(jnp.int32, (1, length), 1) % 2)).astype(F32)
    before = None
    for lag in range(blocks):
        now = spectrum(filt_ref[:, lag * length : (lag + 1) * length], high, low)
        rows = slice(lag * channels, (lag + 1) * channels)
        if before is None:
            g_ref[rows, :] = now
        else:
            g_ref[rows, :length] = now[:, :length] - sign * before[:, length:]
            g_ref[rows, length:] = now[:, length:] + sign * before[:, :length]
        before = now


def conv_forward_kernel(
    channels, blocks, length, seqs,
    x_ref, filt_ref, table_ref, out_ref, s_ref, g_ref,
):
    high, low = table_ref[0], table_ref[1]
    filter_spectra(filt_ref, high, low, g_ref, channels, blocks, length)
    for q in range(seqs):
        s_ref[q] = spectrum(x_ref[:, q * length : (q + 1) * length], high, low)

    def tile(step, carry):
        row = pl.multiple_of(step * 8, 8)
        for lane in range(0, length, 128):
            re, im = slice(lane, lane + 128), slice(length + lane, length + lane + 128)
            for q in range(seqs):
                for i in reversed(range(blocks)):
                    acc_re = acc_im = None
                    for j in range(i + 1):
                        s_rows = pl.ds(j * channels + row, 8)
                        g_rows = pl.ds((i - j) * channels + row, 8)
                        sr, si = s_ref[q, s_rows, re], s_ref[q, s_rows, im]
                        gr, gi = g_ref[g_rows, re], g_ref[g_rows, im]
                        new_re = sr * gr - si * gi
                        new_im = sr * gi + si * gr
                        acc_re = new_re if acc_re is None else acc_re + new_re
                        acc_im = new_im if acc_im is None else acc_im + new_im
                    rows = pl.ds(i * channels + row, 8)
                    s_ref[q, rows, re] = acc_re
                    s_ref[q, rows, im] = acc_im
        return carry

    lax.fori_loop(0, channels // 8, tile, 0)
    for q in range(seqs):
        out_ref[:, q * length : (q + 1) * length] = invert(s_ref[q], high, low).astype(BF16)


def conv_backward_kernel(
    channels, blocks, length, seqs,
    x_ref, y_ref, filt_ref, table_ref, out_ref, gfilt_ref, s_ref, q_ref, g_ref, l_ref,
):
    high, low = table_ref[0], table_ref[1]
    filter_spectra(filt_ref, high, low, g_ref, channels, blocks, length)
    for q in range(seqs):
        s_ref[q] = spectrum(x_ref[:, q * length : (q + 1) * length], high, low)
        q_ref[q] = spectrum(y_ref[:, q * length : (q + 1) * length], high, low)

    def tile(step, carry):
        row = pl.multiple_of(step * 8, 8)
        for lane in range(0, length, 128):
            re, im = slice(lane, lane + 128), slice(length + lane, length + lane + 128)
            for d in range(blocks):
                acc_re = acc_im = None
                for q in range(seqs):
                    for j in range(blocks - d):
                        s_rows = pl.ds(j * channels + row, 8)
                        y_rows = pl.ds((j + d) * channels + row, 8)
                        sr, si = s_ref[q, s_rows, re], s_ref[q, s_rows, im]
                        yr, yi = q_ref[q, y_rows, re], q_ref[q, y_rows, im]
                        new_re = sr * yr + si * yi
                        new_im = sr * yi - si * yr
                        acc_re = new_re if acc_re is None else acc_re + new_re
                        acc_im = new_im if acc_im is None else acc_im + new_im
                rows = pl.ds(d * channels + row, 8)
                l_ref[rows, re] = acc_re
                l_ref[rows, im] = acc_im
            for q in range(seqs):
                for j in range(blocks):
                    acc_re = acc_im = None
                    for i in range(j, blocks):
                        y_rows = pl.ds(i * channels + row, 8)
                        g_rows = pl.ds((i - j) * channels + row, 8)
                        yr, yi = q_ref[q, y_rows, re], q_ref[q, y_rows, im]
                        gr, gi = g_ref[g_rows, re], g_ref[g_rows, im]
                        new_re = gr * yr + gi * yi
                        new_im = gr * yi - gi * yr
                        acc_re = new_re if acc_re is None else acc_re + new_re
                        acc_im = new_im if acc_im is None else acc_im + new_im
                    rows = pl.ds(j * channels + row, 8)
                    q_ref[q, rows, re] = acc_re
                    q_ref[q, rows, im] = acc_im
        return carry

    lax.fori_loop(0, channels // 8, tile, 0)
    for q in range(seqs):
        out_ref[:, q * length : (q + 1) * length] = invert(q_ref[q], high, low).astype(BF16)
    sign = (1 - 2 * (lax.broadcasted_iota(jnp.int32, (1, length), 1) % 2)).astype(F32)
    for d in range(blocks):
        rows = slice(d * channels, (d + 1) * channels)
        real, imag = l_ref[rows, :length], l_ref[rows, length:]
        if d + 1 < blocks:
            after = slice((d + 1) * channels, (d + 2) * channels)
            real = real + sign * l_ref[after, length:]
            imag = imag - sign * l_ref[after, :length]
        both = jnp.concatenate([real, imag], axis=1)
        gfilt_ref[:, d * length : (d + 1) * length] = invert(both, high, low)


def conv_forward(x, filt, table, channels, blocks, length, seqs):
    rows = blocks * channels
    kernel = lambda *refs: conv_forward_kernel(channels, blocks, length, seqs, *refs)
    return pl.pallas_call(
        kernel,
        name="conv_forward",
        out_shape=jax.ShapeDtypeStruct((rows, seqs * length), BF16),
        in_specs=[vmem_spec()] * 3,
        out_specs=vmem_spec(),
        scratch_shapes=[
            pltpu.VMEM((seqs, rows, 2 * length), F32),
            pltpu.VMEM((rows, 2 * length), F32),
        ],
        compiler_params=pltpu.CompilerParams(vmem_limit_bytes=18 << 20),
    )(x, filt, table)


def conv_backward(x, y, filt, table, channels, blocks, length, seqs):
    rows = blocks * channels
    kernel = lambda *refs: conv_backward_kernel(channels, blocks, length, seqs, *refs)
    return pl.pallas_call(
        kernel,
        name="conv_backward",
        out_shape=(
            outside((rows, seqs * length), BF16),
            jax.ShapeDtypeStruct((channels, blocks * length), F32),
        ),
        in_specs=[vmem_spec()] * 4,
        out_specs=(vmem_spec(), vmem_spec()),
        scratch_shapes=[
            pltpu.VMEM((seqs, rows, 2 * length), F32),
            pltpu.VMEM((seqs, rows, 2 * length), F32),
            pltpu.VMEM((rows, 2 * length), F32),
            pltpu.VMEM((rows, 2 * length), F32),
        ],
        compiler_params=pltpu.CompilerParams(vmem_limit_bytes=26 << 20),
    )(x, y, filt, table)


def shifted(block, axis, distance):
    count = lax.axis_size(axis)
    route = [(i - distance, i) for i in range(count) if 0 <= i - distance < count]
    return lax.ppermute(block, axis, route)


def axis_bits(axis):
    size, bits, bit = lax.axis_size(axis), [], 1
    while bit < size:
        bits.append((axis, bit))
        bit *= 2
    return bits


def exchange(value, step):
    axis, bit = step
    return lax.ppermute(value, axis, [(i, i ^ bit) for i in range(lax.axis_size(axis))])


def side_of(step):
    axis, bit = step
    return (lax.axis_index(axis) // bit) % 2


class Route(list):
    twin = None
    lanes = 0


def total_of(kept, other):
    return (kept.astype(F32) + other.astype(F32)).astype(BF16)


def fold_kernel(count, ways, merged, _, *refs):
    ins, outs = refs[: 2 * ways * count], refs[2 * ways * count :]
    for i in range(ways * count):
        value = total_of(ins[2 * i][...], ins[2 * i + 1][...])
        if merged and i < ways:
            outs[i][:, : value.shape[1]] = value
        elif merged:
            outs[i - ways][:, outs[i - ways].shape[1] - value.shape[1] :] = value
        else:
            outs[i][...] = value


def fold(pairs, steps, merged=False):
    count = len(pairs)
    ways = 2 if steps else 1
    sizes = [pair[0].shape[0] // ways for pair in pairs]
    if any(size % 16 for size in sizes):
        sums = [total_of(*pair) for pair in pairs]
        if steps is None:
            return sums
        cut = lambda value, place, size: lax.dynamic_slice_in_dim(value, place * size, size, 0)
        pieces = [
            (cut(value, 1 - side_of(step), size), cut(value, side_of(step), size))
            for value, step, size in zip(sums, steps, sizes)
        ]
        if merged:
            return [tuple(jnp.concatenate(parts, axis=1) for parts in zip(*pieces))]
        return pieces
    most = max(sizes)
    grid = most // 64 if most >= 192 and all(size == most for size in sizes) and most % 64 == 0 else 1
    shapes, in_specs, args = [], [], []
    for i, ((kept, other), size) in enumerate(zip(pairs, sizes)):
        lanes = kept.shape[1]
        for way in range(ways):
            if steps:
                place = lambda j, sides_ref, i=i, way=way: (
                    (1 - sides_ref[i] if way == 0 else sides_ref[i]) * grid + j, 0
                )
            else:
                place = lambda j, sides_ref: (j, 0)
            in_specs += [pl.BlockSpec((size // grid, lanes), place)] * 2
            args += [kept, other]
            make = outside if most >= 384 and lanes >= 1536 else jax.ShapeDtypeStruct
            shapes.append(make((size, lanes), BF16))
    if merged:
        lanes = sum(pair[0].shape[1] for pair in pairs)
        shapes = [jax.ShapeDtypeStruct((most, lanes), BF16)] * ways
    out_specs = [
        pl.BlockSpec((shape.shape[0] // grid, shape.shape[1]), lambda j, sides_ref: (j, 0)) for shape in shapes
    ]
    sides = jnp.stack([side_of(step) for step in steps] if steps else [jnp.zeros((), jnp.int32)])
    outs = pl.pallas_call(
        lambda *refs: fold_kernel(count, ways, merged, *refs),
        name="fold",
        out_shape=shapes,
        grid_spec=pltpu.PrefetchScalarGridSpec(
            num_scalar_prefetch=1, grid=(grid,), in_specs=in_specs, out_specs=out_specs
        ),
        compiler_params=pltpu.CompilerParams(vmem_limit_bytes=(58 if most >= 192 and lanes >= 1536 else 14) << 20),
    )(sides.astype(jnp.int32), *args)
    return list(zip(outs[::2], outs[1::2])) if steps else list(outs)


def join_kernel(count, lanes, sides_ref, *refs):
    for i in range(count):
        for ref, place in ((refs[2 * i], sides_ref[i]), (refs[2 * i + 1], 1 - sides_ref[i])):
            if lanes:
                refs[2 * count][place] = ref[:, :lanes]
                refs[2 * count + 1][place] = ref[:, lanes:]
            else:
                refs[2 * count + i][place] = ref[...]


def join(pairs, steps, lanes=0):
    count = len(pairs)
    if any(pair[0].shape[0] % 16 for pair in pairs):
        outs = []
        for (own, other), step in zip(pairs, steps):
            first = side_of(step) == 0
            outs.append(jnp.concatenate([jnp.where(first, own, other), jnp.where(first, other, own)]))
        return [outs[0][:, :lanes], outs[0][:, lanes:]] if lanes else outs
    sides = jnp.stack([side_of(step) for step in steps]).astype(jnp.int32)
    in_specs, shapes = [], []
    for own, _ in pairs:
        rows, width = own.shape
        in_specs += [pl.BlockSpec((rows, width), lambda j: (0, 0))] * 2
        for part in (lanes, width - lanes) if lanes else (width,):
            shapes.append(jax.ShapeDtypeStruct((2, rows, part), BF16))
    outs = pl.pallas_call(
        lambda *refs: join_kernel(count, lanes, *refs),
        name="join",
        grid=(1,),
        out_shape=shapes,
        in_specs=[smem_spec()] + in_specs,
        out_specs=[pl.BlockSpec(shape.shape, lambda j: (0, 0, 0)) for shape in shapes],
        compiler_params=pltpu.CompilerParams(vmem_limit_bytes=8 << 20),
    )(sides, *[value for pair in pairs for value in pair])
    return [out.reshape(-1, out.shape[2]) for out in outs]


def quarters_do(row_side, lane_side, refs, put):
    for place, ref in enumerate(refs):
        h = row_side if place % 2 == 0 else 1 - row_side
        for l in range(2):

            @pl.when((lane_side == l) if place < 2 else (lane_side != l))
            def _():
                put(h, l, ref[...].astype(F32))


def widen_kernel(stacked, sides_ref, *refs):
    pieces, out_ref = refs[:4], refs[4]
    lanes = pieces[0].shape[1]

    def put(h, l, value):
        if stacked:
            width = lanes // out_ref.shape[1]
            for k in range(out_ref.shape[1]):
                out_ref[l, k, h] = value[:, k * width : (k + 1) * width]
        else:
            out_ref[h, :, l * lanes : (l + 1) * lanes] = value

    quarters_do(sides_ref[0], sides_ref[1], pieces, put)


def widen(sides, pieces, width, stacked):
    rows, lanes = pieces[0].shape
    tile = 64
    if stacked:
        count = lanes // width
        shape = (2, count, 2, rows, width)
        out = pl.BlockSpec((2, count, 2, tile, width), lambda j: (0, 0, 0, j, 0))
    else:
        shape = (2, rows, 2 * lanes)
        out = pl.BlockSpec((2, tile, 2 * lanes), lambda j: (0, j, 0))
    wide = pl.pallas_call(
        lambda *refs: widen_kernel(stacked, *refs),
        name="widen",
        grid=(rows // tile,),
        out_shape=jax.ShapeDtypeStruct(shape, F32),
        in_specs=[smem_spec()] + [pl.BlockSpec((tile, lanes), lambda j: (j, 0))] * 4,
        out_specs=out,
        compiler_params=pltpu.CompilerParams(vmem_limit_bytes=14 << 20),
    )(sides, *pieces)
    return wide.reshape(-1, shape[-1])


def widen_late_kernel(sides_ref, *refs):
    s_pieces, t_pieces, (in_ref, out_ref, last_ref) = refs[:4], refs[4:8], refs[8:]
    width = out_ref.shape[2]

    def put_s(h, l, value):
        in_ref[h, :, (l + 1) * width : (l + 2) * width] = value

    def put_t(h, l, value):
        if l == 0:
            in_ref[h, :, :width] = value[:, :width]
        else:
            out_ref[h] = value[:, :width]
        last_ref[l, h] = value[:, width:]

    quarters_do(sides_ref[0], sides_ref[1], s_pieces, put_s)
    quarters_do(sides_ref[2], sides_ref[1], t_pieces, put_t)


def widen_late(sides, s_pieces, t_pieces):
    rows, width = s_pieces[0].shape
    more = t_pieces[0].shape[1] - width
    tile = 64
    part = lambda lanes: pl.BlockSpec((tile, lanes), lambda j: (j, 0))
    both = lambda lanes: pl.BlockSpec((2, tile, lanes), lambda j: (0, j, 0))
    grad_in, grad_out, last = pl.pallas_call(
        widen_late_kernel,
        name="widen_late",
        grid=(rows // tile,),
        out_shape=(
            jax.ShapeDtypeStruct((2, rows, 3 * width), F32), jax.ShapeDtypeStruct((2, rows, width), F32),
            jax.ShapeDtypeStruct((2, 2, rows, more), F32),
        ),
        in_specs=[smem_spec()] + [part(width)] * 4 + [part(width + more)] * 4,
        out_specs=(
            both(3 * width), both(width), pl.BlockSpec((2, 2, tile, more), lambda j: (0, 0, j, 0)),
        ),
        compiler_params=pltpu.CompilerParams(vmem_limit_bytes=14 << 20),
    )(sides, *s_pieces, *t_pieces)
    return grad_in.reshape(-1, 3 * width), grad_out.reshape(-1, width), last.reshape(2, -1, more)


def unpack_kernel(features, hidden, wide, last_ref, net_ref, *refs):
    (g1, b1, b_in, sw, sb, fw1, fb1, fw2, fb2, fw3, skip, b_out, g2, b2, mb1, mb2) = refs
    width = g1.shape[0]
    fw3[...] = last_ref[0].T[:hidden]
    fw1[...] = net_ref[0, :features, :hidden]
    fb1[...] = net_ref[0, features : features + 1, :hidden].reshape(hidden)
    fw2[...] = net_ref[0, features + 1 : features + 1 + hidden, :hidden]
    fb2[...] = net_ref[0, features + 1 + hidden : features + 2 + hidden, :hidden].reshape(hidden)
    pieces = width // 128

    def put(ref, place, lane, row=None):
        for k in range(pieces):
            at = 128 + place * pieces + k
            value = net_ref[0, at : at + 1, :]
            lanes = slice(lane + k * 128, lane + (k + 1) * 128)
            if row is None:
                ref[lanes] = value.reshape(128)
            else:
                ref[row : row + 1, lanes] = value

    for place, ref in enumerate((skip, b_out, g2, b2, mb2)):
        put(ref, place, 0)
    for k in range(wide):
        put(mb1, 5 + k, k * width)
    put(g1, 5 + wide, 0)
    put(b1, 6 + wide, 0)
    for group in range(3):
        first = 7 + wide + 5 * group
        put(b_in, first, group * width)
        put(sb, first + 1, group * width)
        for tap in range(3):
            put(sw, first + 2 + tap, group * width, tap)


def unpack(last, features, hidden, wide, width):
    flat = lambda size: jax.ShapeDtypeStruct((size,), F32)
    grid = lambda *shape: jax.ShapeDtypeStruct(shape, F32)
    part = lambda h: pl.BlockSpec((1, width, 128), lambda i: (h, 0, 0))
    shapes = (
        flat(width), flat(width), flat(3 * width), grid(3, 3 * width), flat(3 * width),
        grid(features, hidden), flat(hidden), grid(hidden, hidden), flat(hidden), grid(hidden, width),
        flat(width), flat(width), flat(width), flat(width), flat(wide * width), flat(width),
    )
    whole = lambda shape: pl.BlockSpec(shape, lambda i: (0,) * len(shape))
    return pl.pallas_call(
        lambda *refs: unpack_kernel(features, hidden, wide, *refs),
        name="unpack",
        grid=(1,),
        out_shape=shapes,
        in_specs=[part(0), part(1)],
        out_specs=[whole(shape.shape) for shape in shapes],
        compiler_params=pltpu.CompilerParams(vmem_limit_bytes=14 << 20),
    )(last, last)


def orders():
    bits = axis_bits("bucket") + axis_bits("seq")
    first, rest = bits[0], bits[1:]
    if len(rest) == 4:
        y, x, near, far = rest
        turns = ([y, x, near, far], [x, y, near, far])
    else:
        turns = (rest, rest[1:] + rest[:1])
    return [Route([first] + turn) for turn in turns]


def work_order(last):
    if last == 4:
        return [
            ("s", 3), ("p", -3), ("s", 4), ("p", -2), ("s", 5), ("s", -4), ("s", -3), ("s", -2),
            ("last", 0), ("wide", 0),
        ]
    order = [("p", index) for index in range(5, last + 2)]
    order += [("s", index) for index in range(2, last + 2)]
    order += [("p", -index) for index in range(last, 1, -1)]
    order += [("s", -index) for index in range(last, 1, -1)]
    return order + [("last", 0), ("wide", 0)]


def held(value, *awaited):
    return lax.optimization_barrier((value,) + awaited)[0]


def local(
    tokens, cotangent, lengths, decay_rate, norm1_gain, norm1_bias, w_in, b_in,
    short_weight, short_bias, filter_w1, filter_b1, filter_w2, filter_b2, filter_w3,
    skip_gain, w_out, b_out, norm2_gain, norm2_bias, mlp_w1, mlp_b1, mlp_w2, mlp_b2,
):
    seqs, block, width = tokens.shape[1:]
    rows = seqs * block
    blocks = lax.axis_size("seq")
    full = blocks * block
    channels = width // blocks
    position = lax.axis_index("seq")
    place = position.reshape(1).astype(jnp.int32)
    table = jnp.asarray(transform_tables(block))
    flat_tokens = tokens.reshape(rows, width)

    edge_tokens = shifted(tokens[0, :, block - 2 :, :], "seq", 1).reshape(2 * seqs, width)
    normed, edge_normed, mixed_late, factors, signal = front(
        place, flat_tokens, edge_tokens, norm1_gain, norm1_bias, b_in, short_bias, short_weight, w_in,
        seqs, block,
    )
    signal_all = lax.all_to_all(signal, "seq", 0, 0, tiled=True)
    turned, mixed_early, gate_out = gate_part(
        place, normed, edge_normed, b_in, short_bias, short_weight, w_in, seqs, block
    )

    own = position * channels
    rates = lax.dynamic_slice_in_dim(decay_rate, own, channels)
    weight_three = lax.dynamic_slice_in_dim(filter_w3.astype(F32), own, channels, axis=1)

    second_weight = filter_w2.astype(F32)
    feats, hidden_one, slope_one, hidden_two, slope_two = filter_layers(
        filter_w1.astype(F32), filter_b1.astype(F32), second_weight, filter_b2.astype(F32), full
    )
    times = lax.broadcasted_iota(jnp.int32, (1, full), 1).astype(F32) / full
    window = jnp.exp(-times * rates[:, None]) + 0.05
    filt = (precise("hd,hp->dp", weight_three, hidden_two) * window).astype(BF16)
    long_all = conv_forward(signal_all, filt, table, channels, blocks, block, seqs)
    conv_long = lax.all_to_all(long_all, "seq", 0, 0, tiled=True)

    order_p, order_q = orders()
    core = order_p[0]
    side = side_of(core).reshape(1).astype(jnp.int32)
    (
        output, grad_resid, grad_long, grad_gate, given_p, kept_p, given_q, kept_q, grad_w_out, sums,
    ) = middle(
        side, place, lengths.reshape(seqs), conv_long, signal, gate_out, skip_gain, flat_tokens,
        cotangent.reshape(rows, width), w_out, b_out, norm2_gain, norm2_bias, mlp_b2, mlp_b1[None], mlp_w1,
        mlp_w2, seqs, block,
    )
    grad_long_all = lax.all_to_all(grad_long, "seq", 0, 0, tiled=True)

    def turn(streams, index, *awaited):
        pairs, after = [], []
        for (given, kept), order in streams:
            other = exchange(given, order[index])
            if awaited:
                kept, awaited = held(kept, *awaited), ()
            pairs.append((kept, other))
            after.append(order[index + 1] if index + 1 < len(order) else None)
        routes = [order for _, order in streams]
        merged = len(streams) == 2 and after[0] is not None and after[0] == after[1]
        parts = fold(pairs, after if after[0] else None, merged)
        if merged:
            route = Route(routes[0])
            route.twin, route.lanes = routes[1], pairs[0][0].shape[1]
            routes = [route]
        return list(zip(parts, routes))

    def turn_back(streams, index, *awaited):
        pairs = []
        for part, order in streams:
            other = exchange(part, order[index])
            if awaited:
                part, awaited = held(part, *awaited), ()
            pairs.append((part, other))
        routes = [order for _, order in streams]
        route = routes[0]
        lanes = route.lanes if route.twin and route[index - 1] != route.twin[index - 1] else 0
        parts = join(pairs, [order[index] for order in routes], lanes)
        return list(zip(parts, [Route(route), route.twin] if lanes else routes))

    def quarters(streams, *awaited):
        others = [exchange(part, order[1]) for part, order in streams]
        if awaited:
            others = lax.optimization_barrier(tuple(others) + awaited)[: len(others)]
        return [
            [part, other, exchange(part, core), exchange(other, core)]
            for (part, _), other in zip(streams, others)
        ]

    def first_of(streams):
        value = streams[0][0]
        return value[0] if isinstance(value, tuple) else value

    last = len(order_p) - 1
    parts = turn([((given_p, kept_p), order_p), ((given_q, kept_q), order_q)], 0)
    grad_long_all = held(grad_long_all, first_of(parts))
    back_all, grad_filter = conv_backward(
        signal_all, grad_long_all, filt, table, channels, blocks, block, seqs
    )
    back_conv = lax.all_to_all(back_all, "seq", 0, 0, tiled=True)
    last_w3, net = filter_back(
        own.reshape(1).astype(jnp.int32), grad_filter, window, feats, hidden_one, slope_one, hidden_two,
        slope_two, second_weight, weight_three, width,
    )
    features, hidden = filter_w1.shape
    heads = features + hidden + 2
    parts = turn(parts, 1, last_w3)
    back_conv = held(back_conv, first_of(parts))
    edges = all_edges(back_conv, grad_long, skip_gain, factors, grad_gate, seqs, block)
    edges = shifted(edges, "seq", -1)
    late_grads, given_s, kept_s, sums_late = late_back(
        side, back_conv, grad_long, skip_gain, factors, edges, mixed_late, short_weight, turned, seqs,
        block,
    )
    parts = turn(parts, 2, late_grads)
    stream_s = turn([((held(given_s, first_of(parts)), kept_s), order_p)], 0)
    gate_grads, w_in_early, sums_early = early_back(
        held(grad_gate, first_of(stream_s)), edges, mixed_early, short_weight, turned, seqs, block
    )
    parts = turn(parts, 3, gate_grads)
    tokens_grad, sums_norm = back(
        gate_grads, held(late_grads, first_of(parts)), w_in, flat_tokens, grad_resid, norm1_gain,
        norm1_bias,
    )
    if last == 4:
        stream_s = turn(stream_s, 1, tokens_grad)
        parts = turn(parts, 4, first_of(stream_s))
    wide = sums.shape[0] - 8
    shorts = jnp.concatenate([sums_early, sums_late], axis=0)
    small = jnp.concatenate(
        [sums[:5], sums[8:], sums_norm[:2], shorts[:, :5].reshape(-1, width)], axis=0
    )
    more = small.size // 128
    net = jnp.concatenate(
        [net, small.reshape(more, 128), jnp.zeros((width - 128 - more, 128), F32)], axis=0
    )
    part_t = choose(side, held(w_in_early, first_of(parts)), last_w3, grad_w_out, net)
    stream_t = turn([(part_t, order_q)], 0)
    token = first_of(stream_t)
    if last == 4:
        parts = turn_back(parts, 4, token)
        stream_t = turn(stream_t, 1, first_of(parts))
        token = first_of(stream_t)
    state = {"p": parts, "s": stream_s + stream_t}
    for piece, index in work_order(last):
        if piece == "last":
            last_p, last_q = quarters(state["p"], token)
            token = last_q[1]
        elif piece == "wide":
            sides_of = lambda order: jnp.stack([side_of(order[1]), side_of(core)]).astype(jnp.int32)
            last_p[0] = held(last_p[0], token)
            sum_w1 = widen(sides_of(order_p), last_p, width, False)
            last_q[0] = held(last_q[0], sum_w1)
            sum_w2 = widen(sides_of(order_q), last_q, width, True)
            token = sum_w2
        elif index > 0:
            state[piece] = turn(state[piece], index - 1, token)
            token = first_of(state[piece])
        else:
            state[piece] = turn_back(state[piece], -index, token)
            token = first_of(state[piece])
    last_s, last_t = quarters(state["s"], token)
    sides = jnp.stack([side_of(order_p[1]), side_of(core), side_of(order_q[1])]).astype(jnp.int32)
    sum_w_in, sum_w_out, sum_last = widen_late(sides, last_s, last_t)
    small = unpack(sum_last, features, hidden, wide, width)
    return (
        output.reshape(tokens.shape), tokens_grad.reshape(tokens.shape), *small[:2], sum_w_in, *small[2:11],
        sum_w_out, *small[11:14], sum_w1, small[14], sum_w2, small[15],
    )


def solution(mesh):
    split = P("bucket", None, "seq", None)
    in_specs = (split, split, P("bucket", None)) + (P(),) * 21
    out_specs = (split, split) + (P(),) * 20
    return jax.shard_map(local, mesh=mesh, in_specs=in_specs, out_specs=out_specs, check_vma=False)
```

```python
import math

import jax
import jax.numpy as jnp
import numpy as np
from jax import lax
from jax.experimental import pallas as pl
from jax.experimental.pallas import tpu as pltpu
from jax.sharding import PartitionSpec as P

HIGH = lax.Precision.HIGHEST
EPSILON = 1e-05
F32 = jnp.float32
BF16 = jnp.bfloat16


def norm_forward(values, gain, bias):
    center = values - jnp.mean(values, axis=-1, keepdims=True)
    inverse = lax.rsqrt(jnp.mean(center * center, axis=-1, keepdims=True) + EPSILON)
    unit = center * inverse
    return (unit * gain + bias, unit, inverse)


def precise(formula, left, right):
    return jnp.einsum(formula, left, right, precision=HIGH, preferred_element_type=F32)


def position_features(length):
    steps = lax.broadcasted_iota(jnp.int32, (1, length), 1).astype(F32)
    bands = 0.0001 + lax.broadcasted_iota(jnp.int32, (16, 1), 0).astype(F32) * (
        (15.0 - 0.0001) / 15.0
    )
    phase = 2.0 * math.pi / length * steps * bands
    return jnp.concatenate([steps / length, jnp.cos(phase), -jnp.sin(phase)], axis=0)


def filter_layers(weight_one, bias_one, weight_two, bias_two, length):
    feats = position_features(length)
    first = precise("eh,ep->hp", weight_one, feats) + bias_one[:, None]
    hidden = jnp.sin(first)
    second = precise("hk,hp->kp", weight_two, hidden) + bias_two[:, None]
    return feats, hidden, jnp.cos(first), jnp.sin(second), jnp.cos(second)


def exact(left, right, dims):
    return lax.dot_general(
        left, right, (dims, ((), ())), precision=HIGH, preferred_element_type=F32
    )


def filter_back_kernel(
    channels, own_ref, grad_ref, window_ref, feats_ref, h1_ref, c1_ref, h2_ref, c2_ref, w2_ref, w3_ref,
    last_ref, net_ref,
):
    hidden = h1_ref.shape[0]
    features = feats_ref.shape[0]
    shaped = grad_ref[...] * window_ref[...]
    ones = jnp.ones((8, shaped.shape[1]), F32)
    last_ref[...] = jnp.zeros_like(last_ref)
    net_ref[...] = jnp.zeros_like(net_ref)
    rows = pl.ds(pl.multiple_of(own_ref[0], 16), channels)
    grad_w3 = exact(shaped, h2_ref[...], ((1,), (1,)))
    last_ref[rows, :] = jnp.concatenate([grad_w3, jnp.zeros_like(grad_w3)], axis=1).astype(BF16)
    second = exact(w3_ref[...], shaped, ((1,), (0,))) * c2_ref[...]
    first = exact(w2_ref[...], second, ((1,), (0,))) * c1_ref[...]
    place = 0
    for value in (
        exact(feats_ref[...], first, ((1,), (1,))), exact(ones, first, ((1,), (1,)))[:1],
        exact(h1_ref[...], second, ((1,), (1,))), exact(ones, second, ((1,), (1,)))[:1],
    ):
        net_ref[place : place + value.shape[0], :hidden] = value
        place += value.shape[0]


def filter_back(own, grad, window, feats, h1, c1, h2, c2, w2, w3, width):
    channels = grad.shape[0]
    return pl.pallas_call(
        lambda *refs: filter_back_kernel(channels, *refs),
        name="filter_back",
        out_shape=(
            jax.ShapeDtypeStruct((width, 128), BF16), jax.ShapeDtypeStruct((128, 128), F32),
        ),
        in_specs=[smem_spec()] + [vmem_spec()] * 9,
        out_specs=(vmem_spec(), vmem_spec()),
        compiler_params=pltpu.CompilerParams(vmem_limit_bytes=14 << 20),
    )(own, grad, window, feats, h1, c1, h2, c2, w2, w3)


def choose_kernel(side_ref, early_ref, last_ref, out_ref, net_ref, given_ref, kept_ref):
    low_side = side_ref[0] == 0
    width = early_ref.shape[1]
    parts = (
        (early_ref[...], out_ref[...], slice(0, width)),
        (last_ref[...], net_ref[...].astype(BF16), slice(width, width + 128)),
    )
    for low_half, high_half, lanes in parts:
        given_ref[:, lanes] = jnp.where(low_side, high_half, low_half)
        kept_ref[:, lanes] = jnp.where(low_side, low_half, high_half)


def choose(side, early, last, grad_out, net):
    width = early.shape[0]
    tile = 128
    part = lambda lanes: pl.BlockSpec((tile, lanes), lambda j: (j, 0))
    shape = jax.ShapeDtypeStruct((width, width + 128), BF16)
    return tuple(
        pl.pallas_call(
            choose_kernel,
            name="choose",
            grid=(width // tile,),
            out_shape=(shape, shape),
            in_specs=[smem_spec(), part(width), part(128), part(width), part(128)],
            out_specs=(part(width + 128), part(width + 128)),
            compiler_params=pltpu.CompilerParams(vmem_limit_bytes=8 << 20),
        )(side, early, last, grad_out, net)
    )


def outside(shape, dtype):
    return pltpu.HBM(shape, dtype)


def vmem_spec():
    return pl.BlockSpec(memory_space=pltpu.VMEM)


def smem_spec():
    return pl.BlockSpec(memory_space=pltpu.SMEM)


def contract(left, right, dims):
    return lax.dot_general(left, right, (dims, ((), ())), preferred_element_type=F32)


def lane_sums(parts):
    ones = jnp.ones((8, 128), BF16)
    heads, tails = [], []
    for part in parts:
        folded = part[:, :128]
        for lane in range(128, part.shape[1], 128):
            folded = folded + part[:, lane : lane + 128]
        head = folded.astype(BF16)
        heads.append(head)
        tails.append((folded - head.astype(F32)).astype(BF16))
    both = contract(ones, jnp.concatenate(heads + tails, axis=0), ((1,), (1,)))
    count = parts[0].shape[0]
    half = count * len(parts)
    return [
        both[:1, k * count : (k + 1) * count] + both[:1, half + k * count : half + (k + 1) * count]
        for k in range(len(parts))
    ]


def columns(*rows):
    parts = [row[...].astype(F32).reshape(-1, row.shape[-1]) for row in rows]
    count = sum(part.shape[0] for part in parts)
    parts.append(jnp.zeros((8 - count, parts[0].shape[1]), F32))
    return jnp.concatenate(parts, axis=0).T


def row(ref):
    return ref[...].astype(F32).reshape(1, ref.shape[0])


def short_filter(mixed, edge, cols, seqs, block):
    spots = lax.broadcasted_iota(jnp.int32, (1, block), 1)
    pieces = []
    for q in range(seqs):
        now = mixed[:, q * block : (q + 1) * block]
        near, far = edge[:, 2 * q + 1 : 2 * q + 2], edge[:, 2 * q : 2 * q + 1]
        once = jnp.where(spots == 0, near, pltpu.roll(now, 1, 1))
        twice = jnp.where(spots == 0, far, jnp.where(spots == 1, near, pltpu.roll(now, 2, 1)))
        pieces.append(
            cols[:, 2:3] * now + cols[:, 3:4] * once + cols[:, 4:5] * twice + cols[:, 1:2]
        )
    return jnp.concatenate(pieces, axis=1)


def project(weight, normed, edge_normed, cols, inside, seqs, block):
    mixed = (contract(weight, normed, ((0,), (1,))) + cols[:, 0:1]).astype(BF16)
    edge = (contract(weight, edge_normed, ((0,), (1,))) + cols[:, 0:1]).astype(BF16)
    edge = edge.astype(F32) * inside
    return mixed, short_filter(mixed.astype(F32), edge, cols, seqs, block)


def front_kernel(
    seqs, block, first_ref, tok_ref, edge_ref, gain_ref, bias_ref, bb_ref, bc_ref, sbb_ref, sbc_ref, swb_ref,
    swc_ref, wb_ref, wc_ref, normed_ref, edge_normed_ref, mixed_ref, factor_ref, signal_ref,
):
    @pl.when(pl.program_id(0) == 0)
    def _():
        gain, bias = row(gain_ref), row(bias_ref)
        normed_ref[...] = norm_forward(tok_ref[...].astype(F32), gain, bias)[0].astype(BF16)
        edge_normed_ref[...] = norm_forward(edge_ref[...].astype(F32), gain, bias)[0].astype(BF16)

    normed, edge_normed = normed_ref[...], edge_normed_ref[...]
    inside = (first_ref[0] > 0).astype(F32)
    mixed_ref[0], gate_in = project(
        wb_ref[...], normed, edge_normed, columns(bb_ref, sbb_ref, swb_ref), inside, seqs, block
    )
    mixed_ref[1], values = project(
        wc_ref[...], normed, edge_normed, columns(bc_ref, sbc_ref, swc_ref), inside, seqs, block
    )
    factor_ref[0] = values
    factor_ref[1] = gate_in
    signal_ref[...] = (gate_in * values).astype(BF16)


def front(position, tokens, edge, gain, bias, b_in, short_bias, short_weight, w_in, seqs, block):
    rows, width = tokens.shape
    tile = 256
    steps = width // tile
    fixed = lambda shape: pl.BlockSpec(shape, lambda j: (0,) * len(shape))
    weight = lambda part: pl.BlockSpec((width, tile), lambda j: (0, part * steps + j))
    flat = lambda part: pl.BlockSpec((tile,), lambda j: (part * steps + j,))
    taps = lambda part: pl.BlockSpec((3, tile), lambda j: (0, part * steps + j))
    both = pl.BlockSpec((2, tile, rows), lambda j: (0, j, 0))
    return pl.pallas_call(
        lambda *refs: front_kernel(seqs, block, *refs),
        name="front",
        grid=(steps,),
        out_shape=(
            jax.ShapeDtypeStruct((rows, width), BF16), jax.ShapeDtypeStruct(edge.shape, BF16),
            jax.ShapeDtypeStruct((2, width, rows), BF16), jax.ShapeDtypeStruct((2, width, rows), F32),
            jax.ShapeDtypeStruct((width, rows), BF16),
        ),
        in_specs=[
            smem_spec(), fixed((rows, width)), fixed(edge.shape), fixed(gain.shape), fixed(bias.shape),
            flat(1), flat(2), flat(1), flat(2), taps(1), taps(2), weight(1), weight(2),
        ],
        out_specs=(
            fixed((rows, width)), fixed(edge.shape), both, both,
            pl.BlockSpec((tile, rows), lambda j: (j, 0)),
        ),
        compiler_params=pltpu.CompilerParams(vmem_limit_bytes=58 << 20),
    )(
        position, tokens, edge, gain, bias, b_in, b_in, short_bias, short_bias, short_weight,
        short_weight, w_in, w_in,
    )


def gate_kernel(
    seqs, block, first_ref, normed_ref, edge_normed_ref, b_ref, sb_ref, sw_ref, w_ref, turned_ref,
    mixed_ref, gate_ref,
):
    normed = normed_ref[...]

    @pl.when(pl.program_id(0) == 0)
    def _():
        turned_ref[...] = normed.T

    inside = (first_ref[0] > 0).astype(F32)
    mixed_ref[...], gate_ref[...] = project(
        w_ref[...], normed, edge_normed_ref[...], columns(b_ref, sb_ref, sw_ref), inside, seqs, block
    )


def gate_part(position, normed, edge_normed, b_in, short_bias, short_weight, w_in, seqs, block):
    rows, width = normed.shape
    tile = 256
    fixed = lambda shape: pl.BlockSpec(shape, lambda j: (0,) * len(shape))
    flat = pl.BlockSpec((tile,), lambda j: (j,))
    out = pl.BlockSpec((tile, rows), lambda j: (j, 0))
    return pl.pallas_call(
        lambda *refs: gate_kernel(seqs, block, *refs),
        name="gate_part",
        grid=(width // tile,),
        out_shape=(
            jax.ShapeDtypeStruct((width, rows), BF16), jax.ShapeDtypeStruct((width, rows), BF16),
            jax.ShapeDtypeStruct((width, rows), F32),
        ),
        in_specs=[
            smem_spec(), fixed((rows, width)), fixed(edge_normed.shape), flat, flat,
            pl.BlockSpec((3, tile), lambda j: (0, j)), pl.BlockSpec((width, tile), lambda j: (0, j)),
        ],
        out_specs=(fixed((width, rows)), out, out),
        compiler_params=pltpu.CompilerParams(vmem_limit_bytes=58 << 20),
    )(position, normed, edge_normed, b_in, short_bias, short_weight, w_in)


def row_mask(position, lengths_ref, seqs, block):
    spots = position * block + lax.broadcasted_iota(jnp.int32, (block, 1), 0)
    return jnp.concatenate([(spots < lengths_ref[q]).astype(F32) for q in range(seqs)], axis=0)


def middle_kernel(
    seqs, block, side_ref, position_ref, lengths_ref, conv_ref, signal_ref, gate_ref, skip_ref, tok_ref,
    cot_ref, w_out_ref, b_out_ref, gain_ref, bias_ref, b2_ref, b1_ref, w1_ref, w2_ref,
    out_ref, resid_grad_ref, long_ref, gate_grad_ref, given1_ref, kept1_ref, given2_ref, kept2_ref,
    gwo_ref, sums_ref,
    gated_ref, n2_ref, n2t_ref, unit_ref, inv_ref, final_ref, gf_ref, q_ref, lout_ref,
):
    step = pl.program_id(0)
    last = pl.num_programs(0) - 1
    b_out, gain, bias, b2 = row(b_out_ref), row(gain_ref), row(bias_ref), row(b2_ref)

    @pl.when(step == 0)
    def _():
        skip = columns(skip_ref)[:, 0:1]
        long_out = conv_ref[...].astype(F32) + signal_ref[...].astype(F32) * skip
        lout_ref[...] = long_out
        gated = (long_out * gate_ref[...]).astype(BF16)
        gated_ref[...] = gated
        branch = contract(gated, w_out_ref[...], ((0,), (0,))) + b_out
        resid = tok_ref[...].astype(F32) + branch
        normed, unit, inverse = norm_forward(resid, gain, bias)
        n2_ref[...] = normed.astype(BF16)
        n2t_ref[...] = normed.astype(BF16).T
        unit_ref[...] = unit
        inv_ref[...] = jnp.broadcast_to(inverse, inv_ref.shape)
        final_ref[...] = resid + b2
        valid = row_mask(position_ref[0], lengths_ref, seqs, block)
        gf_ref[...] = (cot_ref[...].astype(F32) * valid).astype(BF16)
        q_ref[...] = jnp.zeros_like(q_ref)

    w1, w2, gf = w1_ref[...], w2_ref[...], gf_ref[...]
    pre = contract(n2_ref[...], w1, ((1,), (0,))) + b1_ref[...].astype(F32)
    grad_active = contract(gf, w2, ((1,), (1,)))
    cumulative, slope = normal_terms(pre)
    active = (pre * cumulative).astype(BF16)
    grad_pre = grad_active * slope
    grad_low = grad_pre.astype(BF16)
    final_ref[...] += contract(active, w2, ((1,), (0,)))
    q_ref[...] += contract(grad_low, w1, ((1,), (1,)))
    grad_two = contract(active, gf, ((0,), (0,))).astype(BF16)
    grad_one = contract(n2t_ref[...], grad_low, ((1,), (0,))).astype(BF16)

    @pl.when(step <= last // 2)
    def _():
        given1_ref[...] = grad_one
        given2_ref[...] = grad_two

    @pl.when(step > last // 2)
    def _():
        kept1_ref[...] = grad_one
        kept2_ref[...] = grad_two

    half = pl.num_programs(0) // 2
    chunk = jnp.where(step < half, half * (1 - side_ref[0]) + step, half * side_ref[0] + step - half)
    sums_ref[pl.ds(8 + chunk, 1)] = jnp.sum(grad_low.astype(F32), axis=0, keepdims=True)

    @pl.when(step == last)
    def _():
        valid = row_mask(position_ref[0], lengths_ref, seqs, block)
        out_ref[...] = (final_ref[...] * valid).astype(BF16)
        grad_final = gf_ref[...].astype(F32)
        q, unit = q_ref[...], unit_ref[...]
        scaled = q * gain
        grad_resid = grad_final + inv_ref[:, 0:1] * (
            scaled
            - jnp.mean(scaled, axis=-1, keepdims=True)
            - unit * jnp.mean(scaled * unit, axis=-1, keepdims=True)
        )
        resid_grad_ref[...] = grad_resid
        grad_branch = grad_resid.astype(BF16)
        grad_gated = contract(w_out_ref[...], grad_branch, ((1,), (1,)))
        grad_long = (grad_gated * gate_ref[...]).astype(BF16)
        long_ref[...] = grad_long
        gate_grad_ref[...] = grad_gated * lout_ref[...]
        gwo_ref[...] = contract(gated_ref[...], grad_branch, ((1,), (0,))).astype(BF16)
        skip_sum = lane_sums([grad_long.astype(F32) * signal_ref[...].astype(F32)])[0]
        total = lambda part: jnp.sum(part, axis=0, keepdims=True)
        sums_ref[0:1] = skip_sum
        sums_ref[1:2] = total(grad_branch.astype(F32))
        sums_ref[2:3] = total(q * unit)
        sums_ref[3:4] = total(q)
        sums_ref[4:5] = total(grad_final)
        sums_ref[5:8] = jnp.zeros((3, sums_ref.shape[1]), F32)


def normal_terms(pre):
    cumulative = 0.5 * (1.0 + lax.erf(pre * (1.0 / math.sqrt(2.0))))
    density = jnp.exp(-0.5 * pre * pre) * (1.0 / math.sqrt(2.0 * math.pi))
    return cumulative, cumulative + pre * density


def middle(
    side, position, lengths, conv, signal, gate, skip, tokens, cotangent, w_out, b_out, gain, bias, b2, b1, w1,
    w2, seqs, block,
):
    count, width = tokens.shape
    hidden = w1.shape[1]
    chunk = width
    steps = hidden // chunk
    half = steps // 2
    once = lambda shape: pl.BlockSpec(
        shape, lambda j, side_ref: (0,) * len(shape), pipeline_mode=pl.Buffered(1)
    )

    def which(j, side_ref):
        side = side_ref[0]
        return jnp.where(j < half, half * (1 - side) + j, half * side + j - half)

    across = lambda height: pl.BlockSpec((height, chunk), lambda j, side_ref: (0, which(j, side_ref)))
    given = pl.BlockSpec((width, chunk), lambda j, side_ref: (0, jnp.minimum(j, half - 1)))
    kept = pl.BlockSpec((width, chunk), lambda j, side_ref: (0, jnp.maximum(j - half, 0)))
    wide, tall = (count, width), (width, count)
    shape = jax.ShapeDtypeStruct
    scratch = pltpu.VMEM
    part = shape((width, half * chunk), BF16)
    return pl.pallas_call(
        lambda *refs: middle_kernel(seqs, block, *refs),
        name="middle",
        out_shape=(
            shape(wide, BF16), shape(wide, F32), shape(tall, BF16), shape(tall, F32),
            part, part, part, part, shape((width, width), BF16),
            shape((8 + steps, width), F32),
        ),
        grid_spec=pltpu.PrefetchScalarGridSpec(
            num_scalar_prefetch=1,
            grid=(steps,),
            in_specs=[
                smem_spec(), smem_spec(), once(tall), once(tall), once(tall), once(skip.shape),
                once(wide), once(wide), once((width, width)), once(b_out.shape), once(gain.shape),
                once(bias.shape), once(b2.shape),
                across(1), across(width),
                pl.BlockSpec((chunk, width), lambda j, side_ref: (which(j, side_ref), 0)),
            ],
            out_specs=(
                once(wide), once(wide), once(tall), once(tall), given, kept, given, kept,
                once((width, width)), once((8 + steps, width)),
            ),
            scratch_shapes=[
                scratch(tall, BF16), scratch(wide, BF16), scratch(tall, BF16), scratch(wide, F32),
                scratch((count, 128), F32), scratch(wide, F32), scratch(wide, BF16), scratch(wide, F32),
                scratch(tall, F32),
            ],
        ),
        compiler_params=pltpu.CompilerParams(vmem_limit_bytes=58 << 20),
    )(
        side, position, lengths, conv, signal, gate, skip, tokens, cotangent, w_out, b_out, gain, bias, b2, b1,
        w1, w2,
    )


def first_spots(heads):
    lanes = lax.broadcasted_iota(jnp.int32, (1, 128), 1)
    edge = jnp.zeros(heads[0].shape, F32)
    for q, head in enumerate(heads):
        head = pltpu.roll(head, 2 * q, 1) if q else head
        edge = jnp.where((lanes >= 2 * q) & (lanes < 2 * q + 2), head, edge)
    return edge.T[:8]


def edges_kernel(seqs, skip_ref, *refs):
    skip = columns(skip_ref)[:, 0:1]
    out_ref = refs[-1]
    signals = [
        refs[4 * q][...].astype(F32) + refs[4 * q + 1][...].astype(F32) * skip for q in range(seqs)
    ]
    for part in range(2):
        out_ref[part] = first_spots([signals[q] * refs[4 * q + 2][part] for q in range(seqs)])
    out_ref[2] = first_spots([refs[4 * q + 3][...] for q in range(seqs)])


def all_edges(conv, grad_long, skip, factors, gate, seqs, block):
    width = conv.shape[0]
    specs, args = [], []
    for q in range(seqs):
        place = q * block // 128
        flat = pl.BlockSpec((width, 128), lambda i, place=place: (0, place))
        specs += [flat, flat, pl.BlockSpec((2, width, 128), lambda i, place=place: (0, 0, place)), flat]
        args += [conv, grad_long, factors, gate]
    return pl.pallas_call(
        lambda *refs: edges_kernel(seqs, *refs),
        name="all_edges",
        grid=(1,),
        out_shape=jax.ShapeDtypeStruct((3, 8, width), F32),
        in_specs=[pl.BlockSpec(skip.shape, lambda i: (0,))] + specs,
        out_specs=pl.BlockSpec((3, 8, width), lambda i: (0, 0, 0)),
        compiler_params=pltpu.CompilerParams(vmem_limit_bytes=14 << 20),
    )(skip, *args)


def short_back_body(grad, edge_ref, mixed_ref, sw_ref, turned_ref, out_ref, sums_ref, seqs, block):
    taps = columns(sw_ref)
    edge = edge_ref[0].T
    spots = lax.broadcasted_iota(jnp.int32, (1, block), 1)
    mixed = mixed_ref[0].astype(F32)
    once, twice = [], []
    for q in range(seqs):
        now = grad[:, q * block : (q + 1) * block]
        near, far = edge[:, 2 * q : 2 * q + 1], edge[:, 2 * q + 1 : 2 * q + 2]
        end = block - 1
        once.append(jnp.where(spots == end, near, pltpu.roll(now, block - 1, 1)))
        twice.append(
            jnp.where(
                spots == end, far, jnp.where(spots == end - 1, near, pltpu.roll(now, block - 2, 1))
            )
        )
    once, twice = jnp.concatenate(once, axis=1), jnp.concatenate(twice, axis=1)
    low = (taps[:, 0:1] * grad + taps[:, 1:2] * once + taps[:, 2:3] * twice).astype(BF16)
    out_ref[0] = low
    sums_ref[0, 0:1] = contract(jnp.ones((8, low.shape[1]), BF16), low, ((1,), (1,)))[:1]
    for place, total in enumerate(lane_sums([grad, mixed * grad, mixed * once, mixed * twice])):
        sums_ref[0, place + 1 : place + 2] = total
    sums_ref[0, 5:8] = jnp.zeros((3, sums_ref.shape[2]), F32)
    return contract(turned_ref[...], low, ((1,), (1,))).astype(BF16)


def early_back_kernel(
    seqs, block, grad_ref, edge_ref, mixed_ref, sw_ref, turned_ref, out_ref, gw_ref, sums_ref
):
    gw_ref[...] = short_back_body(
        grad_ref[...], edge_ref, mixed_ref, sw_ref, turned_ref, out_ref, sums_ref, seqs, block
    )


def early_back(grad, edges, mixed, short_weight, turned, seqs, block):
    width, rows = grad.shape
    tile = 256
    flat = pl.BlockSpec((tile, rows), lambda j: (j, 0))
    part = pl.BlockSpec((1, tile, rows), lambda j: (0, j, 0))
    across = lambda height: pl.BlockSpec((1, height, tile), lambda j: (0, 0, j))
    return pl.pallas_call(
        lambda *refs: early_back_kernel(seqs, block, *refs),
        name="early_back",
        grid=(width // tile,),
        out_shape=(
            outside((1, width, rows), BF16), jax.ShapeDtypeStruct((width, width), BF16),
            jax.ShapeDtypeStruct((1, 8, width), F32),
        ),
        in_specs=[
            flat, pl.BlockSpec((1, 8, tile), lambda j: (2, 0, j)), part, pl.BlockSpec((3, tile), lambda j: (0, j)),
            pl.BlockSpec((width, rows), lambda j: (0, 0)),
        ],
        out_specs=(part, pl.BlockSpec((width, tile), lambda j: (0, j)), across(8)),
        compiler_params=pltpu.CompilerParams(vmem_limit_bytes=18 << 20),
    )(grad, edges, mixed[None], short_weight, turned)


def late_back_kernel(
    seqs, block, side_ref, conv_ref, long_ref, skip_ref, factor_ref, edge_ref, mixed_ref, sw_ref, turned_ref,
    out_ref, given_ref, kept_ref, sums_ref,
):
    skip = columns(skip_ref)[:, 0:1]
    grad = (conv_ref[...].astype(F32) + long_ref[...].astype(F32) * skip) * factor_ref[0]
    weight = short_back_body(
        grad, edge_ref, mixed_ref, sw_ref, turned_ref, out_ref, sums_ref, seqs, block
    )

    @pl.when(pl.program_id(0) == 0)
    def _():
        given_ref[...] = weight

    @pl.when(pl.program_id(0) == 1)
    def _():
        kept_ref[...] = weight


def late_back(side, conv, grad_long, skip, factors, edges, mixed, short_weight, turned, seqs, block):
    count, width, rows = mixed.shape
    tile = 256
    steps = width // tile
    group = lambda i, side_ref: jnp.where(i == 0, 1 - side_ref[0], side_ref[0])
    part = pl.BlockSpec((1, tile, rows), lambda i, j, side_ref: (group(i, side_ref), j, 0))
    flat = pl.BlockSpec((tile, rows), lambda i, j, side_ref: (j, 0))
    across = pl.BlockSpec((1, 8, tile), lambda i, j, side_ref: (group(i, side_ref), 0, j))
    given = pl.BlockSpec((width, tile), lambda i, j, side_ref: (0, jnp.where(i == 0, j, steps - 1)))
    kept = pl.BlockSpec((width, tile), lambda i, j, side_ref: (0, jnp.where(i == 0, 0, j)))
    return pl.pallas_call(
        lambda *refs: late_back_kernel(seqs, block, *refs),
        name="late_back",
        out_shape=(
            outside((count, width, rows), BF16), jax.ShapeDtypeStruct((width, width), BF16), jax.ShapeDtypeStruct((width, width), BF16),
            jax.ShapeDtypeStruct((count, 8, width), F32),
        ),
        grid_spec=pltpu.PrefetchScalarGridSpec(
            num_scalar_prefetch=1,
            grid=(2, steps),
            in_specs=[
                flat, flat, pl.BlockSpec((tile,), lambda i, j, side_ref: (j,)), part, across, part,
                pl.BlockSpec((3, tile), lambda i, j, side_ref: (0, (1 + group(i, side_ref)) * steps + j)),
                pl.BlockSpec((width, rows), lambda i, j, side_ref: (0, 0)),
            ],
            out_specs=(part, given, kept, across),
        ),
        compiler_params=pltpu.CompilerParams(vmem_limit_bytes=20 << 20),
    )(side, conv, grad_long, skip, factors, edges, mixed, short_weight, turned)


def back_kernel(ga_ref, gb_ref, w_ref, tok_ref, resid_ref, gain_ref, bias_ref, out_ref, sums_ref):
    width = tok_ref.shape[1]
    turned = contract(w_ref[:, :width], ga_ref[0], ((1,), (0,)))
    for part in range(2):
        turned += contract(w_ref[:, (part + 1) * width : (part + 2) * width], gb_ref[part], ((1,), (0,)))
    q = turned.T
    gain = row(gain_ref)
    _, unit, inverse = norm_forward(tok_ref[...].astype(F32), gain, row(bias_ref))
    scaled = q * gain
    out_ref[...] = resid_ref[...] + inverse * (
        scaled
        - jnp.mean(scaled, axis=-1, keepdims=True)
        - unit * jnp.mean(scaled * unit, axis=-1, keepdims=True)
    )
    sums_ref[0:1] = jnp.sum(q * unit, axis=0, keepdims=True)
    sums_ref[1:2] = jnp.sum(q, axis=0, keepdims=True)
    sums_ref[2:8] = jnp.zeros((6, width), F32)


def back(mixed_early, mixed_late, w_in, tokens, grad_resid, gain, bias):
    return pl.pallas_call(
        back_kernel,
        name="back",
        out_shape=(
            jax.ShapeDtypeStruct(tokens.shape, F32), jax.ShapeDtypeStruct((8, tokens.shape[1]), F32),
        ),
        in_specs=[vmem_spec()] * 7,
        out_specs=(vmem_spec(), vmem_spec()),
        compiler_params=pltpu.CompilerParams(vmem_limit_bytes=26 << 20),
    )(mixed_early, mixed_late, w_in, tokens, grad_resid, gain, bias)


def transform_tables(block):
    spots = np.arange(block, dtype=np.float64)
    angle = np.pi / block * (spots[None, :] + 0.5) * spots[:, None]
    table = np.concatenate([np.cos(angle), -np.sin(angle)], axis=1)
    high = table.astype(np.float32).astype(jnp.bfloat16)
    low = (table - high.astype(np.float64)).astype(np.float32).astype(jnp.bfloat16)
    return np.stack([high, low])


def mm(left, right):
    return contract(left, right, ((1,), (0,)))


def spectrum(block, high, low):
    return mm(block, high) + mm(block, low)


def invert(spec, high, low):
    head = spec.astype(BF16)
    tail = (spec - head.astype(F32)).astype(BF16)
    back = lambda part, table: contract(part, table, ((1,), (1,)))
    return (back(head, high) + (back(tail, high) + back(head, low))) * (1.0 / high.shape[0])


def filter_spectra(filt_ref, high, low, g_ref, channels, blocks, length):
    sign = (1 - 2 * (lax.broadcasted_iota(jnp.int32, (1, length), 1) % 2)).astype(F32)
    before = None
    for lag in range(blocks):
        now = spectrum(filt_ref[:, lag * length : (lag + 1) * length], high, low)
        rows = slice(lag * channels, (lag + 1) * channels)
        if before is None:
            g_ref[rows, :] = now
        else:
            g_ref[rows, :length] = now[:, :length] - sign * before[:, length:]
            g_ref[rows, length:] = now[:, length:] + sign * before[:, :length]
        before = now


def conv_forward_kernel(
    channels, blocks, length, seqs,
    x_ref, filt_ref, table_ref, out_ref, s_ref, g_ref,
):
    high, low = table_ref[0], table_ref[1]
    filter_spectra(filt_ref, high, low, g_ref, channels, blocks, length)
    for q in range(seqs):
        s_ref[q] = spectrum(x_ref[:, q * length : (q + 1) * length], high, low)

    def tile(step, carry):
        row = pl.multiple_of(step * 8, 8)
        for lane in range(0, length, 128):
            re, im = slice(lane, lane + 128), slice(length + lane, length + lane + 128)
            for q in range(seqs):
                for i in reversed(range(blocks)):
                    acc_re = acc_im = None
                    for j in range(i + 1):
                        s_rows = pl.ds(j * channels + row, 8)
                        g_rows = pl.ds((i - j) * channels + row, 8)
                        sr, si = s_ref[q, s_rows, re], s_ref[q, s_rows, im]
                        gr, gi = g_ref[g_rows, re], g_ref[g_rows, im]
                        new_re = sr * gr - si * gi
                        new_im = sr * gi + si * gr
                        acc_re = new_re if acc_re is None else acc_re + new_re
                        acc_im = new_im if acc_im is None else acc_im + new_im
                    rows = pl.ds(i * channels + row, 8)
                    s_ref[q, rows, re] = acc_re
                    s_ref[q, rows, im] = acc_im
        return carry

    lax.fori_loop(0, channels // 8, tile, 0)
    for q in range(seqs):
        out_ref[:, q * length : (q + 1) * length] = invert(s_ref[q], high, low).astype(BF16)


def conv_backward_kernel(
    channels, blocks, length, seqs,
    x_ref, y_ref, filt_ref, table_ref, out_ref, gfilt_ref, s_ref, q_ref, g_ref, l_ref,
):
    high, low = table_ref[0], table_ref[1]
    filter_spectra(filt_ref, high, low, g_ref, channels, blocks, length)
    for q in range(seqs):
        s_ref[q] = spectrum(x_ref[:, q * length : (q + 1) * length], high, low)
        q_ref[q] = spectrum(y_ref[:, q * length : (q + 1) * length], high, low)

    def tile(step, carry):
        row = pl.multiple_of(step * 8, 8)
        for lane in range(0, length, 128):
            re, im = slice(lane, lane + 128), slice(length + lane, length + lane + 128)
            for d in range(blocks):
                acc_re = acc_im = None
                for q in range(seqs):
                    for j in range(blocks - d):
                        s_rows = pl.ds(j * channels + row, 8)
                        y_rows = pl.ds((j + d) * channels + row, 8)
                        sr, si = s_ref[q, s_rows, re], s_ref[q, s_rows, im]
                        yr, yi = q_ref[q, y_rows, re], q_ref[q, y_rows, im]
                        new_re = sr * yr + si * yi
                        new_im = sr * yi - si * yr
                        acc_re = new_re if acc_re is None else acc_re + new_re
                        acc_im = new_im if acc_im is None else acc_im + new_im
                rows = pl.ds(d * channels + row, 8)
                l_ref[rows, re] = acc_re
                l_ref[rows, im] = acc_im
            for q in range(seqs):
                for j in range(blocks):
                    acc_re = acc_im = None
                    for i in range(j, blocks):
                        y_rows = pl.ds(i * channels + row, 8)
                        g_rows = pl.ds((i - j) * channels + row, 8)
                        yr, yi = q_ref[q, y_rows, re], q_ref[q, y_rows, im]
                        gr, gi = g_ref[g_rows, re], g_ref[g_rows, im]
                        new_re = gr * yr + gi * yi
                        new_im = gr * yi - gi * yr
                        acc_re = new_re if acc_re is None else acc_re + new_re
                        acc_im = new_im if acc_im is None else acc_im + new_im
                    rows = pl.ds(j * channels + row, 8)
                    q_ref[q, rows, re] = acc_re
                    q_ref[q, rows, im] = acc_im
        return carry

    lax.fori_loop(0, channels // 8, tile, 0)
    for q in range(seqs):
        out_ref[:, q * length : (q + 1) * length] = invert(q_ref[q], high, low).astype(BF16)
    sign = (1 - 2 * (lax.broadcasted_iota(jnp.int32, (1, length), 1) % 2)).astype(F32)
    for d in range(blocks):
        rows = slice(d * channels, (d + 1) * channels)
        real, imag = l_ref[rows, :length], l_ref[rows, length:]
        if d + 1 < blocks:
            after = slice((d + 1) * channels, (d + 2) * channels)
            real = real + sign * l_ref[after, length:]
            imag = imag - sign * l_ref[after, :length]
        both = jnp.concatenate([real, imag], axis=1)
        gfilt_ref[:, d * length : (d + 1) * length] = invert(both, high, low)


def conv_forward(x, filt, table, channels, blocks, length, seqs):
    rows = blocks * channels
    kernel = lambda *refs: conv_forward_kernel(channels, blocks, length, seqs, *refs)
    return pl.pallas_call(
        kernel,
        name="conv_forward",
        out_shape=jax.ShapeDtypeStruct((rows, seqs * length), BF16),
        in_specs=[vmem_spec()] * 3,
        out_specs=vmem_spec(),
        scratch_shapes=[
            pltpu.VMEM((seqs, rows, 2 * length), F32),
            pltpu.VMEM((rows, 2 * length), F32),
        ],
        compiler_params=pltpu.CompilerParams(vmem_limit_bytes=18 << 20),
    )(x, filt, table)


def conv_backward(x, y, filt, table, channels, blocks, length, seqs):
    rows = blocks * channels
    kernel = lambda *refs: conv_backward_kernel(channels, blocks, length, seqs, *refs)
    return pl.pallas_call(
        kernel,
        name="conv_backward",
        out_shape=(
            outside((rows, seqs * length), BF16),
            jax.ShapeDtypeStruct((channels, blocks * length), F32),
        ),
        in_specs=[vmem_spec()] * 4,
        out_specs=(vmem_spec(), vmem_spec()),
        scratch_shapes=[
            pltpu.VMEM((seqs, rows, 2 * length), F32),
            pltpu.VMEM((seqs, rows, 2 * length), F32),
            pltpu.VMEM((rows, 2 * length), F32),
            pltpu.VMEM((rows, 2 * length), F32),
        ],
        compiler_params=pltpu.CompilerParams(vmem_limit_bytes=26 << 20),
    )(x, y, filt, table)


def shifted(block, axis, distance):
    count = lax.axis_size(axis)
    route = [(i - distance, i) for i in range(count) if 0 <= i - distance < count]
    return lax.ppermute(block, axis, route)


def axis_bits(axis):
    size, bits, bit = lax.axis_size(axis), [], 1
    while bit < size:
        bits.append((axis, bit))
        bit *= 2
    return bits


def exchange(value, step):
    axis, bit = step
    return lax.ppermute(value, axis, [(i, i ^ bit) for i in range(lax.axis_size(axis))])


def side_of(step):
    axis, bit = step
    return (lax.axis_index(axis) // bit) % 2


class Route(list):
    twin = None
    lanes = 0


def total_of(kept, other):
    return (kept.astype(F32) + other.astype(F32)).astype(BF16)


def fold_kernel(count, ways, merged, _, *refs):
    ins, outs = refs[: 2 * ways * count], refs[2 * ways * count :]
    for i in range(ways * count):
        value = total_of(ins[2 * i][...], ins[2 * i + 1][...])
        if merged and i < ways:
            outs[i][:, : value.shape[1]] = value
        elif merged:
            outs[i - ways][:, outs[i - ways].shape[1] - value.shape[1] :] = value
        else:
            outs[i][...] = value


def fold(pairs, steps, merged=False):
    count = len(pairs)
    ways = 2 if steps else 1
    sizes = [pair[0].shape[0] // ways for pair in pairs]
    if any(size % 16 for size in sizes):
        sums = [total_of(*pair) for pair in pairs]
        if steps is None:
            return sums
        cut = lambda value, place, size: lax.dynamic_slice_in_dim(value, place * size, size, 0)
        pieces = [
            (cut(value, 1 - side_of(step), size), cut(value, side_of(step), size))
            for value, step, size in zip(sums, steps, sizes)
        ]
        if merged:
            return [tuple(jnp.concatenate(parts, axis=1) for parts in zip(*pieces))]
        return pieces
    most = max(sizes)
    grid = most // 64 if most >= 192 and all(size == most for size in sizes) and most % 64 == 0 else 1
    shapes, in_specs, args = [], [], []
    for i, ((kept, other), size) in enumerate(zip(pairs, sizes)):
        lanes = kept.shape[1]
        for way in range(ways):
            if steps:
                place = lambda j, sides_ref, i=i, way=way: (
                    (1 - sides_ref[i] if way == 0 else sides_ref[i]) * grid + j, 0
                )
            else:
                place = lambda j, sides_ref: (j, 0)
            in_specs += [pl.BlockSpec((size // grid, lanes), place)] * 2
            args += [kept, other]
            make = outside if most >= 384 and lanes >= 1536 else jax.ShapeDtypeStruct
            shapes.append(make((size, lanes), BF16))
    if merged:
        lanes = sum(pair[0].shape[1] for pair in pairs)
        shapes = [jax.ShapeDtypeStruct((most, lanes), BF16)] * ways
    out_specs = [
        pl.BlockSpec((shape.shape[0] // grid, shape.shape[1]), lambda j, sides_ref: (j, 0)) for shape in shapes
    ]
    sides = jnp.stack([side_of(step) for step in steps] if steps else [jnp.zeros((), jnp.int32)])
    outs = pl.pallas_call(
        lambda *refs: fold_kernel(count, ways, merged, *refs),
        name="fold",
        out_shape=shapes,
        grid_spec=pltpu.PrefetchScalarGridSpec(
            num_scalar_prefetch=1, grid=(grid,), in_specs=in_specs, out_specs=out_specs
        ),
        compiler_params=pltpu.CompilerParams(vmem_limit_bytes=(58 if most >= 192 and lanes >= 1536 else 14) << 20),
    )(sides.astype(jnp.int32), *args)
    return list(zip(outs[::2], outs[1::2])) if steps else list(outs)


def join_kernel(count, lanes, sides_ref, *refs):
    for i in range(count):
        for ref, place in ((refs[2 * i], sides_ref[i]), (refs[2 * i + 1], 1 - sides_ref[i])):
            if lanes:
                refs[2 * count][place] = ref[:, :lanes]
                refs[2 * count + 1][place] = ref[:, lanes:]
            else:
                refs[2 * count + i][place] = ref[...]


def join(pairs, steps, lanes=0):
    count = len(pairs)
    if any(pair[0].shape[0] % 16 for pair in pairs):
        outs = []
        for (own, other), step in zip(pairs, steps):
            first = side_of(step) == 0
            outs.append(jnp.concatenate([jnp.where(first, own, other), jnp.where(first, other, own)]))
        return [outs[0][:, :lanes], outs[0][:, lanes:]] if lanes else outs
    sides = jnp.stack([side_of(step) for step in steps]).astype(jnp.int32)
    in_specs, shapes = [], []
    for own, _ in pairs:
        rows, width = own.shape
        in_specs += [pl.BlockSpec((rows, width), lambda j: (0, 0))] * 2
        for part in (lanes, width - lanes) if lanes else (width,):
            shapes.append(jax.ShapeDtypeStruct((2, rows, part), BF16))
    outs = pl.pallas_call(
        lambda *refs: join_kernel(count, lanes, *refs),
        name="join",
        grid=(1,),
        out_shape=shapes,
        in_specs=[smem_spec()] + in_specs,
        out_specs=[pl.BlockSpec(shape.shape, lambda j: (0, 0, 0)) for shape in shapes],
        compiler_params=pltpu.CompilerParams(vmem_limit_bytes=8 << 20),
    )(sides, *[value for pair in pairs for value in pair])
    return [out.reshape(-1, out.shape[2]) for out in outs]


def quarters_do(row_side, lane_side, refs, put):
    for place, ref in enumerate(refs):
        h = row_side if place % 2 == 0 else 1 - row_side
        for l in range(2):

            @pl.when((lane_side == l) if place < 2 else (lane_side != l))
            def _():
                put(h, l, ref[...].astype(F32))


def widen_kernel(stacked, sides_ref, *refs):
    pieces, out_ref = refs[:4], refs[4]
    lanes = pieces[0].shape[1]

    def put(h, l, value):
        if stacked:
            width = lanes // out_ref.shape[1]
            for k in range(out_ref.shape[1]):
                out_ref[l, k, h] = value[:, k * width : (k + 1) * width]
        else:
            out_ref[h, :, l * lanes : (l + 1) * lanes] = value

    quarters_do(sides_ref[0], sides_ref[1], pieces, put)


def widen(sides, pieces, width, stacked):
    rows, lanes = pieces[0].shape
    tile = 64
    if stacked:
        count = lanes // width
        shape = (2, count, 2, rows, width)
        out = pl.BlockSpec((2, count, 2, tile, width), lambda j: (0, 0, 0, j, 0))
    else:
        shape = (2, rows, 2 * lanes)
        out = pl.BlockSpec((2, tile, 2 * lanes), lambda j: (0, j, 0))
    wide = pl.pallas_call(
        lambda *refs: widen_kernel(stacked, *refs),
        name="widen",
        grid=(rows // tile,),
        out_shape=jax.ShapeDtypeStruct(shape, F32),
        in_specs=[smem_spec()] + [pl.BlockSpec((tile, lanes), lambda j: (j, 0))] * 4,
        out_specs=out,
        compiler_params=pltpu.CompilerParams(vmem_limit_bytes=14 << 20),
    )(sides, *pieces)
    return wide.reshape(-1, shape[-1])


def widen_late_kernel(sides_ref, *refs):
    s_pieces, t_pieces, (in_ref, out_ref, last_ref) = refs[:4], refs[4:8], refs[8:]
    width = out_ref.shape[2]

    def put_s(h, l, value):
        in_ref[h, :, (l + 1) * width : (l + 2) * width] = value

    def put_t(h, l, value):
        if l == 0:
            in_ref[h, :, :width] = value[:, :width]
        else:
            out_ref[h] = value[:, :width]
        last_ref[l, h] = value[:, width:]

    quarters_do(sides_ref[0], sides_ref[1], s_pieces, put_s)
    quarters_do(sides_ref[2], sides_ref[1], t_pieces, put_t)


def widen_late(sides, s_pieces, t_pieces):
    rows, width = s_pieces[0].shape
    more = t_pieces[0].shape[1] - width
    tile = 64
    part = lambda lanes: pl.BlockSpec((tile, lanes), lambda j: (j, 0))
    both = lambda lanes: pl.BlockSpec((2, tile, lanes), lambda j: (0, j, 0))
    grad_in, grad_out, last = pl.pallas_call(
        widen_late_kernel,
        name="widen_late",
        grid=(rows // tile,),
        out_shape=(
            jax.ShapeDtypeStruct((2, rows, 3 * width), F32), jax.ShapeDtypeStruct((2, rows, width), F32),
            jax.ShapeDtypeStruct((2, 2, rows, more), F32),
        ),
        in_specs=[smem_spec()] + [part(width)] * 4 + [part(width + more)] * 4,
        out_specs=(
            both(3 * width), both(width), pl.BlockSpec((2, 2, tile, more), lambda j: (0, 0, j, 0)),
        ),
        compiler_params=pltpu.CompilerParams(vmem_limit_bytes=14 << 20),
    )(sides, *s_pieces, *t_pieces)
    return grad_in.reshape(-1, 3 * width), grad_out.reshape(-1, width), last.reshape(2, -1, more)


def unpack_kernel(features, hidden, wide, last_ref, net_ref, *refs):
    (g1, b1, b_in, sw, sb, fw1, fb1, fw2, fb2, fw3, skip, b_out, g2, b2, mb1, mb2) = refs
    width = g1.shape[0]
    fw3[...] = last_ref[0].T[:hidden]
    fw1[...] = net_ref[0, :features, :hidden]
    fb1[...] = net_ref[0, features : features + 1, :hidden].reshape(hidden)
    fw2[...] = net_ref[0, features + 1 : features + 1 + hidden, :hidden]
    fb2[...] = net_ref[0, features + 1 + hidden : features + 2 + hidden, :hidden].reshape(hidden)
    pieces = width // 128

    def put(ref, place, lane, row=None):
        for k in range(pieces):
            at = 128 + place * pieces + k
            value = net_ref[0, at : at + 1, :]
            lanes = slice(lane + k * 128, lane + (k + 1) * 128)
            if row is None:
                ref[lanes] = value.reshape(128)
            else:
                ref[row : row + 1, lanes] = value

    for place, ref in enumerate((skip, b_out, g2, b2, mb2)):
        put(ref, place, 0)
    for k in range(wide):
        put(mb1, 5 + k, k * width)
    put(g1, 5 + wide, 0)
    put(b1, 6 + wide, 0)
    for group in range(3):
        first = 7 + wide + 5 * group
        put(b_in, first, group * width)
        put(sb, first + 1, group * width)
        for tap in range(3):
            put(sw, first + 2 + tap, group * width, tap)


def unpack(last, features, hidden, wide, width):
    flat = lambda size: jax.ShapeDtypeStruct((size,), F32)
    grid = lambda *shape: jax.ShapeDtypeStruct(shape, F32)
    part = lambda h: pl.BlockSpec((1, width, 128), lambda i: (h, 0, 0))
    shapes = (
        flat(width), flat(width), flat(3 * width), grid(3, 3 * width), flat(3 * width),
        grid(features, hidden), flat(hidden), grid(hidden, hidden), flat(hidden), grid(hidden, width),
        flat(width), flat(width), flat(width), flat(width), flat(wide * width), flat(width),
    )
    whole = lambda shape: pl.BlockSpec(shape, lambda i: (0,) * len(shape))
    return pl.pallas_call(
        lambda *refs: unpack_kernel(features, hidden, wide, *refs),
        name="unpack",
        grid=(1,),
        out_shape=shapes,
        in_specs=[part(0), part(1)],
        out_specs=[whole(shape.shape) for shape in shapes],
        compiler_params=pltpu.CompilerParams(vmem_limit_bytes=14 << 20),
    )(last, last)


def orders():
    bits = axis_bits("bucket") + axis_bits("seq")
    first, rest = bits[0], bits[1:]
    if len(rest) == 4:
        y, x, near, far = rest
        return Route([first, y, x, near]), Route([first, x, y, near]), far
    return Route([first] + rest), Route([first] + rest[1:] + rest[:1]), None


def work_order(last):
    if last == 3:
        return [
            ("s", 3), ("p", -3), ("s", 4), ("p", -2), ("meet", 0), ("s", -3), ("s", -2), ("last", 0),
            ("wide", 0),
        ]
    order = [("p", index) for index in range(5, last + 2)]
    order += [("s", index) for index in range(2, last + 2)]
    order += [("p", -index) for index in range(last, 1, -1)]
    order += [("s", -index) for index in range(last, 1, -1)]
    return order + [("last", 0), ("wide", 0)]


def held(value, *awaited):
    return lax.optimization_barrier((value,) + awaited)[0]


def local(
    tokens, cotangent, lengths, decay_rate, norm1_gain, norm1_bias, w_in, b_in,
    short_weight, short_bias, filter_w1, filter_b1, filter_w2, filter_b2, filter_w3,
    skip_gain, w_out, b_out, norm2_gain, norm2_bias, mlp_w1, mlp_b1, mlp_w2, mlp_b2,
):
    seqs, block, width = tokens.shape[1:]
    rows = seqs * block
    blocks = lax.axis_size("seq")
    full = blocks * block
    channels = width // blocks
    position = lax.axis_index("seq")
    place = position.reshape(1).astype(jnp.int32)
    table = jnp.asarray(transform_tables(block))
    flat_tokens = tokens.reshape(rows, width)

    edge_tokens = shifted(tokens[0, :, block - 2 :, :], "seq", 1).reshape(2 * seqs, width)
    normed, edge_normed, mixed_late, factors, signal = front(
        place, flat_tokens, edge_tokens, norm1_gain, norm1_bias, b_in, short_bias, short_weight, w_in,
        seqs, block,
    )
    signal_all = lax.all_to_all(signal, "seq", 0, 0, tiled=True)
    turned, mixed_early, gate_out = gate_part(
        place, normed, edge_normed, b_in, short_bias, short_weight, w_in, seqs, block
    )

    own = position * channels
    rates = lax.dynamic_slice_in_dim(decay_rate, own, channels)
    weight_three = lax.dynamic_slice_in_dim(filter_w3.astype(F32), own, channels, axis=1)

    second_weight = filter_w2.astype(F32)
    feats, hidden_one, slope_one, hidden_two, slope_two = filter_layers(
        filter_w1.astype(F32), filter_b1.astype(F32), second_weight, filter_b2.astype(F32), full
    )
    times = lax.broadcasted_iota(jnp.int32, (1, full), 1).astype(F32) / full
    window = jnp.exp(-times * rates[:, None]) + 0.05
    filt = (precise("hd,hp->dp", weight_three, hidden_two) * window).astype(BF16)
    long_all = conv_forward(signal_all, filt, table, channels, blocks, block, seqs)
    conv_long = lax.all_to_all(long_all, "seq", 0, 0, tiled=True)

    order_p, order_q, far = orders()
    core = order_p[0]
    side = side_of(core).reshape(1).astype(jnp.int32)
    (
        output, grad_resid, grad_long, grad_gate, given_p, kept_p, given_q, kept_q, grad_w_out, sums,
    ) = middle(
        side, place, lengths.reshape(seqs), conv_long, signal, gate_out, skip_gain, flat_tokens,
        cotangent.reshape(rows, width), w_out, b_out, norm2_gain, norm2_bias, mlp_b2, mlp_b1[None], mlp_w1,
        mlp_w2, seqs, block,
    )
    grad_long_all = lax.all_to_all(grad_long, "seq", 0, 0, tiled=True)

    def turn(streams, index, *awaited):
        pairs, after = [], []
        for (given, kept), order in streams:
            other = exchange(given, order[index])
            if awaited:
                kept, awaited = held(kept, *awaited), ()
            pairs.append((kept, other))
            after.append(order[index + 1] if index + 1 < len(order) else None)
        routes = [order for _, order in streams]
        merged = len(streams) == 2 and after[0] is not None and after[0] == after[1]
        parts = fold(pairs, after if after[0] else None, merged)
        if merged:
            route = Route(routes[0])
            route.twin, route.lanes = routes[1], pairs[0][0].shape[1]
            routes = [route]
        return list(zip(parts, routes))

    def turn_back(streams, index, *awaited):
        pairs = []
        for part, order in streams:
            other = exchange(part, order[index])
            if awaited:
                part, awaited = held(part, *awaited), ()
            pairs.append((part, other))
        routes = [order for _, order in streams]
        route = routes[0]
        lanes = route.lanes if route.twin and route[index - 1] != route.twin[index - 1] else 0
        parts = join(pairs, [order[index] for order in routes], lanes)
        return list(zip(parts, [Route(route), route.twin] if lanes else routes))

    def meet(streams, *awaited):
        pairs = []
        for part, _ in streams:
            other = exchange(part, far)
            if awaited:
                part, awaited = held(part, *awaited), ()
            pairs.append((part, other))
        return list(zip(fold(pairs, None), [route for _, route in streams]))

    def quarters(streams, *awaited):
        others = [exchange(part, order[1]) for part, order in streams]
        if awaited:
            others = lax.optimization_barrier(tuple(others) + awaited)[: len(others)]
        return [
            [part, other, exchange(part, core), exchange(other, core)]
            for (part, _), other in zip(streams, others)
        ]

    def first_of(streams):
        value = streams[0][0]
        return value[0] if isinstance(value, tuple) else value

    last = len(order_p) - 1
    parts = turn([((given_p, kept_p), order_p), ((given_q, kept_q), order_q)], 0)
    grad_long_all = held(grad_long_all, first_of(parts))
    back_all, grad_filter = conv_backward(
        signal_all, grad_long_all, filt, table, channels, blocks, block, seqs
    )
    back_conv = lax.all_to_all(back_all, "seq", 0, 0, tiled=True)
    last_w3, net = filter_back(
        own.reshape(1).astype(jnp.int32), grad_filter, window, feats, hidden_one, slope_one, hidden_two,
        slope_two, second_weight, weight_three, width,
    )
    features, hidden = filter_w1.shape
    heads = features + hidden + 2
    parts = turn(parts, 1, last_w3)
    back_conv = held(back_conv, first_of(parts))
    edges = all_edges(back_conv, grad_long, skip_gain, factors, grad_gate, seqs, block)
    edges = shifted(edges, "seq", -1)
    late_grads, given_s, kept_s, sums_late = late_back(
        side, back_conv, grad_long, skip_gain, factors, edges, mixed_late, short_weight, turned, seqs,
        block,
    )
    parts = turn(parts, 2, late_grads)
    stream_s = turn([((held(given_s, first_of(parts)), kept_s), order_p)], 0)
    gate_grads, w_in_early, sums_early = early_back(
        held(grad_gate, first_of(stream_s)), edges, mixed_early, short_weight, turned, seqs, block
    )
    parts = turn(parts, 3, gate_grads)
    tokens_grad, sums_norm = back(
        gate_grads, held(late_grads, first_of(parts)), w_in, flat_tokens, grad_resid, norm1_gain,
        norm1_bias,
    )
    if far:
        stream_s = turn(stream_s, 1, tokens_grad)
    wide = sums.shape[0] - 8
    shorts = jnp.concatenate([sums_early, sums_late], axis=0)
    small = jnp.concatenate(
        [sums[:5], sums[8:], sums_norm[:2], shorts[:, :5].reshape(-1, width)], axis=0
    )
    more = small.size // 128
    net = jnp.concatenate(
        [net, small.reshape(more, 128), jnp.zeros((width - 128 - more, 128), F32)], axis=0
    )
    part_t = choose(side, held(w_in_early, first_of(stream_s)), last_w3, grad_w_out, net)
    stream_t = turn([(part_t, order_q)], 0)
    token = first_of(stream_t)
    if far:
        parts = meet(parts, token)
        stream_t = turn(stream_t, 1, first_of(parts))
        token = first_of(stream_t)
    state = {"p": parts, "s": stream_s + stream_t}
    for piece, index in work_order(last):
        if piece == "last":
            last_p, last_q = quarters(state["p"], token)
            token = last_q[1]
        elif piece == "meet":
            state["s"] = meet(state["s"], token)
            token = first_of(state["s"])
        elif piece == "wide":
            sides_of = lambda order: jnp.stack([side_of(order[1]), side_of(core)]).astype(jnp.int32)
            last_p[0] = held(last_p[0], token)
            sum_w1 = widen(sides_of(order_p), last_p, width, False)
            last_q[0] = held(last_q[0], sum_w1)
            sum_w2 = widen(sides_of(order_q), last_q, width, True)
            token = sum_w2
        elif index > 0:
            state[piece] = turn(state[piece], index - 1, token)
            token = first_of(state[piece])
        else:
            state[piece] = turn_back(state[piece], -index, token)
            token = first_of(state[piece])
    last_s, last_t = quarters(state["s"], token)
    sides = jnp.stack([side_of(order_p[1]), side_of(core), side_of(order_q[1])]).astype(jnp.int32)
    sum_w_in, sum_w_out, sum_last = widen_late(sides, last_s, last_t)
    small = unpack(sum_last, features, hidden, wide, width)
    return (
        output.reshape(tokens.shape), tokens_grad.reshape(tokens.shape), *small[:2], sum_w_in, *small[2:11],
        sum_w_out, *small[11:14], sum_w1, small[14], sum_w2, small[15],
    )


def solution(mesh):
    split = P("bucket", None, "seq", None)
    in_specs = (split, split, P("bucket", None)) + (P(),) * 21
    out_specs = (split, split) + (P(),) * 20
    return jax.shard_map(local, mesh=mesh, in_specs=in_specs, out_specs=out_specs, check_vma=False)
```

```python
import math

import jax
import jax.numpy as jnp
import numpy as np
from jax import lax
from jax.experimental import pallas as pl
from jax.experimental.pallas import tpu as pltpu
from jax.sharding import PartitionSpec as P

HIGH = lax.Precision.HIGHEST
EPSILON = 1e-05
F32 = jnp.float32
BF16 = jnp.bfloat16


def norm_forward(values, gain, bias):
    center = values - jnp.mean(values, axis=-1, keepdims=True)
    inverse = lax.rsqrt(jnp.mean(center * center, axis=-1, keepdims=True) + EPSILON)
    unit = center * inverse
    return (unit * gain + bias, unit, inverse)


def precise(formula, left, right):
    return jnp.einsum(formula, left, right, precision=HIGH, preferred_element_type=F32)


def position_features(length):
    steps = lax.broadcasted_iota(jnp.int32, (1, length), 1).astype(F32)
    bands = 0.0001 + lax.broadcasted_iota(jnp.int32, (16, 1), 0).astype(F32) * (
        (15.0 - 0.0001) / 15.0
    )
    phase = 2.0 * math.pi / length * steps * bands
    return jnp.concatenate([steps / length, jnp.cos(phase), -jnp.sin(phase)], axis=0)


def filter_layers(weight_one, bias_one, weight_two, bias_two, length):
    feats = position_features(length)
    first = precise("eh,ep->hp", weight_one, feats) + bias_one[:, None]
    hidden = jnp.sin(first)
    second = precise("hk,hp->kp", weight_two, hidden) + bias_two[:, None]
    return feats, hidden, jnp.cos(first), jnp.sin(second), jnp.cos(second)


def exact(left, right, dims):
    return lax.dot_general(
        left, right, (dims, ((), ())), precision=HIGH, preferred_element_type=F32
    )


def filter_back_kernel(
    channels, own_ref, grad_ref, window_ref, feats_ref, h1_ref, c1_ref, h2_ref, c2_ref, w2_ref, w3_ref,
    last_ref, net_ref,
):
    hidden = h1_ref.shape[0]
    features = feats_ref.shape[0]
    shaped = grad_ref[...] * window_ref[...]
    ones = jnp.ones((8, shaped.shape[1]), F32)
    last_ref[...] = jnp.zeros_like(last_ref)
    net_ref[...] = jnp.zeros_like(net_ref)
    rows = pl.ds(pl.multiple_of(own_ref[0], 16), channels)
    grad_w3 = exact(shaped, h2_ref[...], ((1,), (1,)))
    last_ref[rows, :] = jnp.concatenate([grad_w3, jnp.zeros_like(grad_w3)], axis=1).astype(BF16)
    second = exact(w3_ref[...], shaped, ((1,), (0,))) * c2_ref[...]
    first = exact(w2_ref[...], second, ((1,), (0,))) * c1_ref[...]
    place = 0
    for value in (
        exact(feats_ref[...], first, ((1,), (1,))), exact(ones, first, ((1,), (1,)))[:1],
        exact(h1_ref[...], second, ((1,), (1,))), exact(ones, second, ((1,), (1,)))[:1],
    ):
        net_ref[place : place + value.shape[0], :hidden] = value
        place += value.shape[0]


def filter_back(own, grad, window, feats, h1, c1, h2, c2, w2, w3, width):
    channels = grad.shape[0]
    return pl.pallas_call(
        lambda *refs: filter_back_kernel(channels, *refs),
        name="filter_back",
        out_shape=(
            jax.ShapeDtypeStruct((width, 128), BF16), jax.ShapeDtypeStruct((128, 128), F32),
        ),
        in_specs=[smem_spec()] + [vmem_spec()] * 9,
        out_specs=(vmem_spec(), vmem_spec()),
        compiler_params=pltpu.CompilerParams(vmem_limit_bytes=14 << 20),
    )(own, grad, window, feats, h1, c1, h2, c2, w2, w3)


def choose_kernel(side_ref, early_ref, last_ref, out_ref, net_ref, given_ref, kept_ref):
    low_side = side_ref[0] == 0
    width = early_ref.shape[1]
    parts = (
        (early_ref[...], out_ref[...], slice(0, width)),
        (last_ref[...], net_ref[...].astype(BF16), slice(width, width + 128)),
    )
    for low_half, high_half, lanes in parts:
        given_ref[:, lanes] = jnp.where(low_side, high_half, low_half)
        kept_ref[:, lanes] = jnp.where(low_side, low_half, high_half)


def choose(side, early, last, grad_out, net):
    width = early.shape[0]
    tile = 128
    part = lambda lanes: pl.BlockSpec((tile, lanes), lambda j: (j, 0))
    shape = jax.ShapeDtypeStruct((width, width + 128), BF16)
    return tuple(
        pl.pallas_call(
            choose_kernel,
            name="choose",
            grid=(width // tile,),
            out_shape=(shape, shape),
            in_specs=[smem_spec(), part(width), part(128), part(width), part(128)],
            out_specs=(part(width + 128), part(width + 128)),
            compiler_params=pltpu.CompilerParams(vmem_limit_bytes=8 << 20),
        )(side, early, last, grad_out, net)
    )


def outside(shape, dtype):
    return pltpu.HBM(shape, dtype)


def vmem_spec():
    return pl.BlockSpec(memory_space=pltpu.VMEM)


def smem_spec():
    return pl.BlockSpec(memory_space=pltpu.SMEM)


def contract(left, right, dims):
    return lax.dot_general(left, right, (dims, ((), ())), preferred_element_type=F32)


def lane_sums(parts):
    ones = jnp.ones((8, 128), BF16)
    heads, tails = [], []
    for part in parts:
        folded = part[:, :128]
        for lane in range(128, part.shape[1], 128):
            folded = folded + part[:, lane : lane + 128]
        head = folded.astype(BF16)
        heads.append(head)
        tails.append((folded - head.astype(F32)).astype(BF16))
    both = contract(ones, jnp.concatenate(heads + tails, axis=0), ((1,), (1,)))
    count = parts[0].shape[0]
    half = count * len(parts)
    return [
        both[:1, k * count : (k + 1) * count] + both[:1, half + k * count : half + (k + 1) * count]
        for k in range(len(parts))
    ]


def columns(*rows):
    parts = [row[...].astype(F32).reshape(-1, row.shape[-1]) for row in rows]
    count = sum(part.shape[0] for part in parts)
    parts.append(jnp.zeros((8 - count, parts[0].shape[1]), F32))
    return jnp.concatenate(parts, axis=0).T


def row(ref):
    return ref[...].astype(F32).reshape(1, ref.shape[0])


def short_filter(mixed, edge, cols, seqs, block):
    spots = lax.broadcasted_iota(jnp.int32, (1, block), 1)
    pieces = []
    for q in range(seqs):
        now = mixed[:, q * block : (q + 1) * block]
        near, far = edge[:, 2 * q + 1 : 2 * q + 2], edge[:, 2 * q : 2 * q + 1]
        once = jnp.where(spots == 0, near, pltpu.roll(now, 1, 1))
        twice = jnp.where(spots == 0, far, jnp.where(spots == 1, near, pltpu.roll(now, 2, 1)))
        pieces.append(
            cols[:, 2:3] * now + cols[:, 3:4] * once + cols[:, 4:5] * twice + cols[:, 1:2]
        )
    return jnp.concatenate(pieces, axis=1)


def project(weight, normed, edge_normed, cols, inside, seqs, block):
    mixed = (contract(weight, normed, ((0,), (1,))) + cols[:, 0:1]).astype(BF16)
    edge = (contract(weight, edge_normed, ((0,), (1,))) + cols[:, 0:1]).astype(BF16)
    edge = edge.astype(F32) * inside
    return mixed, short_filter(mixed.astype(F32), edge, cols, seqs, block)


def front_kernel(
    seqs, block, first_ref, tok_ref, edge_ref, gain_ref, bias_ref, bb_ref, bc_ref, sbb_ref, sbc_ref, swb_ref,
    swc_ref, wb_ref, wc_ref, normed_ref, edge_normed_ref, mixed_ref, factor_ref, signal_ref,
):
    @pl.when(pl.program_id(0) == 0)
    def _():
        gain, bias = row(gain_ref), row(bias_ref)
        normed_ref[...] = norm_forward(tok_ref[...].astype(F32), gain, bias)[0].astype(BF16)
        edge_normed_ref[...] = norm_forward(edge_ref[...].astype(F32), gain, bias)[0].astype(BF16)

    normed, edge_normed = normed_ref[...], edge_normed_ref[...]
    inside = (first_ref[0] > 0).astype(F32)
    mixed_ref[0], gate_in = project(
        wb_ref[...], normed, edge_normed, columns(bb_ref, sbb_ref, swb_ref), inside, seqs, block
    )
    mixed_ref[1], values = project(
        wc_ref[...], normed, edge_normed, columns(bc_ref, sbc_ref, swc_ref), inside, seqs, block
    )
    factor_ref[0] = values
    factor_ref[1] = gate_in
    signal_ref[...] = (gate_in * values).astype(BF16)


def front(position, tokens, edge, gain, bias, b_in, short_bias, short_weight, w_in, seqs, block):
    rows, width = tokens.shape
    tile = 256
    steps = width // tile
    fixed = lambda shape: pl.BlockSpec(shape, lambda j: (0,) * len(shape))
    weight = lambda part: pl.BlockSpec((width, tile), lambda j: (0, part * steps + j))
    flat = lambda part: pl.BlockSpec((tile,), lambda j: (part * steps + j,))
    taps = lambda part: pl.BlockSpec((3, tile), lambda j: (0, part * steps + j))
    both = pl.BlockSpec((2, tile, rows), lambda j: (0, j, 0))
    return pl.pallas_call(
        lambda *refs: front_kernel(seqs, block, *refs),
        name="front",
        grid=(steps,),
        out_shape=(
            jax.ShapeDtypeStruct((rows, width), BF16), jax.ShapeDtypeStruct(edge.shape, BF16),
            jax.ShapeDtypeStruct((2, width, rows), BF16), jax.ShapeDtypeStruct((2, width, rows), F32),
            jax.ShapeDtypeStruct((width, rows), BF16),
        ),
        in_specs=[
            smem_spec(), fixed((rows, width)), fixed(edge.shape), fixed(gain.shape), fixed(bias.shape),
            flat(1), flat(2), flat(1), flat(2), taps(1), taps(2), weight(1), weight(2),
        ],
        out_specs=(
            fixed((rows, width)), fixed(edge.shape), both, both,
            pl.BlockSpec((tile, rows), lambda j: (j, 0)),
        ),
        compiler_params=pltpu.CompilerParams(vmem_limit_bytes=58 << 20),
    )(
        position, tokens, edge, gain, bias, b_in, b_in, short_bias, short_bias, short_weight,
        short_weight, w_in, w_in,
    )


def gate_kernel(
    seqs, block, first_ref, normed_ref, edge_normed_ref, b_ref, sb_ref, sw_ref, w_ref, turned_ref,
    mixed_ref, gate_ref,
):
    normed = normed_ref[...]

    @pl.when(pl.program_id(0) == 0)
    def _():
        turned_ref[...] = normed.T

    inside = (first_ref[0] > 0).astype(F32)
    mixed_ref[...], gate_ref[...] = project(
        w_ref[...], normed, edge_normed_ref[...], columns(b_ref, sb_ref, sw_ref), inside, seqs, block
    )


def gate_part(position, normed, edge_normed, b_in, short_bias, short_weight, w_in, seqs, block):
    rows, width = normed.shape
    tile = 256
    fixed = lambda shape: pl.BlockSpec(shape, lambda j: (0,) * len(shape))
    flat = pl.BlockSpec((tile,), lambda j: (j,))
    out = pl.BlockSpec((tile, rows), lambda j: (j, 0))
    return pl.pallas_call(
        lambda *refs: gate_kernel(seqs, block, *refs),
        name="gate_part",
        grid=(width // tile,),
        out_shape=(
            jax.ShapeDtypeStruct((width, rows), BF16), jax.ShapeDtypeStruct((width, rows), BF16),
            jax.ShapeDtypeStruct((width, rows), F32),
        ),
        in_specs=[
            smem_spec(), fixed((rows, width)), fixed(edge_normed.shape), flat, flat,
            pl.BlockSpec((3, tile), lambda j: (0, j)), pl.BlockSpec((width, tile), lambda j: (0, j)),
        ],
        out_specs=(fixed((width, rows)), out, out),
        compiler_params=pltpu.CompilerParams(vmem_limit_bytes=58 << 20),
    )(position, normed, edge_normed, b_in, short_bias, short_weight, w_in)


def row_mask(position, lengths_ref, seqs, block):
    spots = position * block + lax.broadcasted_iota(jnp.int32, (block, 1), 0)
    return jnp.concatenate([(spots < lengths_ref[q]).astype(F32) for q in range(seqs)], axis=0)


def middle_kernel(
    seqs, block, side_ref, position_ref, lengths_ref, conv_ref, signal_ref, gate_ref, skip_ref, tok_ref,
    cot_ref, w_out_ref, b_out_ref, gain_ref, bias_ref, b2_ref, b1_ref, w1_ref, w2_ref,
    out_ref, resid_grad_ref, long_ref, gate_grad_ref, given1_ref, kept1_ref, given2_ref, kept2_ref,
    gwo_ref, sums_ref,
    gated_ref, n2_ref, n2t_ref, unit_ref, inv_ref, final_ref, gf_ref, q_ref, lout_ref,
):
    step = pl.program_id(0)
    last = pl.num_programs(0) - 1
    b_out, gain, bias, b2 = row(b_out_ref), row(gain_ref), row(bias_ref), row(b2_ref)

    @pl.when(step == 0)
    def _():
        skip = columns(skip_ref)[:, 0:1]
        long_out = conv_ref[...].astype(F32) + signal_ref[...].astype(F32) * skip
        lout_ref[...] = long_out
        gated = (long_out * gate_ref[...]).astype(BF16)
        gated_ref[...] = gated
        branch = contract(gated, w_out_ref[...], ((0,), (0,))) + b_out
        resid = tok_ref[...].astype(F32) + branch
        normed, unit, inverse = norm_forward(resid, gain, bias)
        n2_ref[...] = normed.astype(BF16)
        n2t_ref[...] = normed.astype(BF16).T
        unit_ref[...] = unit
        inv_ref[...] = jnp.broadcast_to(inverse, inv_ref.shape)
        final_ref[...] = resid + b2
        valid = row_mask(position_ref[0], lengths_ref, seqs, block)
        gf_ref[...] = (cot_ref[...].astype(F32) * valid).astype(BF16)
        q_ref[...] = jnp.zeros_like(q_ref)

    w1, w2, gf = w1_ref[...], w2_ref[...], gf_ref[...]
    pre = contract(n2_ref[...], w1, ((1,), (0,))) + b1_ref[...].astype(F32)
    grad_active = contract(gf, w2, ((1,), (1,)))
    cumulative, slope = normal_terms(pre)
    active = (pre * cumulative).astype(BF16)
    grad_pre = grad_active * slope
    grad_low = grad_pre.astype(BF16)
    final_ref[...] += contract(active, w2, ((1,), (0,)))
    q_ref[...] += contract(grad_low, w1, ((1,), (1,)))
    grad_two = contract(active, gf, ((0,), (0,))).astype(BF16)
    grad_one = contract(n2t_ref[...], grad_low, ((1,), (0,))).astype(BF16)

    @pl.when(step <= last // 2)
    def _():
        given1_ref[...] = grad_one
        given2_ref[...] = grad_two

    @pl.when(step > last // 2)
    def _():
        kept1_ref[...] = grad_one
        kept2_ref[...] = grad_two

    half = pl.num_programs(0) // 2
    chunk = jnp.where(step < half, half * (1 - side_ref[0]) + step, half * side_ref[0] + step - half)
    sums_ref[pl.ds(8 + chunk, 1)] = jnp.sum(grad_low.astype(F32), axis=0, keepdims=True)

    @pl.when(step == last)
    def _():
        valid = row_mask(position_ref[0], lengths_ref, seqs, block)
        out_ref[...] = (final_ref[...] * valid).astype(BF16)
        grad_final = gf_ref[...].astype(F32)
        q, unit = q_ref[...], unit_ref[...]
        scaled = q * gain
        grad_resid = grad_final + inv_ref[:, 0:1] * (
            scaled
            - jnp.mean(scaled, axis=-1, keepdims=True)
            - unit * jnp.mean(scaled * unit, axis=-1, keepdims=True)
        )
        resid_grad_ref[...] = grad_resid
        grad_branch = grad_resid.astype(BF16)
        grad_gated = contract(w_out_ref[...], grad_branch, ((1,), (1,)))
        grad_long = (grad_gated * gate_ref[...]).astype(BF16)
        long_ref[...] = grad_long
        gate_grad_ref[...] = grad_gated * lout_ref[...]
        gwo_ref[...] = contract(gated_ref[...], grad_branch, ((1,), (0,))).astype(BF16)
        skip_sum = lane_sums([grad_long.astype(F32) * signal_ref[...].astype(F32)])[0]
        total = lambda part: jnp.sum(part, axis=0, keepdims=True)
        sums_ref[0:1] = skip_sum
        sums_ref[1:2] = total(grad_branch.astype(F32))
        sums_ref[2:3] = total(q * unit)
        sums_ref[3:4] = total(q)
        sums_ref[4:5] = total(grad_final)
        sums_ref[5:8] = jnp.zeros((3, sums_ref.shape[1]), F32)


def normal_terms(pre):
    cumulative = 0.5 * (1.0 + lax.erf(pre * (1.0 / math.sqrt(2.0))))
    density = jnp.exp(-0.5 * pre * pre) * (1.0 / math.sqrt(2.0 * math.pi))
    return cumulative, cumulative + pre * density


def middle(
    side, position, lengths, conv, signal, gate, skip, tokens, cotangent, w_out, b_out, gain, bias, b2, b1, w1,
    w2, seqs, block,
):
    count, width = tokens.shape
    hidden = w1.shape[1]
    chunk = width
    steps = hidden // chunk
    half = steps // 2
    once = lambda shape: pl.BlockSpec(
        shape, lambda j, side_ref: (0,) * len(shape), pipeline_mode=pl.Buffered(1)
    )

    def which(j, side_ref):
        side = side_ref[0]
        return jnp.where(j < half, half * (1 - side) + j, half * side + j - half)

    across = lambda height: pl.BlockSpec((height, chunk), lambda j, side_ref: (0, which(j, side_ref)))
    given = pl.BlockSpec((width, chunk), lambda j, side_ref: (0, jnp.minimum(j, half - 1)))
    kept = pl.BlockSpec((width, chunk), lambda j, side_ref: (0, jnp.maximum(j - half, 0)))
    wide, tall = (count, width), (width, count)
    shape = jax.ShapeDtypeStruct
    scratch = pltpu.VMEM
    part = shape((width, half * chunk), BF16)
    return pl.pallas_call(
        lambda *refs: middle_kernel(seqs, block, *refs),
        name="middle",
        out_shape=(
            shape(wide, BF16), shape(wide, F32), shape(tall, BF16), shape(tall, F32),
            part, part, part, part, shape((width, width), BF16),
            shape((8 + steps, width), F32),
        ),
        grid_spec=pltpu.PrefetchScalarGridSpec(
            num_scalar_prefetch=1,
            grid=(steps,),
            in_specs=[
                smem_spec(), smem_spec(), once(tall), once(tall), once(tall), once(skip.shape),
                once(wide), once(wide), once((width, width)), once(b_out.shape), once(gain.shape),
                once(bias.shape), once(b2.shape),
                across(1), across(width),
                pl.BlockSpec((chunk, width), lambda j, side_ref: (which(j, side_ref), 0)),
            ],
            out_specs=(
                once(wide), once(wide), once(tall), once(tall), given, kept, given, kept,
                once((width, width)), once((8 + steps, width)),
            ),
            scratch_shapes=[
                scratch(tall, BF16), scratch(wide, BF16), scratch(tall, BF16), scratch(wide, F32),
                scratch((count, 128), F32), scratch(wide, F32), scratch(wide, BF16), scratch(wide, F32),
                scratch(tall, F32),
            ],
        ),
        compiler_params=pltpu.CompilerParams(vmem_limit_bytes=58 << 20),
    )(
        side, position, lengths, conv, signal, gate, skip, tokens, cotangent, w_out, b_out, gain, bias, b2, b1,
        w1, w2,
    )


def first_spots(heads):
    lanes = lax.broadcasted_iota(jnp.int32, (1, 128), 1)
    edge = jnp.zeros(heads[0].shape, F32)
    for q, head in enumerate(heads):
        head = pltpu.roll(head, 2 * q, 1) if q else head
        edge = jnp.where((lanes >= 2 * q) & (lanes < 2 * q + 2), head, edge)
    return edge.T[:8]


def edges_kernel(seqs, skip_ref, *refs):
    skip = columns(skip_ref)[:, 0:1]
    out_ref = refs[-1]
    signals = [
        refs[4 * q][...].astype(F32) + refs[4 * q + 1][...].astype(F32) * skip for q in range(seqs)
    ]
    for part in range(2):
        out_ref[part] = first_spots([signals[q] * refs[4 * q + 2][part] for q in range(seqs)])
    out_ref[2] = first_spots([refs[4 * q + 3][...] for q in range(seqs)])


def all_edges(conv, grad_long, skip, factors, gate, seqs, block):
    width = conv.shape[0]
    specs, args = [], []
    for q in range(seqs):
        place = q * block // 128
        flat = pl.BlockSpec((width, 128), lambda i, place=place: (0, place))
        specs += [flat, flat, pl.BlockSpec((2, width, 128), lambda i, place=place: (0, 0, place)), flat]
        args += [conv, grad_long, factors, gate]
    return pl.pallas_call(
        lambda *refs: edges_kernel(seqs, *refs),
        name="all_edges",
        grid=(1,),
        out_shape=jax.ShapeDtypeStruct((3, 8, width), F32),
        in_specs=[pl.BlockSpec(skip.shape, lambda i: (0,))] + specs,
        out_specs=pl.BlockSpec((3, 8, width), lambda i: (0, 0, 0)),
        compiler_params=pltpu.CompilerParams(vmem_limit_bytes=14 << 20),
    )(skip, *args)


def short_back_body(grad, edge_ref, mixed_ref, sw_ref, turned_ref, out_ref, sums_ref, seqs, block):
    taps = columns(sw_ref)
    edge = edge_ref[0].T
    spots = lax.broadcasted_iota(jnp.int32, (1, block), 1)
    mixed = mixed_ref[0].astype(F32)
    once, twice = [], []
    for q in range(seqs):
        now = grad[:, q * block : (q + 1) * block]
        near, far = edge[:, 2 * q : 2 * q + 1], edge[:, 2 * q + 1 : 2 * q + 2]
        end = block - 1
        once.append(jnp.where(spots == end, near, pltpu.roll(now, block - 1, 1)))
        twice.append(
            jnp.where(
                spots == end, far, jnp.where(spots == end - 1, near, pltpu.roll(now, block - 2, 1))
            )
        )
    once, twice = jnp.concatenate(once, axis=1), jnp.concatenate(twice, axis=1)
    low = (taps[:, 0:1] * grad + taps[:, 1:2] * once + taps[:, 2:3] * twice).astype(BF16)
    out_ref[0] = low
    sums_ref[0, 0:1] = contract(jnp.ones((8, low.shape[1]), BF16), low, ((1,), (1,)))[:1]
    for place, total in enumerate(lane_sums([grad, mixed * grad, mixed * once, mixed * twice])):
        sums_ref[0, place + 1 : place + 2] = total
    sums_ref[0, 5:8] = jnp.zeros((3, sums_ref.shape[2]), F32)
    return contract(turned_ref[...], low, ((1,), (1,))).astype(BF16)


def early_back_kernel(
    seqs, block, grad_ref, edge_ref, mixed_ref, sw_ref, turned_ref, out_ref, gw_ref, sums_ref
):
    gw_ref[...] = short_back_body(
        grad_ref[...], edge_ref, mixed_ref, sw_ref, turned_ref, out_ref, sums_ref, seqs, block
    )


def early_back(grad, edges, mixed, short_weight, turned, seqs, block):
    width, rows = grad.shape
    tile = 256
    flat = pl.BlockSpec((tile, rows), lambda j: (j, 0))
    part = pl.BlockSpec((1, tile, rows), lambda j: (0, j, 0))
    across = lambda height: pl.BlockSpec((1, height, tile), lambda j: (0, 0, j))
    return pl.pallas_call(
        lambda *refs: early_back_kernel(seqs, block, *refs),
        name="early_back",
        grid=(width // tile,),
        out_shape=(
            outside((1, width, rows), BF16), jax.ShapeDtypeStruct((width, width), BF16),
            jax.ShapeDtypeStruct((1, 8, width), F32),
        ),
        in_specs=[
            flat, pl.BlockSpec((1, 8, tile), lambda j: (2, 0, j)), part, pl.BlockSpec((3, tile), lambda j: (0, j)),
            pl.BlockSpec((width, rows), lambda j: (0, 0)),
        ],
        out_specs=(part, pl.BlockSpec((width, tile), lambda j: (0, j)), across(8)),
        compiler_params=pltpu.CompilerParams(vmem_limit_bytes=18 << 20),
    )(grad, edges, mixed[None], short_weight, turned)


def late_back_kernel(
    seqs, block, side_ref, conv_ref, long_ref, skip_ref, factor_ref, edge_ref, mixed_ref, sw_ref, turned_ref,
    out_ref, given_ref, kept_ref, sums_ref,
):
    skip = columns(skip_ref)[:, 0:1]
    grad = (conv_ref[...].astype(F32) + long_ref[...].astype(F32) * skip) * factor_ref[0]
    weight = short_back_body(
        grad, edge_ref, mixed_ref, sw_ref, turned_ref, out_ref, sums_ref, seqs, block
    )

    @pl.when(pl.program_id(0) == 0)
    def _():
        given_ref[...] = weight

    @pl.when(pl.program_id(0) == 1)
    def _():
        kept_ref[...] = weight


def late_back(side, conv, grad_long, skip, factors, edges, mixed, short_weight, turned, seqs, block):
    count, width, rows = mixed.shape
    tile = 256
    steps = width // tile
    group = lambda i, side_ref: jnp.where(i == 0, 1 - side_ref[0], side_ref[0])
    part = pl.BlockSpec((1, tile, rows), lambda i, j, side_ref: (group(i, side_ref), j, 0))
    flat = pl.BlockSpec((tile, rows), lambda i, j, side_ref: (j, 0))
    across = pl.BlockSpec((1, 8, tile), lambda i, j, side_ref: (group(i, side_ref), 0, j))
    given = pl.BlockSpec((width, tile), lambda i, j, side_ref: (0, jnp.where(i == 0, j, steps - 1)))
    kept = pl.BlockSpec((width, tile), lambda i, j, side_ref: (0, jnp.where(i == 0, 0, j)))
    return pl.pallas_call(
        lambda *refs: late_back_kernel(seqs, block, *refs),
        name="late_back",
        out_shape=(
            outside((count, width, rows), BF16), jax.ShapeDtypeStruct((width, width), BF16), jax.ShapeDtypeStruct((width, width), BF16),
            jax.ShapeDtypeStruct((count, 8, width), F32),
        ),
        grid_spec=pltpu.PrefetchScalarGridSpec(
            num_scalar_prefetch=1,
            grid=(2, steps),
            in_specs=[
                flat, flat, pl.BlockSpec((tile,), lambda i, j, side_ref: (j,)), part, across, part,
                pl.BlockSpec((3, tile), lambda i, j, side_ref: (0, (1 + group(i, side_ref)) * steps + j)),
                pl.BlockSpec((width, rows), lambda i, j, side_ref: (0, 0)),
            ],
            out_specs=(part, given, kept, across),
        ),
        compiler_params=pltpu.CompilerParams(vmem_limit_bytes=20 << 20),
    )(side, conv, grad_long, skip, factors, edges, mixed, short_weight, turned)


def back_kernel(ga_ref, gb_ref, w_ref, tok_ref, resid_ref, gain_ref, bias_ref, out_ref, sums_ref):
    width = tok_ref.shape[1]
    turned = contract(w_ref[:, :width], ga_ref[0], ((1,), (0,)))
    for part in range(2):
        turned += contract(w_ref[:, (part + 1) * width : (part + 2) * width], gb_ref[part], ((1,), (0,)))
    q = turned.T
    gain = row(gain_ref)
    _, unit, inverse = norm_forward(tok_ref[...].astype(F32), gain, row(bias_ref))
    scaled = q * gain
    out_ref[...] = resid_ref[...] + inverse * (
        scaled
        - jnp.mean(scaled, axis=-1, keepdims=True)
        - unit * jnp.mean(scaled * unit, axis=-1, keepdims=True)
    )
    sums_ref[0:1] = jnp.sum(q * unit, axis=0, keepdims=True)
    sums_ref[1:2] = jnp.sum(q, axis=0, keepdims=True)
    sums_ref[2:8] = jnp.zeros((6, width), F32)


def back(mixed_early, mixed_late, w_in, tokens, grad_resid, gain, bias):
    return pl.pallas_call(
        back_kernel,
        name="back",
        out_shape=(
            jax.ShapeDtypeStruct(tokens.shape, F32), jax.ShapeDtypeStruct((8, tokens.shape[1]), F32),
        ),
        in_specs=[vmem_spec()] * 7,
        out_specs=(vmem_spec(), vmem_spec()),
        compiler_params=pltpu.CompilerParams(vmem_limit_bytes=26 << 20),
    )(mixed_early, mixed_late, w_in, tokens, grad_resid, gain, bias)


def transform_tables(block):
    spots = np.arange(block, dtype=np.float64)
    angle = np.pi / block * (spots[None, :] + 0.5) * spots[:, None]
    table = np.concatenate([np.cos(angle), -np.sin(angle)], axis=1)
    high = table.astype(np.float32).astype(jnp.bfloat16)
    low = (table - high.astype(np.float64)).astype(np.float32).astype(jnp.bfloat16)
    return np.stack([high, low])


def mm(left, right):
    return contract(left, right, ((1,), (0,)))


def spectrum(block, high, low):
    return mm(block, high) + mm(block, low)


def invert(spec, high, low):
    head = spec.astype(BF16)
    tail = (spec - head.astype(F32)).astype(BF16)
    back = lambda part, table: contract(part, table, ((1,), (1,)))
    return (back(head, high) + (back(tail, high) + back(head, low))) * (1.0 / high.shape[0])


def filter_spectra(filt_ref, high, low, g_ref, channels, blocks, length):
    sign = (1 - 2 * (lax.broadcasted_iota(jnp.int32, (1, length), 1) % 2)).astype(F32)
    before = None
    for lag in range(blocks):
        now = spectrum(filt_ref[:, lag * length : (lag + 1) * length], high, low)
        rows = slice(lag * channels, (lag + 1) * channels)
        if before is None:
            g_ref[rows, :] = now
        else:
            g_ref[rows, :length] = now[:, :length] - sign * before[:, length:]
            g_ref[rows, length:] = now[:, length:] + sign * before[:, :length]
        before = now


def conv_forward_kernel(
    channels, blocks, length, seqs,
    x_ref, filt_ref, table_ref, out_ref, s_ref, g_ref,
):
    high, low = table_ref[0], table_ref[1]
    filter_spectra(filt_ref, high, low, g_ref, channels, blocks, length)
    for q in range(seqs):
        s_ref[q] = spectrum(x_ref[:, q * length : (q + 1) * length], high, low)

    def tile(step, carry):
        row = pl.multiple_of(step * 8, 8)
        for lane in range(0, length, 128):
            re, im = slice(lane, lane + 128), slice(length + lane, length + lane + 128)
            for q in range(seqs):
                for i in reversed(range(blocks)):
                    acc_re = acc_im = None
                    for j in range(i + 1):
                        s_rows = pl.ds(j * channels + row, 8)
                        g_rows = pl.ds((i - j) * channels + row, 8)
                        sr, si = s_ref[q, s_rows, re], s_ref[q, s_rows, im]
                        gr, gi = g_ref[g_rows, re], g_ref[g_rows, im]
                        new_re = sr * gr - si * gi
                        new_im = sr * gi + si * gr
                        acc_re = new_re if acc_re is None else acc_re + new_re
                        acc_im = new_im if acc_im is None else acc_im + new_im
                    rows = pl.ds(i * channels + row, 8)
                    s_ref[q, rows, re] = acc_re
                    s_ref[q, rows, im] = acc_im
        return carry

    lax.fori_loop(0, channels // 8, tile, 0)
    for q in range(seqs):
        out_ref[:, q * length : (q + 1) * length] = invert(s_ref[q], high, low).astype(BF16)


def conv_backward_kernel(
    channels, blocks, length, seqs,
    x_ref, y_ref, filt_ref, table_ref, out_ref, gfilt_ref, s_ref, q_ref, g_ref, l_ref,
):
    high, low = table_ref[0], table_ref[1]
    filter_spectra(filt_ref, high, low, g_ref, channels, blocks, length)
    for q in range(seqs):
        s_ref[q] = spectrum(x_ref[:, q * length : (q + 1) * length], high, low)
        q_ref[q] = spectrum(y_ref[:, q * length : (q + 1) * length], high, low)

    def tile(step, carry):
        row = pl.multiple_of(step * 8, 8)
        for lane in range(0, length, 128):
            re, im = slice(lane, lane + 128), slice(length + lane, length + lane + 128)
            for d in range(blocks):
                acc_re = acc_im = None
                for q in range(seqs):
                    for j in range(blocks - d):
                        s_rows = pl.ds(j * channels + row, 8)
                        y_rows = pl.ds((j + d) * channels + row, 8)
                        sr, si = s_ref[q, s_rows, re], s_ref[q, s_rows, im]
                        yr, yi = q_ref[q, y_rows, re], q_ref[q, y_rows, im]
                        new_re = sr * yr + si * yi
                        new_im = sr * yi - si * yr
                        acc_re = new_re if acc_re is None else acc_re + new_re
                        acc_im = new_im if acc_im is None else acc_im + new_im
                rows = pl.ds(d * channels + row, 8)
                l_ref[rows, re] = acc_re
                l_ref[rows, im] = acc_im
            for q in range(seqs):
                for j in range(blocks):
                    acc_re = acc_im = None
                    for i in range(j, blocks):
                        y_rows = pl.ds(i * channels + row, 8)
                        g_rows = pl.ds((i - j) * channels + row, 8)
                        yr, yi = q_ref[q, y_rows, re], q_ref[q, y_rows, im]
                        gr, gi = g_ref[g_rows, re], g_ref[g_rows, im]
                        new_re = gr * yr + gi * yi
                        new_im = gr * yi - gi * yr
                        acc_re = new_re if acc_re is None else acc_re + new_re
                        acc_im = new_im if acc_im is None else acc_im + new_im
                    rows = pl.ds(j * channels + row, 8)
                    q_ref[q, rows, re] = acc_re
                    q_ref[q, rows, im] = acc_im
        return carry

    lax.fori_loop(0, channels // 8, tile, 0)
    for q in range(seqs):
        out_ref[:, q * length : (q + 1) * length] = invert(q_ref[q], high, low).astype(BF16)
    sign = (1 - 2 * (lax.broadcasted_iota(jnp.int32, (1, length), 1) % 2)).astype(F32)
    for d in range(blocks):
        rows = slice(d * channels, (d + 1) * channels)
        real, imag = l_ref[rows, :length], l_ref[rows, length:]
        if d + 1 < blocks:
            after = slice((d + 1) * channels, (d + 2) * channels)
            real = real + sign * l_ref[after, length:]
            imag = imag - sign * l_ref[after, :length]
        both = jnp.concatenate([real, imag], axis=1)
        gfilt_ref[:, d * length : (d + 1) * length] = invert(both, high, low)


def conv_forward(x, filt, table, channels, blocks, length, seqs):
    rows = blocks * channels
    kernel = lambda *refs: conv_forward_kernel(channels, blocks, length, seqs, *refs)
    return pl.pallas_call(
        kernel,
        name="conv_forward",
        out_shape=jax.ShapeDtypeStruct((rows, seqs * length), BF16),
        in_specs=[vmem_spec()] * 3,
        out_specs=vmem_spec(),
        scratch_shapes=[
            pltpu.VMEM((seqs, rows, 2 * length), F32),
            pltpu.VMEM((rows, 2 * length), F32),
        ],
        compiler_params=pltpu.CompilerParams(vmem_limit_bytes=18 << 20),
    )(x, filt, table)


def conv_backward(x, y, filt, table, channels, blocks, length, seqs):
    rows = blocks * channels
    kernel = lambda *refs: conv_backward_kernel(channels, blocks, length, seqs, *refs)
    return pl.pallas_call(
        kernel,
        name="conv_backward",
        out_shape=(
            outside((rows, seqs * length), BF16),
            jax.ShapeDtypeStruct((channels, blocks * length), F32),
        ),
        in_specs=[vmem_spec()] * 4,
        out_specs=(vmem_spec(), vmem_spec()),
        scratch_shapes=[
            pltpu.VMEM((seqs, rows, 2 * length), F32),
            pltpu.VMEM((seqs, rows, 2 * length), F32),
            pltpu.VMEM((rows, 2 * length), F32),
            pltpu.VMEM((rows, 2 * length), F32),
        ],
        compiler_params=pltpu.CompilerParams(vmem_limit_bytes=26 << 20),
    )(x, y, filt, table)


def shifted(block, axis, distance):
    count = lax.axis_size(axis)
    route = [(i - distance, i) for i in range(count) if 0 <= i - distance < count]
    return lax.ppermute(block, axis, route)


def axis_bits(axis):
    size, bits, bit = lax.axis_size(axis), [], 1
    while bit < size:
        bits.append((axis, bit))
        bit *= 2
    return bits


def exchange(value, step):
    axis, bit = step
    return lax.ppermute(value, axis, [(i, i ^ bit) for i in range(lax.axis_size(axis))])


def side_of(step):
    axis, bit = step
    return (lax.axis_index(axis) // bit) % 2


class Route(list):
    twin = None
    lanes = 0


def total_of(kept, other):
    return (kept.astype(F32) + other.astype(F32)).astype(BF16)


def fold_kernel(count, ways, merged, _, *refs):
    ins, outs = refs[: 2 * ways * count], refs[2 * ways * count :]
    for i in range(ways * count):
        value = total_of(ins[2 * i][...], ins[2 * i + 1][...])
        if merged and i < ways:
            outs[i][:, : value.shape[1]] = value
        elif merged:
            outs[i - ways][:, outs[i - ways].shape[1] - value.shape[1] :] = value
        else:
            outs[i][...] = value


def fold(pairs, steps, merged=False):
    count = len(pairs)
    ways = 2 if steps else 1
    sizes = [pair[0].shape[0] // ways for pair in pairs]
    if any(size % 16 for size in sizes):
        sums = [total_of(*pair) for pair in pairs]
        if steps is None:
            return sums
        cut = lambda value, place, size: lax.dynamic_slice_in_dim(value, place * size, size, 0)
        pieces = [
            (cut(value, 1 - side_of(step), size), cut(value, side_of(step), size))
            for value, step, size in zip(sums, steps, sizes)
        ]
        if merged:
            return [tuple(jnp.concatenate(parts, axis=1) for parts in zip(*pieces))]
        return pieces
    most = max(sizes)
    grid = most // 64 if most >= 192 and all(size == most for size in sizes) and most % 64 == 0 else 1
    shapes, in_specs, args = [], [], []
    for i, ((kept, other), size) in enumerate(zip(pairs, sizes)):
        lanes = kept.shape[1]
        for way in range(ways):
            if steps:
                place = lambda j, sides_ref, i=i, way=way: (
                    (1 - sides_ref[i] if way == 0 else sides_ref[i]) * grid + j, 0
                )
            else:
                place = lambda j, sides_ref: (j, 0)
            in_specs += [pl.BlockSpec((size // grid, lanes), place)] * 2
            args += [kept, other]
            make = outside if most >= 384 and lanes >= 1536 else jax.ShapeDtypeStruct
            shapes.append(make((size, lanes), BF16))
    if merged:
        lanes = sum(pair[0].shape[1] for pair in pairs)
        shapes = [jax.ShapeDtypeStruct((most, lanes), BF16)] * ways
    out_specs = [
        pl.BlockSpec((shape.shape[0] // grid, shape.shape[1]), lambda j, sides_ref: (j, 0)) for shape in shapes
    ]
    sides = jnp.stack([side_of(step) for step in steps] if steps else [jnp.zeros((), jnp.int32)])
    outs = pl.pallas_call(
        lambda *refs: fold_kernel(count, ways, merged, *refs),
        name="fold",
        out_shape=shapes,
        grid_spec=pltpu.PrefetchScalarGridSpec(
            num_scalar_prefetch=1, grid=(grid,), in_specs=in_specs, out_specs=out_specs
        ),
        compiler_params=pltpu.CompilerParams(vmem_limit_bytes=(58 if most >= 192 and lanes >= 1536 else 14) << 20),
    )(sides.astype(jnp.int32), *args)
    return list(zip(outs[::2], outs[1::2])) if steps else list(outs)


def join_kernel(count, lanes, sides_ref, *refs):
    for i in range(count):
        for ref, place in ((refs[2 * i], sides_ref[i]), (refs[2 * i + 1], 1 - sides_ref[i])):
            if lanes:
                refs[2 * count][place] = ref[:, :lanes]
                refs[2 * count + 1][place] = ref[:, lanes:]
            else:
                refs[2 * count + i][place] = ref[...]


def join(pairs, steps, lanes=0):
    count = len(pairs)
    if any(pair[0].shape[0] % 16 for pair in pairs):
        outs = []
        for (own, other), step in zip(pairs, steps):
            first = side_of(step) == 0
            outs.append(jnp.concatenate([jnp.where(first, own, other), jnp.where(first, other, own)]))
        return [outs[0][:, :lanes], outs[0][:, lanes:]] if lanes else outs
    sides = jnp.stack([side_of(step) for step in steps]).astype(jnp.int32)
    in_specs, shapes = [], []
    for own, _ in pairs:
        rows, width = own.shape
        in_specs += [pl.BlockSpec((rows, width), lambda j: (0, 0))] * 2
        for part in (lanes, width - lanes) if lanes else (width,):
            shapes.append(jax.ShapeDtypeStruct((2, rows, part), BF16))
    outs = pl.pallas_call(
        lambda *refs: join_kernel(count, lanes, *refs),
        name="join",
        grid=(1,),
        out_shape=shapes,
        in_specs=[smem_spec()] + in_specs,
        out_specs=[pl.BlockSpec(shape.shape, lambda j: (0, 0, 0)) for shape in shapes],
        compiler_params=pltpu.CompilerParams(vmem_limit_bytes=8 << 20),
    )(sides, *[value for pair in pairs for value in pair])
    return [out.reshape(-1, out.shape[2]) for out in outs]


def quarters_do(row_side, lane_side, refs, put):
    for place, ref in enumerate(refs):
        h = row_side if place % 2 == 0 else 1 - row_side
        for l in range(2):

            @pl.when((lane_side == l) if place < 2 else (lane_side != l))
            def _():
                put(h, l, ref[...].astype(F32))


def widen_kernel(stacked, sides_ref, *refs):
    pieces, out_ref = refs[:4], refs[4]
    lanes = pieces[0].shape[1]

    def put(h, l, value):
        if stacked:
            width = lanes // out_ref.shape[1]
            for k in range(out_ref.shape[1]):
                out_ref[l, k, h] = value[:, k * width : (k + 1) * width]
        else:
            out_ref[h, :, l * lanes : (l + 1) * lanes] = value

    quarters_do(sides_ref[0], sides_ref[1], pieces, put)


def widen(sides, pieces, width, stacked):
    rows, lanes = pieces[0].shape
    tile = 64
    if stacked:
        count = lanes // width
        shape = (2, count, 2, rows, width)
        out = pl.BlockSpec((2, count, 2, tile, width), lambda j: (0, 0, 0, j, 0))
    else:
        shape = (2, rows, 2 * lanes)
        out = pl.BlockSpec((2, tile, 2 * lanes), lambda j: (0, j, 0))
    wide = pl.pallas_call(
        lambda *refs: widen_kernel(stacked, *refs),
        name="widen",
        grid=(rows // tile,),
        out_shape=jax.ShapeDtypeStruct(shape, F32),
        in_specs=[smem_spec()] + [pl.BlockSpec((tile, lanes), lambda j: (j, 0))] * 4,
        out_specs=out,
        compiler_params=pltpu.CompilerParams(vmem_limit_bytes=14 << 20),
    )(sides, *pieces)
    return wide.reshape(-1, shape[-1])


def widen_late_kernel(sides_ref, *refs):
    s_pieces, t_pieces, (in_ref, out_ref, last_ref) = refs[:4], refs[4:8], refs[8:]
    width = out_ref.shape[2]

    def put_s(h, l, value):
        in_ref[h, :, (l + 1) * width : (l + 2) * width] = value

    def put_t(h, l, value):
        if l == 0:
            in_ref[h, :, :width] = value[:, :width]
        else:
            out_ref[h] = value[:, :width]
        last_ref[l, h] = value[:, width:]

    quarters_do(sides_ref[0], sides_ref[1], s_pieces, put_s)
    quarters_do(sides_ref[2], sides_ref[1], t_pieces, put_t)


def widen_late(sides, s_pieces, t_pieces):
    rows, width = s_pieces[0].shape
    more = t_pieces[0].shape[1] - width
    tile = 64
    part = lambda lanes: pl.BlockSpec((tile, lanes), lambda j: (j, 0))
    both = lambda lanes: pl.BlockSpec((2, tile, lanes), lambda j: (0, j, 0))
    grad_in, grad_out, last = pl.pallas_call(
        widen_late_kernel,
        name="widen_late",
        grid=(rows // tile,),
        out_shape=(
            jax.ShapeDtypeStruct((2, rows, 3 * width), F32), jax.ShapeDtypeStruct((2, rows, width), F32),
            jax.ShapeDtypeStruct((2, 2, rows, more), F32),
        ),
        in_specs=[smem_spec()] + [part(width)] * 4 + [part(width + more)] * 4,
        out_specs=(
            both(3 * width), both(width), pl.BlockSpec((2, 2, tile, more), lambda j: (0, 0, j, 0)),
        ),
        compiler_params=pltpu.CompilerParams(vmem_limit_bytes=14 << 20),
    )(sides, *s_pieces, *t_pieces)
    return grad_in.reshape(-1, 3 * width), grad_out.reshape(-1, width), last.reshape(2, -1, more)


def unpack_kernel(features, hidden, wide, last_ref, net_ref, *refs):
    (g1, b1, b_in, sw, sb, fw1, fb1, fw2, fb2, fw3, skip, b_out, g2, b2, mb1, mb2) = refs
    width = g1.shape[0]
    fw3[...] = last_ref[0].T[:hidden]
    fw1[...] = net_ref[0, :features, :hidden]
    fb1[...] = net_ref[0, features : features + 1, :hidden].reshape(hidden)
    fw2[...] = net_ref[0, features + 1 : features + 1 + hidden, :hidden]
    fb2[...] = net_ref[0, features + 1 + hidden : features + 2 + hidden, :hidden].reshape(hidden)
    pieces = width // 128

    def put(ref, place, lane, row=None):
        for k in range(pieces):
            at = 128 + place * pieces + k
            value = net_ref[0, at : at + 1, :]
            lanes = slice(lane + k * 128, lane + (k + 1) * 128)
            if row is None:
                ref[lanes] = value.reshape(128)
            else:
                ref[row : row + 1, lanes] = value

    for place, ref in enumerate((skip, b_out, g2, b2, mb2)):
        put(ref, place, 0)
    for k in range(wide):
        put(mb1, 5 + k, k * width)
    put(g1, 5 + wide, 0)
    put(b1, 6 + wide, 0)
    for group in range(3):
        first = 7 + wide + 5 * group
        put(b_in, first, group * width)
        put(sb, first + 1, group * width)
        for tap in range(3):
            put(sw, first + 2 + tap, group * width, tap)


def unpack(last, features, hidden, wide, width):
    flat = lambda size: jax.ShapeDtypeStruct((size,), F32)
    grid = lambda *shape: jax.ShapeDtypeStruct(shape, F32)
    part = lambda h: pl.BlockSpec((1, width, 128), lambda i: (h, 0, 0))
    shapes = (
        flat(width), flat(width), flat(3 * width), grid(3, 3 * width), flat(3 * width),
        grid(features, hidden), flat(hidden), grid(hidden, hidden), flat(hidden), grid(hidden, width),
        flat(width), flat(width), flat(width), flat(width), flat(wide * width), flat(width),
    )
    whole = lambda shape: pl.BlockSpec(shape, lambda i: (0,) * len(shape))
    return pl.pallas_call(
        lambda *refs: unpack_kernel(features, hidden, wide, *refs),
        name="unpack",
        grid=(1,),
        out_shape=shapes,
        in_specs=[part(0), part(1)],
        out_specs=[whole(shape.shape) for shape in shapes],
        compiler_params=pltpu.CompilerParams(vmem_limit_bytes=14 << 20),
    )(last, last)


def orders():
    bits = axis_bits("bucket") + axis_bits("seq")
    first, rest = bits[0], bits[1:]
    if len(rest) == 4:
        y, x, near, far = rest
        return Route([first, y, x, near]), Route([first, x, y, near]), far
    return Route([first] + rest), Route([first] + rest[1:] + rest[:1]), None


def work_order(last):
    if last == 3:
        return [
            ("s", 3), ("p", -3), ("s", 4), ("p", -2), ("meet", 0), ("s", -3), ("s", -2), ("last", 0),
            ("wide", 0),
        ]
    order = [("p", index) for index in range(5, last + 2)]
    order += [("s", index) for index in range(2, last + 2)]
    order += [("p", -index) for index in range(last, 1, -1)]
    order += [("s", -index) for index in range(last, 1, -1)]
    return order + [("last", 0), ("wide", 0)]


def held(value, *awaited):
    return lax.optimization_barrier((value,) + awaited)[0]


def local(
    tokens, cotangent, lengths, decay_rate, norm1_gain, norm1_bias, w_in, b_in,
    short_weight, short_bias, filter_w1, filter_b1, filter_w2, filter_b2, filter_w3,
    skip_gain, w_out, b_out, norm2_gain, norm2_bias, mlp_w1, mlp_b1, mlp_w2, mlp_b2,
):
    seqs, block, width = tokens.shape[1:]
    rows = seqs * block
    blocks = lax.axis_size("seq")
    full = blocks * block
    channels = width // blocks
    position = lax.axis_index("seq")
    place = position.reshape(1).astype(jnp.int32)
    table = jnp.asarray(transform_tables(block))
    flat_tokens = tokens.reshape(rows, width)

    edge_tokens = shifted(tokens[0, :, block - 2 :, :], "seq", 1).reshape(2 * seqs, width)
    normed, edge_normed, mixed_late, factors, signal = front(
        place, flat_tokens, edge_tokens, norm1_gain, norm1_bias, b_in, short_bias, short_weight, w_in,
        seqs, block,
    )
    signal_all = lax.all_to_all(signal, "seq", 0, 0, tiled=True)
    turned, mixed_early, gate_out = gate_part(
        place, normed, edge_normed, b_in, short_bias, short_weight, w_in, seqs, block
    )

    own = position * channels
    rates = lax.dynamic_slice_in_dim(decay_rate, own, channels)
    weight_three = lax.dynamic_slice_in_dim(filter_w3.astype(F32), own, channels, axis=1)

    second_weight = filter_w2.astype(F32)
    feats, hidden_one, slope_one, hidden_two, slope_two = filter_layers(
        filter_w1.astype(F32), filter_b1.astype(F32), second_weight, filter_b2.astype(F32), full
    )
    times = lax.broadcasted_iota(jnp.int32, (1, full), 1).astype(F32) / full
    window = jnp.exp(-times * rates[:, None]) + 0.05
    filt = (precise("hd,hp->dp", weight_three, hidden_two) * window).astype(BF16)
    long_all = conv_forward(signal_all, filt, table, channels, blocks, block, seqs)
    conv_long = lax.all_to_all(long_all, "seq", 0, 0, tiled=True)

    order_p, order_q, far = orders()
    core = order_p[0]
    side = side_of(core).reshape(1).astype(jnp.int32)
    (
        output, grad_resid, grad_long, grad_gate, given_p, kept_p, given_q, kept_q, grad_w_out, sums,
    ) = middle(
        side, place, lengths.reshape(seqs), conv_long, signal, gate_out, skip_gain, flat_tokens,
        cotangent.reshape(rows, width), w_out, b_out, norm2_gain, norm2_bias, mlp_b2, mlp_b1[None], mlp_w1,
        mlp_w2, seqs, block,
    )
    grad_long_all = lax.all_to_all(grad_long, "seq", 0, 0, tiled=True)

    def turn(streams, index, *awaited):
        pairs, after = [], []
        for (given, kept), order in streams:
            other = exchange(given, order[index])
            if awaited:
                kept, awaited = held(kept, *awaited), ()
            pairs.append((kept, other))
            after.append(order[index + 1] if index + 1 < len(order) else None)
        routes = [order for _, order in streams]
        merged = len(streams) == 2 and after[0] is not None and after[0] == after[1]
        parts = fold(pairs, after if after[0] else None, merged)
        if merged:
            route = Route(routes[0])
            route.twin, route.lanes = routes[1], pairs[0][0].shape[1]
            routes = [route]
        return list(zip(parts, routes))

    def turn_back(streams, index, *awaited):
        pairs = []
        for part, order in streams:
            other = exchange(part, order[index])
            if awaited:
                part, awaited = held(part, *awaited), ()
            pairs.append((part, other))
        routes = [order for _, order in streams]
        route = routes[0]
        lanes = route.lanes if route.twin and route[index - 1] != route.twin[index - 1] else 0
        parts = join(pairs, [order[index] for order in routes], lanes)
        return list(zip(parts, [Route(route), route.twin] if lanes else routes))

    def meet(streams, *awaited):
        pairs = []
        for part, _ in streams:
            other = exchange(part, far)
            if awaited:
                part, awaited = held(part, *awaited), ()
            pairs.append((part, other))
        return list(zip(fold(pairs, None), [route for _, route in streams]))

    def quarters(streams, *awaited):
        others = [exchange(part, order[1]) for part, order in streams]
        if awaited:
            others = lax.optimization_barrier(tuple(others) + awaited)[: len(others)]
        return [
            [part, other, exchange(part, core), exchange(other, core)]
            for (part, _), other in zip(streams, others)
        ]

    def first_of(streams):
        value = streams[0][0]
        return value[0] if isinstance(value, tuple) else value

    last = len(order_p) - 1
    parts = turn([((given_p, kept_p), order_p), ((given_q, kept_q), order_q)], 0)
    grad_long_all = held(grad_long_all, first_of(parts))
    back_all, grad_filter = conv_backward(
        signal_all, grad_long_all, filt, table, channels, blocks, block, seqs
    )
    back_conv = lax.all_to_all(back_all, "seq", 0, 0, tiled=True)
    last_w3, net = filter_back(
        own.reshape(1).astype(jnp.int32), grad_filter, window, feats, hidden_one, slope_one, hidden_two,
        slope_two, second_weight, weight_three, width,
    )
    features, hidden = filter_w1.shape
    heads = features + hidden + 2
    parts = turn(parts, 1, last_w3)
    back_conv = held(back_conv, first_of(parts))
    edges = all_edges(back_conv, grad_long, skip_gain, factors, grad_gate, seqs, block)
    edges = shifted(edges, "seq", -1)
    late_grads, given_s, kept_s, sums_late = late_back(
        side, back_conv, grad_long, skip_gain, factors, edges, mixed_late, short_weight, turned, seqs,
        block,
    )
    parts = turn(parts, 2, late_grads)
    stream_s = turn([((held(given_s, first_of(parts)), kept_s), order_p)], 0)
    gate_grads, w_in_early, sums_early = early_back(
        held(grad_gate, first_of(stream_s)), edges, mixed_early, short_weight, turned, seqs, block
    )
    tokens_grad, sums_norm = back(
        gate_grads, late_grads, w_in, flat_tokens, grad_resid, norm1_gain, norm1_bias
    )
    parts = turn(parts, 3, tokens_grad)
    if far:
        stream_s = turn(stream_s, 1, first_of(parts))
    wide = sums.shape[0] - 8
    shorts = jnp.concatenate([sums_early, sums_late], axis=0)
    small = jnp.concatenate(
        [sums[:5], sums[8:], sums_norm[:2], shorts[:, :5].reshape(-1, width)], axis=0
    )
    more = small.size // 128
    net = jnp.concatenate(
        [net, small.reshape(more, 128), jnp.zeros((width - 128 - more, 128), F32)], axis=0
    )
    part_t = choose(side, held(w_in_early, first_of(stream_s)), last_w3, grad_w_out, net)
    stream_t = turn([(part_t, order_q)], 0)
    token = first_of(stream_t)
    if far:
        parts = meet(parts, token)
        stream_t = turn(stream_t, 1, first_of(parts))
        token = first_of(stream_t)
    state = {"p": parts, "s": stream_s + stream_t}
    for piece, index in work_order(last):
        if piece == "last":
            last_p, last_q = quarters(state["p"], token)
            token = last_q[1]
        elif piece == "meet":
            state["s"] = meet(state["s"], token)
            token = first_of(state["s"])
        elif piece == "wide":
            sides_of = lambda order: jnp.stack([side_of(order[1]), side_of(core)]).astype(jnp.int32)
            last_p[0] = held(last_p[0], token)
            sum_w1 = widen(sides_of(order_p), last_p, width, False)
            last_q[0] = held(last_q[0], sum_w1)
            sum_w2 = widen(sides_of(order_q), last_q, width, True)
            token = sum_w2
        elif index > 0:
            state[piece] = turn(state[piece], index - 1, token)
            token = first_of(state[piece])
        else:
            state[piece] = turn_back(state[piece], -index, token)
            token = first_of(state[piece])
    last_s, last_t = quarters(state["s"], token)
    sides = jnp.stack([side_of(order_p[1]), side_of(core), side_of(order_q[1])]).astype(jnp.int32)
    sum_w_in, sum_w_out, sum_last = widen_late(sides, last_s, last_t)
    small = unpack(sum_last, features, hidden, wide, width)
    return (
        output.reshape(tokens.shape), tokens_grad.reshape(tokens.shape), *small[:2], sum_w_in, *small[2:11],
        sum_w_out, *small[11:14], sum_w1, small[14], sum_w2, small[15],
    )


def solution(mesh):
    split = P("bucket", None, "seq", None)
    in_specs = (split, split, P("bucket", None)) + (P(),) * 21
    out_specs = (split, split) + (P(),) * 20
    return jax.shard_map(local, mesh=mesh, in_specs=in_specs, out_specs=out_specs, check_vma=False)
```
